32 devices in a mesh: gx: 4 (over x, core), gy: 8 (over z, y).
Axes of the slice: x: 2, y: 2, z: 4, core: 2. Of those that a mesh axis runs over, the one named last changes fastest.
Arguments:
- field: float32 [5, 1, 128, 1024], P(None, None, 'gx', 'gy'), may hold values from -6 to 6
- cotangent: float32 [5, 1, 128, 1024], P(None, None, 'gx', 'gy'), may hold values from -6 to 6
- lift: float32 [15, 32], replicated, may hold values from -1.5 to 1.5
- spectral: float32 [2, 2, 64, 32, 32], replicated, may hold values from -6 to 6
- pointwise: float32 [2, 32, 32], replicated, may hold values from -1 to 1
- project: float32 [32, 5], replicated, may hold values from -1 to 1
Outputs:
- field_grad: float32 [5, 1, 128, 1024], P(None, None, 'gx', 'gy')
The draws below stay inside these ranges and needn't reach their ends.
All inputs are finite; a program needn't handle non-finite values.
Results may differ from the reference program's by a relative error of at most 0.0003.
Values sent between devices are 32-bit elements; how exact they have to be, the bound alone decides.
No kernel may reach another device: no remote copies, remote signals or barrier semaphores. Data moves between devices by JAX's collectives and lax.ppermute only.
A program may use at most 64 MiB of HBM per device.

```python
import jax
import jax.numpy as jnp
from jax import lax

VARS = 5
W = 32
MODES = 8
LAYERS = 2
NZ = 1
PX = 32
PY = 128
NX = 128
NY = 1024
N_GX = 4
N_GY = 8


def block_scale(rng, extent, split, smallest, high):
    factor_of, own = 1.0, jax.random.fold_in(rng, 6)
    for axis_at, blocks in split:
        heights = jnp.exp(jax.random.uniform(jax.random.fold_in(own, axis_at), (blocks,), jnp.float32, smallest / len(split), high / len(split)))
        factor_of = factor_of * jnp.repeat(heights, extent[axis_at] // blocks).reshape([-1 if axis == axis_at else 1 for axis in range(len(extent))])
    return factor_of


def gaussian(own_key, shape, deviation, limit, shards=(), kind=jnp.bfloat16):
    gain = block_scale(own_key, shape, shards, -0.22, 0.18) if shards else 1.0
    drawn = jax.random.normal(own_key, shape, jnp.float32) * deviation * gain
    return jnp.minimum(jnp.maximum(drawn, -limit), limit).astype(kind)


def setup_inputs(seed: int = 0) -> dict:
    streams_of = jax.random.split(jax.random.key(seed), 7)
    return {
        "field": gaussian(streams_of[0], (VARS, NZ, NX, NY), 1.0, 6.0, ((2, 4), (3, 8)), jnp.float32),
        "cotangent": gaussian(streams_of[1], (VARS, NZ, NX, NY), 1.0, 6.0, ((2, 4), (3, 8)), jnp.float32),
        "lift": gaussian(streams_of[2], (3 * VARS, W), (3 * VARS) ** -0.5, 1.5, (), jnp.float32),
        "spectral": gaussian(streams_of[3], (LAYERS, 2, MODES * MODES, W, W), ((PX * PY) ** 0.5 * (2 * W * MODES * MODES) ** -0.5), 6.0, (), jnp.float32),
        "pointwise": gaussian(streams_of[4], (LAYERS, W, W), W ** -0.5, 1.0, (), jnp.float32),
        "project": gaussian(streams_of[5], (W, VARS), W ** -0.5, 1.0, (), jnp.float32),
    }


highest = lax.Precision.HIGHEST

def pooled(values, factor):
    channels, levels, row_count, col_count = values.shape
    blocked = values.reshape(channels, levels, row_count // factor, factor, col_count // factor, factor)
    return blocked.mean(axis=(3, 5))

def spread(grads, factor):
    channels, levels, row_count, col_count = grads.shape
    widened = jnp.broadcast_to(grads[:, :, :, None, :, None], (channels, levels, row_count, factor, col_count, factor))
    return widened.reshape(channels, levels, row_count * factor, col_count * factor) / (factor * factor)

def mode_table(row_count, col_count, mode_side):
    cell_ids = jnp.arange(row_count * col_count, dtype=jnp.int32)
    cell_row = cell_ids // col_count
    cell_col = cell_ids % col_count
    mode_ids = jnp.arange(mode_side * mode_side, dtype=jnp.int32)
    wave_x = mode_ids // mode_side - mode_side // 2
    wave_y = mode_ids % mode_side
    period = row_count * col_count
    turns = (cell_row[:, None] * wave_x[None, :] * col_count + cell_col[:, None] * wave_y[None, :] * row_count) % period
    phase_angle = 2.0 * jnp.pi * turns.astype(jnp.float32) / period
    normalizer = 1.0 / jnp.sqrt(jnp.float32(period))
    return jnp.concatenate([jnp.cos(phase_angle), -jnp.sin(phase_angle)], axis=1) * normalizer

def network(features, lift, spectral, pointwise, project, table):
    channels, levels, row_count, col_count = features.shape
    cell_total = row_count * col_count
    hidden_width = lift.shape[1]
    mode_count = table.shape[1] // 2
    hidden = jnp.dot(lift.T, features.reshape(channels, levels * cell_total), precision=highest)
    for layer_index in range(spectral.shape[0]):
        coefficients = jnp.dot(hidden.reshape(hidden_width * levels, cell_total), table, precision=highest)
        coefficients = coefficients.reshape(hidden_width, levels, 2, mode_count)
        real_part = coefficients[:, :, 0]
        imag_part = coefficients[:, :, 1]
        w_real = spectral[layer_index, 0]
        w_imag = spectral[layer_index, 1]
        mixed_real = jnp.einsum('wzk,kwo->ozk', real_part, w_real, precision=highest) - jnp.einsum('wzk,kwo->ozk', imag_part, w_imag, precision=highest)
        mixed_imag = jnp.einsum('wzk,kwo->ozk', imag_part, w_real, precision=highest) + jnp.einsum('wzk,kwo->ozk', real_part, w_imag, precision=highest)
        mixed_modes = jnp.stack([mixed_real, mixed_imag], axis=2).reshape(hidden_width * levels, 2 * mode_count)
        spectral_part = jnp.dot(mixed_modes, table.T, precision=highest).reshape(hidden_width, levels * cell_total)
        pointwise_part = jnp.dot(pointwise[layer_index].T, hidden, precision=highest)
        hidden = jax.nn.gelu(spectral_part + pointwise_part, approximate=False)
    projected = jnp.dot(project.T, hidden, precision=highest)
    return projected.reshape(project.shape[1], levels, row_count, col_count)

def window_of(coarse, first_row, first_col, row_count, col_count):
    row_ids = ((first_row + jnp.arange(row_count, dtype=jnp.int32)) % coarse.shape[2]).astype(jnp.int32)
    col_ids = ((first_col + jnp.arange(col_count, dtype=jnp.int32)) % coarse.shape[3]).astype(jnp.int32)
    return (row_ids, col_ids, jnp.take(jnp.take(coarse, row_ids, axis=2), col_ids, axis=3))

def reference(field, cotangent, lift, spectral, pointwise, project):
    table = mode_table(PX, PY, MODES)
    half_pooled = pooled(field, 2)
    quarter = pooled(field, 4)

    def one_patch(sums_carry, number):
        grad_half, grad_quarter = sums_carry
        patch_row = (number // N_GY).astype(jnp.int32)
        patch_col = (number % N_GY).astype(jnp.int32)
        anchor = (jnp.int32(0), jnp.int32(0), (patch_row * PX).astype(jnp.int32), (patch_col * PY).astype(jnp.int32))
        own_part = lax.dynamic_slice(field, anchor, (VARS, NZ, PX, PY))
        target = lax.dynamic_slice(cotangent, anchor, (VARS, NZ, PX, PY))
        mid_rows, mid_cols, mid_window = window_of(half_pooled, patch_row * (PX // 2) - PX // 4, patch_col * (PY // 2) - PY // 4, PX, PY)
        far_rows, far_cols, far_window = window_of(quarter, patch_row * (PX // 4) - 3 * PX // 8, patch_col * (PY // 4) - 3 * PY // 8, PX, PY)
        features = jnp.concatenate([own_part, mid_window, far_window], axis=0)
        _, pullback = jax.vjp(lambda inputs: network(inputs, lift, spectral, pointwise, project, table), features)
        grad_features, = pullback(target)
        grad_half = grad_half.at[:, :, mid_rows[:, None], mid_cols[None, :]].add(grad_features[VARS:2 * VARS])
        grad_quarter = grad_quarter.at[:, :, far_rows[:, None], far_cols[None, :]].add(grad_features[2 * VARS:])
        return ((grad_half, grad_quarter), grad_features[:VARS])
    start = (jnp.zeros_like(half_pooled), jnp.zeros_like(quarter))
    (grad_half, grad_quarter), own_grads = lax.scan(one_patch, start, jnp.arange(N_GX * N_GY, dtype=jnp.int32))
    own_grads = own_grads.reshape(N_GX, N_GY, VARS, NZ, PX, PY).transpose(2, 3, 0, 4, 1, 5).reshape(VARS, NZ, NX, NY)
    return own_grads + spread(grad_half, 2) + spread(grad_quarter, 4)
```

```python
import functools

import jax
import jax.numpy as jnp
import numpy as np
from jax import lax
from jax.experimental import pallas as pl
from jax.experimental.pallas import tpu as pltpu
from jax.sharding import PartitionSpec as P

MODES = 8
F32 = jnp.float32
BF16 = jnp.bfloat16
HIGHEST = lax.Precision.HIGHEST
SQRT_HALF = float(np.sqrt(0.5))
INV_SQRT_2PI = float(1.0 / np.sqrt(2.0 * np.pi))


class Ring:
    def __init__(self, count):
        self.count = count
        self.whole = count <= 7
        self.offsets = list(range(count)) if self.whole else [0, 1, 2, 3, -3, -2, -1]

    def place(self, offset):
        if self.whole:
            return offset % self.count
        return self.offsets.index(max(-3, min(3, offset)))


def split(value):
    high = value.astype(BF16)
    return high, (value - high.astype(F32)).astype(BF16)


def dot(left, right):
    return jnp.dot(left, right, preferred_element_type=F32)


def dot_t(left, right):
    return lax.dot_general(left, right, (((1,), (1,)), ((), ())), precision=HIGHEST, preferred_element_type=F32)


def exact_dot(left, right):
    return jnp.dot(left, right, precision=HIGHEST, preferred_element_type=F32)


def stacked(value):
    high, low = split(value)
    top = jnp.concatenate([high, high], axis=1)
    bottom = jnp.concatenate([low, jnp.zeros_like(low)], axis=1)
    return jnp.concatenate([top, bottom], axis=0)


def halves(value):
    rows = value.shape[0] // 2
    return value[:rows] + value[rows:]


def row_pool_matrix(cols):
    half = cols // 2
    out = np.zeros((2 * cols, cols), np.float32)
    for j in range(cols):
        out[j, j // 2] = 0.25
        out[cols + j, half + j // 2] = 0.25
    return out


def quarter_matrix(cols):
    half, quarter, eighth = cols // 2, cols // 4, cols // 8
    out = np.zeros((5 * cols, cols), np.float32)
    for lane in range(cols):
        coarse = lane - eighth * 3
        d, t = coarse // quarter, coarse % quarter
        for m in (2 * t, 2 * t + 1, half + 2 * t, half + 2 * t + 1):
            out[(d + 2) * cols + m, lane] = 0.25
    return out


def angle_tables(rows, cols):
    m = np.arange(MODES * MODES)
    wave_x, wave_y = m // MODES - MODES // 2, m % MODES
    a = 2.0 * np.pi * ((np.arange(rows)[:, None] * wave_x[None]) % rows) / rows
    b = 2.0 * np.pi * ((np.arange(cols)[:, None] * wave_y[None]) % cols) / cols
    scale = 1.0 / np.sqrt(rows * cols)
    x = np.concatenate([np.cos(a), -np.sin(a)], 1)
    y = np.concatenate([-np.sin(a), -np.cos(a)], 1)
    b1 = np.concatenate([np.cos(b), np.cos(b)], 1) * scale
    b2 = np.concatenate([np.sin(b), np.sin(b)], 1) * scale
    return [v.astype(np.float32) for v in (x, y, b1, b2)]


def table_kernel(x_ref, y_ref, b1_ref, b2_ref, xt_ref, yt_ref, b1t_ref, b2t_ref, table_ref, flipped_ref):
    rows = x_ref.shape[0]
    cols, modes = b1_ref.shape
    for i in range(rows):
        piece = x_ref[i : i + 1, :] * b1_ref[...] + y_ref[i : i + 1, :] * b2_ref[...]
        high, low = split(piece)
        table_ref[i * cols : (i + 1) * cols, :modes] = high
        table_ref[i * cols : (i + 1) * cols, modes:] = low
        piece = xt_ref[:, i : i + 1] * b1t_ref[...] + yt_ref[:, i : i + 1] * b2t_ref[...]
        high, low = split(piece)
        flipped_ref[:modes, i * cols : (i + 1) * cols] = high
        flipped_ref[modes:, i * cols : (i + 1) * cols] = low


def pool_kernel(field_ref, pool_ref, out_ref):
    count = field_ref.shape[0] // 4
    rows = [field_ref[pl.ds(k, count, stride=4), :] for k in range(4)]
    pairs = jnp.concatenate([rows[0] + rows[1], rows[2] + rows[3]], axis=1)
    out_ref[...] = exact_dot(pairs, pool_ref[...])


def mix(weights, layer, coefficients, swap_ref):
    width, lanes = coefficients.shape
    half = lanes // 2
    lane = lax.broadcasted_iota(jnp.int32, (width, lanes), 1)
    swapped = pltpu.roll(coefficients, half, 1)
    signed = jnp.where(lane < half, coefficients, -coefficients)
    total_real = jnp.zeros((width, lanes), F32)
    total_imag = jnp.zeros((width, lanes), F32)
    for w in range(width):
        block = weights[layer, w]
        total_real += block * signed[w : w + 1]
        total_imag += block * swapped[w : w + 1]
    total_real += pltpu.roll(total_real, half, 1)
    total_imag += pltpu.roll(total_imag, half, 1)
    return jnp.where(lane < half, total_real, total_imag)


def unmix(weights, layer, grads, swap_ref):
    width, lanes = grads.shape
    half = lanes // 2
    lane = lax.broadcasted_iota(jnp.int32, (width, lanes), 1)
    turned = pltpu.roll(grads, half, 1)
    turned = jnp.where(lane < half, turned, -turned)
    for w in range(width):
        block = weights[layer, w]
        swap_ref[0, w : w + 1, :] = jnp.sum(block * grads, axis=0, keepdims=True)
        swap_ref[1, w : w + 1, :] = jnp.sum(block * turned, axis=0, keepdims=True)
    real, imag = swap_ref[0], swap_ref[1]
    real += pltpu.roll(real, half, 1)
    imag += pltpu.roll(imag, half, 1)
    return jnp.where(lane < half, real, imag)


def contract(pair_ref, table_ref):
    both = dot(pair_ref[...], table_ref[...])
    rows, modes = both.shape[0] // 2, both.shape[1] // 2
    return both[:rows, :modes] + both[:rows, modes:] + both[rows:, :modes]


def network_kernel(
    ring, chunk,
    core_ref, field_ref, blocks_ref, near_a, near_b, swap_a, swap_b, cotangent_ref, lift_ref, lift_t_ref, weights,
    pointwise_ref, pointwise_t_ref, project_ref, quarter_ref, quarter_t_ref, table_ref, flipped_ref,
    own_ref, center_ref, keep_a, keep_b, give_a, give_b,
    x_ref, window_ref, feature_pair, hidden_pair, grad_pair, target_pair, slope_one, swap_ref, target_ref, grad_x_ref,
):
    channels, rows, cols = field_ref.shape
    tall = rows // 4
    half, quarter = cols // 2, cols // 4
    cells = rows * cols
    width = pointwise_ref.shape[1]
    padded = x_ref.shape[0] // rows
    odd = core_ref[0] == 1
    lane = lax.broadcasted_iota(jnp.int32, (1, 1, cols), 2)

    for d in range(-2, 3):
        for e in range(-2, 3):
            here = ring.place(e)
            if d == 0:
                block = blocks_ref[here]
            else:
                there = jnp.where(odd, ring.place(e + 1), ring.place(e - 1))
                direct, swapped = (near_a, swap_a) if d > 0 else (near_b, swap_b)
                block = jnp.where(odd == (abs(d) == 1), direct[here], swapped[there])
            if e == -2:
                window_ref[d + 2, :, : tall // 2, :] = block[:, tall // 2 :, :]
            elif e == 2:
                window_ref[d + 2, :, 4 * tall - tall // 2 :, :] = block[:, : tall // 2, :]
            else:
                first = tall // 2 + (e + 1) * tall
                window_ref[d + 2, :, first : first + tall, :] = block

    for c in range(channels):
        x_ref[c * rows : (c + 1) * rows, :] = field_ref[c]
    previous, own, following = (window_ref[d, :, tall : 3 * tall, :] for d in (1, 2, 3))

    def turn(value, steps):
        flat = value.reshape(channels * 2 * tall, cols)
        return pltpu.roll(flat, steps % cols, 1).reshape(value.shape)

    def three(a, b, c):
        return jnp.where(lane < quarter, a, jnp.where(lane < 3 * quarter, b, c))

    even_rows = three(turn(previous, -quarter), turn(own, quarter), turn(following, -quarter))
    odd_rows = three(turn(previous, quarter), turn(own, -quarter), turn(following, quarter))
    for c in range(channels):
        first = (channels + c) * rows
        x_ref[pl.ds(first, 2 * tall, stride=2), :] = even_rows[c]
        x_ref[pl.ds(first + 1, 2 * tall, stride=2), :] = odd_rows[c]
    pieces = []
    for d in range(5):
        high, low = split(window_ref[d].reshape(channels * rows, cols))
        pieces.append(jnp.concatenate([high, low], axis=0))
    far = halves(dot(jnp.concatenate(pieces, axis=1), quarter_ref[...]))
    x_ref[2 * channels * rows : 3 * channels * rows, :] = far
    for c in range(3 * channels, padded):
        x_ref[c * rows : (c + 1) * rows, :] = jnp.zeros((rows, cols), F32)

    target_ref[channels * rows :, :] = jnp.zeros((target_ref.shape[0] - channels * rows, cols), F32)
    for c in range(channels):
        target_ref[c * rows : (c + 1) * rows, :] = cotangent_ref[c]
    small = target_ref.shape[0] // rows
    for i in range(rows):
        at = slice(i * cols, (i + 1) * cols)
        high, low = split(x_ref[pl.ds(i, padded, stride=rows), :])
        feature_pair[:padded, at] = high
        feature_pair[padded:, at] = low
        value = target_ref[pl.ds(i, small, stride=rows), :]
        high = value.astype(BF16).astype(F32)
        target_pair[:, at] = jnp.concatenate([high, value - high], axis=0).astype(BF16)

    lift = lift_ref[...]
    lift_t = lift_t_ref[...]
    steps = [slice(k, k + chunk) for k in range(0, cells, chunk)]

    mixed = mix(weights, 0, exact_dot(lift_t, contract(feature_pair, table_ref)), swap_ref)
    wave = stacked(mixed)
    local = stacked(exact_dot(pointwise_t_ref[0], lift_t))
    for at in steps:
        u = halves(dot(wave, flipped_ref[:, at]) + dot(local, feature_pair[:, at]))
        cdf = 0.5 + 0.5 * lax.erf(u * SQRT_HALF)
        slope_one[:, at] = cdf + u * (INV_SQRT_2PI * jnp.exp(-0.5 * u * u))
        high, low = split(u * cdf)
        hidden_pair[:width, at] = high
        hidden_pair[width:, at] = low

    mixed = mix(weights, 1, contract(hidden_pair, table_ref), swap_ref)
    wave = stacked(mixed)
    local = stacked(pointwise_t_ref[1])
    out = stacked(project_ref[...])
    for at in steps:
        u = halves(dot(wave, flipped_ref[:, at]) + dot(local, hidden_pair[:, at]))
        cdf = 0.5 + 0.5 * lax.erf(u * SQRT_HALF)
        slope = cdf + u * (INV_SQRT_2PI * jnp.exp(-0.5 * u * u))
        high, low = split(slope * halves(dot(out, target_pair[:, at])))
        grad_pair[:width, at] = high
        grad_pair[width:, at] = low
    wave = stacked(unmix(weights, 1, contract(grad_pair, table_ref), swap_ref))
    local = stacked(pointwise_ref[1])
    for at in steps:
        g = halves(dot(wave, flipped_ref[:, at]) + dot(local, grad_pair[:, at]))
        high, low = split(g * slope_one[:, at])
        hidden_pair[:width, at] = high
        hidden_pair[width:, at] = low

    wave = stacked(exact_dot(lift, unmix(weights, 0, contract(hidden_pair, table_ref), swap_ref)))
    local = stacked(exact_dot(lift, pointwise_ref[0]))
    for k, at in enumerate(steps):
        g = halves(dot(wave, flipped_ref[:, at]) + dot(local, hidden_pair[:, at]))
        for n in range(chunk // cols):
            grad_x_ref[pl.ds(k * (chunk // cols) + n, padded, stride=rows), :] = g[:, n * cols : (n + 1) * cols]

    for c in range(channels):
        own_ref[c] = grad_x_ref[c * rows : (c + 1) * rows, :]

    even_grads, odd_grads = [], []
    for c in range(channels):
        first = (channels + c) * rows
        even_grads.append(grad_x_ref[pl.ds(first, 2 * tall, stride=2), :][None])
        odd_grads.append(grad_x_ref[pl.ds(first + 1, 2 * tall, stride=2), :][None])
    even_grads = jnp.concatenate(even_grads, axis=0)
    odd_grads = jnp.concatenate(odd_grads, axis=0)
    even_up, even_down = turn(even_grads, quarter), turn(even_grads, -quarter)
    odd_up, odd_down = turn(odd_grads, quarter), turn(odd_grads, -quarter)
    zero = jnp.zeros_like(even_grads)

    def four(a, b, c, d):
        return jnp.where(lane < quarter, a, jnp.where(lane < half, b, jnp.where(lane < 3 * quarter, c, d)))

    near = {
        -1: four(zero, even_up, zero, odd_down),
        0: four(even_down, even_down, odd_up, odd_up),
        1: four(even_up, zero, odd_down, zero),
    }
    high, low = split(grad_x_ref[2 * channels * rows : 3 * channels * rows, :])
    spread = halves(dot(jnp.concatenate([high, low], axis=0), quarter_t_ref[...]))
    for d in range(5):
        window_ref[d] = spread[:, d * cols : (d + 1) * cols].reshape(channels, rows, cols)
    for d in (-1, 0, 1):
        window_ref[d + 2, :, tall : 3 * tall, :] += near[d]

    def block_of(d, e):
        if abs(e) < 2:
            first = tall // 2 + (e + 1) * tall
            return window_ref[d + 2, :, first : first + tall, :]
        low_part = window_ref[d + 2, :, 4 * tall - tall // 2 :, :]
        high_part = window_ref[d + 2, :, : tall // 2, :]
        if not (ring.whole and ring.count == 4):
            low_part, high_part = (low_part, jnp.zeros_like(low_part)) if e > 0 else (jnp.zeros_like(low_part), high_part)
        return jnp.concatenate([low_part, high_part], axis=1)

    reached = {}
    for e in range(-2, 3):
        reached[ring.place(e)] = e
    for place in range(len(ring.offsets)):
        if place not in reached:
            for ref in (center_ref, keep_a, keep_b, give_a, give_b):
                ref[place] = jnp.zeros((channels, tall, cols), F32)
            continue
        e = reached[place]
        center_ref[place] = block_of(0, e)
        for one, two, keep, give in ((-1, -2, keep_a, give_a), (1, 2, keep_b, give_b)):
            near_block, far_block = block_of(one, e), block_of(two, e)
            keep[place] = jnp.where(odd, near_block, far_block)
            give[place] = jnp.where(odd, far_block, near_block)


def join_kernel(ring, core_ref, keep_a, keep_b, got_a, got_b, out_a, out_b):
    odd = core_ref[0] == 1
    for offset in ring.offsets:
        here = ring.place(offset)
        there = jnp.where(odd, ring.place(offset + 1), ring.place(offset - 1))
        out_a[here] = keep_a[here] + got_a[there]
        out_b[here] = keep_b[here] + got_b[there]


def gather_kernel(center_ref, a_ref, b_ref, *outs):
    for place, out in enumerate(outs):
        out[...] = center_ref[place] + a_ref[place] + b_ref[place]


def final_kernel(channels, own_ref, pool_ref, *refs):
    out_ref = refs[-1]
    total = refs[0][...]
    for ref in refs[1:-1]:
        total = total + ref[...]
    cols = total.shape[2]
    spread = dot_t(total.reshape(-1, cols), pool_ref[...])
    count = spread.shape[0]
    for k in range(4):
        part = spread[:, :cols] if k < 2 else spread[:, cols:]
        at = pl.ds(k, count, stride=4)
        out_ref[at, :] = own_ref[at, :] + part


def in_vmem(count):
    return [pl.BlockSpec(memory_space=pltpu.VMEM)] * count


SCALAR = pl.BlockSpec(memory_space=pltpu.SMEM)


def call(kernel, shapes, *operands, scalars=0, scratch=(), name=None):
    single = not isinstance(shapes, (list, tuple))
    outs = [shapes] if single else list(shapes)
    result = pl.pallas_call(
        kernel,
        out_shape=outs,
        in_specs=[SCALAR] * scalars + in_vmem(len(operands) - scalars),
        out_specs=in_vmem(len(outs)),
        scratch_shapes=list(scratch),
        compiler_params=pltpu.CompilerParams(vmem_limit_bytes=48 << 20),
        name=name,
    )(*operands)
    return result[0] if single else result


def body(field, cotangent, lift, spectral, pointwise, project):
    channels, levels, rows, cols = field.shape
    width = lift.shape[1]
    layers = spectral.shape[0]
    modes = spectral.shape[2]
    features = lift.shape[0]
    cells = rows * cols
    tall = rows // 4
    gx, gy = lax.axis_size("gx"), lax.axis_size("gy")
    ring = Ring(gx)
    blocks = len(ring.offsets)
    core = (lax.axis_index("gx") % 2).astype(jnp.int32).reshape(1)

    def shape(*dims, dtype=F32):
        return jax.ShapeDtypeStruct(dims, dtype)

    def along_x(value, steps):
        return lax.ppermute(value, "gx", [(s, (s + steps) % gx) for s in range(gx)])

    def along_y(value, even_steps, odd_steps):
        pairs = []
        for a in range(gx):
            for b in range(gy):
                steps = odd_steps if a % 2 else even_steps
                pairs.append((a * gy + b, a * gy + (b + steps) % gy))
        return lax.ppermute(value, ("gx", "gy"), pairs)

    def swap(value):
        return lax.ppermute(value, "gx", [(s, s ^ 1) for s in range(gx)])

    flat_field = field.reshape(channels * rows, cols)
    pool = jnp.asarray(row_pool_matrix(cols))
    quarter = quarter_matrix(cols)
    packed = call(pool_kernel, shape(channels * tall, cols), flat_field, pool, name="pool")
    packed = packed.reshape(channels, tall, cols)

    held = [packed] + [along_x(packed, -offset) for offset in ring.offsets[1:]]
    x, y, b1, b2 = angle_tables(rows, cols)
    table, flipped = call(
        table_kernel,
        (shape(cells, 4 * modes, dtype=BF16), shape(4 * modes, cells, dtype=BF16)),
        *(jnp.asarray(v) for v in (x, y, b1, b2, x.T.copy(), y.T.copy(), b1.T.copy(), b2.T.copy())),
        name="table",
    )
    by_mode = jnp.transpose(spectral, (0, 1, 3, 4, 2))
    weights = jnp.concatenate([by_mode[:, 0], by_mode[:, 1]], axis=-1)
    held = jnp.stack(held)
    from_a = along_y(held, -2, -1)
    from_b = along_y(held, 2, 1)
    swap_a, swap_b = swap(from_a), swap(from_b)

    padded = -(-features // 16) * 16
    lift_rows = jnp.pad(lift, ((0, padded - features), (0, 0)))
    small = -(-channels // 8) * 8
    project_cols = jnp.pad(project, ((0, 0), (0, small - channels)))
    group = shape(blocks, channels, tall, cols)
    chunk = 4 * cols
    own, center, keep_a, keep_b, give_a, give_b = call(
        functools.partial(network_kernel, ring, chunk),
        (shape(channels, rows, cols), group, group, group, group, group),
        core, field.reshape(channels, rows, cols), held, from_a, from_b, swap_a, swap_b,
        cotangent.reshape(channels, rows, cols), lift_rows, lift_rows.T, weights,
        pointwise, jnp.transpose(pointwise, (0, 2, 1)), project_cols,
        jnp.asarray(quarter, BF16), jnp.asarray(quarter.T.copy(), BF16), table, flipped,
        scalars=1,
        scratch=(
            pltpu.VMEM((padded * rows, cols), F32),
            pltpu.VMEM((5, channels, rows, cols), F32),
            pltpu.VMEM((2 * padded, cells), BF16),
            pltpu.VMEM((2 * width, cells), BF16),
            pltpu.VMEM((2 * width, cells), BF16),
            pltpu.VMEM((2 * small, cells), BF16),
            pltpu.VMEM((width, cells), F32),
            pltpu.VMEM((2, width, 2 * modes), F32),
            pltpu.VMEM((small * rows, cols), F32),
            pltpu.VMEM((padded * rows, cols), F32),
        ),
        name="network",
    )

    got_a, got_b = swap(give_a), swap(give_b)
    sum_a, sum_b = call(
        functools.partial(join_kernel, ring), (group, group), core, keep_a, keep_b, got_a, got_b, scalars=1, name="join"
    )
    sum_a, sum_b = along_y(sum_a, -2, -1), along_y(sum_b, 2, 1)
    piece = shape(channels, tall, cols)
    parts = call(gather_kernel, [piece] * blocks, center, sum_a, sum_b, name="gather")
    parts = [parts[0]] + [along_x(part, offset) for part, offset in zip(parts[1:], ring.offsets[1:])]
    out = call(
        functools.partial(final_kernel, channels),
        shape(channels * rows, cols),
        own.reshape(channels * rows, cols), pool, *parts,
        name="final",
    )
    return out.reshape(field.shape)


def solution(mesh):
    return jax.shard_map(
        body,
        mesh=mesh,
        in_specs=(P(None, None, "gx", "gy"), P(None, None, "gx", "gy"), P(), P(), P(), P()),
        out_specs=P(None, None, "gx", "gy"),
        check_vma=False,
    )
```

```python
import functools

import jax
import jax.numpy as jnp
import numpy as np
from jax import lax
from jax.experimental import pallas as pl
from jax.experimental.pallas import tpu as pltpu
from jax.sharding import PartitionSpec as P

MODES = 8
F32 = jnp.float32
BF16 = jnp.bfloat16
HIGHEST = lax.Precision.HIGHEST
SQRT_HALF = float(np.sqrt(0.5))
INV_SQRT_2PI = float(1.0 / np.sqrt(2.0 * np.pi))


class Ring:
    def __init__(self, count):
        self.count = count
        self.whole = count <= 7
        self.offsets = list(range(count)) if self.whole else [0, 1, 2, 3, -3, -2, -1]

    def place(self, offset):
        if self.whole:
            return offset % self.count
        return self.offsets.index(max(-3, min(3, offset)))


def split(value):
    high = value.astype(BF16)
    return high, (value - high.astype(F32)).astype(BF16)


def dot(left, right):
    return jnp.dot(left, right, preferred_element_type=F32)


def dot_t(left, right):
    return lax.dot_general(left, right, (((1,), (1,)), ((), ())), precision=HIGHEST, preferred_element_type=F32)


def exact_dot(left, right):
    return jnp.dot(left, right, precision=HIGHEST, preferred_element_type=F32)


def stacked(value):
    high, low = split(value)
    top = jnp.concatenate([high, high], axis=1)
    bottom = jnp.concatenate([low, jnp.zeros_like(low)], axis=1)
    return jnp.concatenate([top, bottom], axis=0)


def halves(value):
    rows = value.shape[0] // 2
    return value[:rows] + value[rows:]


def quarter_matrix(cols):
    half, quarter, eighth = cols // 2, cols // 4, cols // 8
    out = np.zeros((5 * cols, cols), np.float32)
    for lane in range(cols):
        coarse = lane - eighth * 3
        d, t = coarse // quarter, coarse % quarter
        for m in (2 * t, 2 * t + 1, half + 2 * t, half + 2 * t + 1):
            out[(d + 2) * cols + m, lane] = 0.25
    return out


def wave_matrix(rows, cols):
    m = np.arange(MODES * MODES)
    wave_x, wave_y = m // MODES - MODES // 2, m % MODES
    b = 2.0 * np.pi * ((np.arange(cols)[:, None] * wave_y[None]) % cols) / cols
    scale = 1.0 / np.sqrt(rows * cols)
    cos, sin = np.cos(b) * scale, np.sin(b) * scale
    parts = []
    for k in range(MODES // 2 + 1):
        held = (np.abs(wave_x) == k)[None]
        parts.append(np.concatenate([cos * held, -sin * held], 1))
    for k in range(1, MODES // 2 + 1):
        held = (np.sign(wave_x) * (np.abs(wave_x) == k))[None]
        parts.append(np.concatenate([-sin * held, -cos * held], 1))
    return np.concatenate(parts, 0).astype(np.float32)


def wave_pair(matrix, axis):
    high = matrix.astype(BF16)
    low = (matrix - high.astype(np.float32)).astype(BF16)
    return jnp.asarray(np.concatenate([high, low], axis))


def weighted(terms):
    groups = {}
    for factor, value in terms:
        size = round(abs(factor), 12)
        if size == 0:
            continue
        groups.setdefault(size, []).append((factor > 0, value, abs(factor)))
    total = None
    for size, members in groups.items():
        members.sort(key=lambda member: not member[0])
        part = members[0][1] if members[0][0] else -members[0][1]
        for positive, value, _ in members[1:]:
            part = part + value if positive else part - value
        if size != 1:
            part = part * members[0][2]
        total = part if total is None else total + part
    return total


def wave_forward(values):
    n = len(values)
    top = MODES // 2
    angle = lambda k, i: 2.0 * np.pi * ((k * i) % n) / n
    plus = [values[0]] + [values[i] + values[n - i] for i in range(1, n // 2)] + [values[n // 2]]
    minus = [None] + [values[i] - values[n - i] for i in range(1, n // 2)]
    even = [plus[i] + plus[n // 2 - i] for i in range(n // 4)] + [plus[n // 4]]
    odd = [plus[i] - plus[n // 2 - i] for i in range(n // 4)]
    minus_odd = [None] + [minus[i] + minus[n // 2 - i] for i in range(1, n // 4)] + [minus[n // 4]]
    minus_even = [None] + [minus[i] - minus[n // 2 - i] for i in range(1, n // 4)]
    deep = {
        1: [even[i] + even[n // 4 - i] for i in range(n // 8)],
        -1: [even[i] - even[n // 4 - i] for i in range(n // 8)],
    }
    deep_minus = {
        1: [None] + [minus_even[i] - minus_even[n // 4 - i] for i in range(1, n // 8)],
        -1: [None] + [minus_even[i] + minus_even[n // 4 - i] for i in range(1, n // 8)],
    }
    out = []
    for k in range(top + 1):
        if k % 2:
            out.append(weighted([(np.cos(angle(k, i)), odd[i]) for i in range(n // 4)]))
        else:
            sign = 1 if k % 4 == 0 else -1
            terms = [(np.cos(angle(k, i)), deep[sign][i]) for i in range(n // 8)]
            out.append(weighted(terms + [(np.cos(angle(k, n // 8)), even[n // 8])]))
    for k in range(1, top + 1):
        if k % 2:
            out.append(weighted([(np.sin(angle(k, i)), minus_odd[i]) for i in range(1, n // 4 + 1)]))
        else:
            sign = 1 if k % 4 == 0 else -1
            terms = [(np.sin(angle(k, i)), deep_minus[sign][i]) for i in range(1, n // 8)]
            out.append(weighted(terms + [(np.sin(angle(k, n // 8)), minus_even[n // 8])]))
    return out


def added(a, b):
    return b if a is None else a if b is None else a + b


def taken(a, b):
    return a if b is None else -b if a is None else a - b


def wave_backward(parts, n):
    top = MODES // 2
    angle = lambda k, i: 2.0 * np.pi * ((k * i) % n) / n
    cosine = lambda i, ks: weighted([(np.cos(angle(k, i)), parts[k]) for k in ks])
    sine = lambda i, ks: weighted([(np.sin(angle(k, i)), parts[top + k]) for k in ks])
    fours = [k for k in range(top + 1) if k % 4 == 0]
    twos = [k for k in range(top + 1) if k % 4 == 2]
    odds = [k for k in range(top + 1) if k % 2]
    even = [None] * (n // 4 + 1)
    for i in range(n // 8):
        a, b = cosine(i, fours), cosine(i, twos)
        even[i], even[n // 4 - i] = added(a, b), taken(a, b)
    even[n // 8] = cosine(n // 8, sorted(fours + twos))
    plus = [None] * (n // 2 + 1)
    for i in range(n // 4):
        b = cosine(i, odds)
        plus[i], plus[n // 2 - i] = added(even[i], b), taken(even[i], b)
    plus[n // 4] = even[n // 4]
    minus_even = [None] * (n // 4)
    for i in range(1, n // 8):
        a, b = sine(i, [k for k in fours if k]), sine(i, twos)
        minus_even[i], minus_even[n // 4 - i] = added(b, a), taken(b, a)
    minus_even[n // 8] = sine(n // 8, sorted(k for k in fours + twos if k))
    minus = [None] * (n // 2)
    for i in range(1, n // 4):
        a = sine(i, odds)
        minus[i], minus[n // 2 - i] = added(a, minus_even[i]), taken(a, minus_even[i])
    minus[n // 4] = sine(n // 4, odds)
    out = [None] * n
    out[0], out[n // 2] = plus[0], plus[n // 2]
    for i in range(1, n // 2):
        out[i], out[n - i] = added(plus[i], minus[i]), taken(plus[i], minus[i])
    return out


def prepare_kernel(
    cotangent_hbm, lift_hbm, spectral_hbm, pointwise_hbm, project_hbm, *refs
):
    constants_hbm, refs = refs[:3], refs[3:]
    constants, refs = refs[:3], refs[3:]
    by_input, by_output_hbm, lift_ref, lift_t_ref, local_one, local_two, back_two, back_one, target_grad = refs[:9]
    spectral_ref, by_output, target_ref, lift_in, pointwise_ref, project_ref, sems = refs[9:]
    layers, _, width, _, modes = spectral_ref.shape
    small, cols = project_ref.shape[0], target_ref.shape[1]
    rows = target_ref.shape[0] // small
    channels, features = project_hbm.shape[0], lift_hbm.shape[0]
    pairs = [
        (cotangent_hbm, target_ref.at[: channels * rows]),
        (project_hbm, project_ref.at[:channels]),
        (lift_hbm, lift_in.at[:features]),
        (pointwise_hbm, pointwise_ref),
    ]
    pairs += [(spectral_hbm.at[layer], spectral_ref.at[layer]) for layer in range(layers)]
    pairs += list(zip(constants_hbm, constants))
    copies = [pltpu.make_async_copy(source, target, sems.at[k]) for k, (source, target) in enumerate(pairs)]
    for copy in copies:
        copy.start()
    target_ref[channels * rows :, :] = jnp.zeros(((small - channels) * rows, cols), F32)
    project_ref[channels:, :] = jnp.zeros((small - channels, width), F32)
    lift_in[features:, :] = jnp.zeros((lift_in.shape[0] - features, width), F32)
    for copy in copies[:4]:
        copy.wait()

    lift = lift_in[...]
    lift_t = jnp.transpose(lift)
    lift_ref[...] = lift
    lift_t_ref[...] = lift_t
    back_one[...] = tripled(exact_dot(lift, pointwise_ref[0]))
    local_one[...] = tripled(exact_dot(jnp.transpose(pointwise_ref[0]), lift_t))
    local_two[...] = tripled(jnp.transpose(pointwise_ref[1]))
    back_two[...] = tripled(pointwise_ref[1])
    out = tripled(jnp.transpose(project_ref[...]))
    group = 4
    for first in range(0, rows, group):
        pieces = []
        for i in range(first, first + group):
            value = target_ref[pl.ds(i, small, stride=rows), :]
            high = value.astype(BF16).astype(F32)
            pieces.append(jnp.concatenate([high, value - high, high], axis=0).astype(BF16))
        target_grad[:, first * cols : (first + group) * cols] = dot(out, jnp.concatenate(pieces, axis=1))

    for layer in range(layers):
        copies[4 + layer].wait()
        for w in range(width):
            both = [spectral_ref[layer, part, w] for part in range(2)]
            by_input[layer, w] = jnp.concatenate(both, axis=1)
        for o in range(width):
            for first in range(0, width, 8):
                both = [spectral_ref[layer, part, first : first + 8, o, :] for part in range(2)]
                by_output[layer, o, first : first + 8, :] = jnp.concatenate(both, axis=1)
        copies.append(pltpu.make_async_copy(by_output.at[layer], by_output_hbm.at[layer], sems.at[len(copies)]))
        copies[-1].start()
    for copy in copies[4 + layers :]:
        copy.wait()


def pool_matrix(cols):
    half = cols // 2
    row = lax.broadcasted_iota(jnp.int32, (2 * cols, cols), 0)
    col = lax.broadcasted_iota(jnp.int32, (2 * cols, cols), 1)
    return jnp.where(row // 2 == col, 0.25, 0.0).astype(F32)


def pool_kernel(field_ref, out_ref):
    count = field_ref.shape[0] // 4
    rows = [field_ref[pl.ds(k, count, stride=4), :] for k in range(4)]
    pairs = jnp.concatenate([rows[0] + rows[1], rows[2] + rows[3]], axis=1)
    out_ref[...] = exact_dot(pairs, pool_matrix(field_ref.shape[1]))


def mix(weights, layer, coefficients):
    width, lanes = coefficients.shape
    half = lanes // 2
    lane = lax.broadcasted_iota(jnp.int32, (width, lanes), 1)
    swapped = pltpu.roll(coefficients, half, 1)
    signed = jnp.where(lane < half, coefficients, -coefficients)
    total_real = jnp.zeros((width, lanes), F32)
    total_imag = jnp.zeros((width, lanes), F32)
    for w in range(width):
        block = weights[layer, w]
        total_real += block * signed[w : w + 1]
        total_imag += block * swapped[w : w + 1]
    total_real += pltpu.roll(total_real, half, 1)
    total_imag += pltpu.roll(total_imag, half, 1)
    return jnp.where(lane < half, total_real, total_imag)


def unmix(weights, layer, grads):
    width, lanes = grads.shape
    half = lanes // 2
    lane = lax.broadcasted_iota(jnp.int32, (width, lanes), 1)
    turned = pltpu.roll(grads, half, 1)
    turned = jnp.where(lane < half, turned, -turned)
    total_real = jnp.zeros((width, lanes), F32)
    total_imag = jnp.zeros((width, lanes), F32)
    for o in range(width):
        block = weights[layer, o]
        total_real += block * grads[o : o + 1]
        total_imag += block * turned[o : o + 1]
    total_real += pltpu.roll(total_real, half, 1)
    total_imag += pltpu.roll(total_imag, half, 1)
    return jnp.where(lane < half, total_real, total_imag)


def contract(parts, wave):
    high, low = split(parts)
    both = dot(jnp.concatenate([high, low], axis=0), wave)
    rows, modes = both.shape[0] // 2, both.shape[1] // 2
    return both[:rows, :modes] + both[:rows, modes:] + both[rows:, :modes]


def tripled(value):
    high, low = split(value)
    return jnp.concatenate([high, high, low], axis=1)


def local_product(out_ref, left, pair_ref, steps):
    rows = pair_ref.shape[0] // 2
    for at in steps:
        right = jnp.concatenate([pair_ref[:, at], pair_ref[:rows, at]], axis=0)
        out_ref[:, at] = dot(left, right)


def store_pair(pair_ref, first, rows_total, at, value):
    high, low = split(value)
    count = value.shape[0]
    pair_ref[first : first + count, at] = high
    pair_ref[rows_total + first : rows_total + first + count, at] = low


def network_kernel(
    ring, chunk,
    core_ref, field_ref, blocks_ref, near_a, near_b, swap_a, swap_b, quarter_t_hbm, by_output_hbm,
    quarter_ref, wave_ref, wave_t_ref, by_input, lift_ref, lift_t_ref, local_one, local_two, back_two, back_one, target_grad,
    own_ref, center_ref, keep_a, keep_b, give_a, give_b,
    x_ref, window_ref, feature_pair, hidden_pair, slope_one, local_ref, grad_x_ref, parts_ref,
    quarter_t_ref, by_output, sems,
):
    channels, rows, cols = field_ref.shape
    tall = rows // 4
    half, quarter = cols // 2, cols // 4
    cells = rows * cols
    width = slope_one.shape[0]
    padded = x_ref.shape[0] // rows
    odd = core_ref[0] == 1
    lane = lax.broadcasted_iota(jnp.int32, (1, 1, cols), 2)

    late = [(by_output_hbm, by_output), (quarter_t_hbm, quarter_t_ref)]
    late = [pltpu.make_async_copy(source, target, sems.at[k]) for k, (source, target) in enumerate(late)]
    for copy in late:
        copy.start()

    for d in range(-2, 3):
        for e in range(-2, 3):
            here = ring.place(e)
            if d == 0:
                block = blocks_ref[here]
            else:
                there = jnp.where(odd, ring.place(e + 1), ring.place(e - 1))
                direct, swapped = (near_a, swap_a) if d > 0 else (near_b, swap_b)
                block = jnp.where(odd == (abs(d) == 1), direct[here], swapped[there])
            if e == -2:
                window_ref[d + 2, :, : tall // 2, :] = block[:, tall // 2 :, :]
            elif e == 2:
                window_ref[d + 2, :, 4 * tall - tall // 2 :, :] = block[:, : tall // 2, :]
            else:
                first = tall // 2 + (e + 1) * tall
                window_ref[d + 2, :, first : first + tall, :] = block

    for c in range(channels):
        x_ref[c * rows : (c + 1) * rows, :] = field_ref[c]
    previous, own, following = (window_ref[d, :, tall : 3 * tall, :] for d in (1, 2, 3))

    def turn(value, steps):
        flat = value.reshape(channels * 2 * tall, cols)
        return pltpu.roll(flat, steps % cols, 1).reshape(value.shape)

    def three(a, b, c):
        return jnp.where(lane < quarter, a, jnp.where(lane < 3 * quarter, b, c))

    even_rows = three(turn(previous, -quarter), turn(own, quarter), turn(following, -quarter))
    odd_rows = three(turn(previous, quarter), turn(own, -quarter), turn(following, quarter))
    for c in range(channels):
        first = (channels + c) * rows
        x_ref[pl.ds(first, 2 * tall, stride=2), :] = even_rows[c]
        x_ref[pl.ds(first + 1, 2 * tall, stride=2), :] = odd_rows[c]
    pieces = []
    for d in range(5):
        high, low = split(window_ref[d].reshape(channels * rows, cols))
        pieces.append(jnp.concatenate([high, low], axis=0))
    far = halves(dot(jnp.concatenate(pieces, axis=1), quarter_ref[...]))
    x_ref[2 * channels * rows : 3 * channels * rows, :] = far
    for c in range(3 * channels, padded):
        x_ref[c * rows : (c + 1) * rows, :] = jnp.zeros((rows, cols), F32)

    for i in range(rows):
        at = slice(i * cols, (i + 1) * cols)
        high, low = split(x_ref[pl.ds(i, padded, stride=rows), :])
        feature_pair[:padded, at] = high
        feature_pair[padded:, at] = low

    lift = lift_ref[...]
    lift_t = lift_t_ref[...]
    steps = [slice(k, k + chunk) for k in range(0, cells, chunk)]
    columns = [slice(i * cols, (i + 1) * cols) for i in range(rows)]
    part_count = parts_ref.shape[1] // cols
    part_columns = [slice(i * cols, (i + 1) * cols) for i in range(part_count)]

    def store_parts(band, values):
        for at, value in zip(part_columns, wave_forward(values)):
            parts_ref[band, at] = value

    def expanded(modes, band_rows):
        parts_ref[:band_rows, :] = halves(dot(stacked(modes), wave_t_ref[...]))

    def unfolded(band):
        return wave_backward([parts_ref[band, at] for at in part_columns], rows)

    bands = [slice(k, k + 8) for k in range(0, width, 8)]

    for k in range(0, padded, 8):
        store_parts(slice(k, k + 8), [x_ref[pl.ds(k * rows + i, 8, stride=rows), :] for i in range(rows)])
    local_product(local_ref, local_one[...], feature_pair, steps)
    modes = contract(parts_ref[:padded, :], wave_ref[...])
    expanded(mix(by_input, 0, exact_dot(lift_t, modes)), width)
    for band in bands:
        hidden = []
        for at, value in zip(columns, unfolded(band)):
            u = value + local_ref[band, at]
            cdf = 0.5 + 0.5 * lax.erf(u * SQRT_HALF)
            slope_one[band, at] = cdf + u * (INV_SQRT_2PI * jnp.exp(-0.5 * u * u))
            hidden.append(u * cdf)
            store_pair(hidden_pair, band.start, width, at, hidden[-1])
        store_parts(band, hidden)

    local_product(local_ref, local_two[...], hidden_pair, steps)
    modes = contract(parts_ref[...], wave_ref[...])
    expanded(mix(by_input, 1, modes), width)
    for band in bands:
        grads = []
        for at, value in zip(columns, unfolded(band)):
            u = value + local_ref[band, at]
            cdf = 0.5 + 0.5 * lax.erf(u * SQRT_HALF)
            slope = cdf + u * (INV_SQRT_2PI * jnp.exp(-0.5 * u * u))
            grads.append(slope * target_grad[band, at])
            store_pair(hidden_pair, band.start, width, at, grads[-1])
        store_parts(band, grads)
    local_product(local_ref, back_two[...], hidden_pair, steps)
    modes = contract(parts_ref[...], wave_ref[...])
    late[0].wait()
    expanded(unmix(by_output, 1, modes), width)
    for band in bands:
        grads = []
        for at, value in zip(columns, unfolded(band)):
            grads.append((value + local_ref[band, at]) * slope_one[band, at])
            store_pair(hidden_pair, band.start, width, at, grads[-1])
        store_parts(band, grads)

    local_product(local_ref.at[:padded], back_one[...], hidden_pair, steps)
    modes = contract(parts_ref[...], wave_ref[...])
    expanded(exact_dot(lift, unmix(by_output, 0, modes)), padded)
    for k in range(0, padded, 8):
        band = slice(k, k + 8)
        for i, (at, value) in enumerate(zip(columns, unfolded(band))):
            grad_x_ref[pl.ds(k * rows + i, 8, stride=rows), :] = value + local_ref[band, at]

    for c in range(channels):
        own_ref[c] = grad_x_ref[c * rows : (c + 1) * rows, :]

    even_grads, odd_grads = [], []
    for c in range(channels):
        first = (channels + c) * rows
        even_grads.append(grad_x_ref[pl.ds(first, 2 * tall, stride=2), :][None])
        odd_grads.append(grad_x_ref[pl.ds(first + 1, 2 * tall, stride=2), :][None])
    even_grads = jnp.concatenate(even_grads, axis=0)
    odd_grads = jnp.concatenate(odd_grads, axis=0)
    even_up, even_down = turn(even_grads, quarter), turn(even_grads, -quarter)
    odd_up, odd_down = turn(odd_grads, quarter), turn(odd_grads, -quarter)
    zero = jnp.zeros_like(even_grads)

    def four(a, b, c, d):
        return jnp.where(lane < quarter, a, jnp.where(lane < half, b, jnp.where(lane < 3 * quarter, c, d)))

    near = {
        -1: four(zero, even_up, zero, odd_down),
        0: four(even_down, even_down, odd_up, odd_up),
        1: four(even_up, zero, odd_down, zero),
    }
    late[1].wait()
    high, low = split(grad_x_ref[2 * channels * rows : 3 * channels * rows, :])
    spread = halves(dot(jnp.concatenate([high, low], axis=0), quarter_t_ref[...]))
    for d in range(5):
        window_ref[d] = spread[:, d * cols : (d + 1) * cols].reshape(channels, rows, cols)
    for d in (-1, 0, 1):
        window_ref[d + 2, :, tall : 3 * tall, :] += near[d]

    def block_of(d, e):
        if abs(e) < 2:
            first = tall // 2 + (e + 1) * tall
            return window_ref[d + 2, :, first : first + tall, :]
        low_part = window_ref[d + 2, :, 4 * tall - tall // 2 :, :]
        high_part = window_ref[d + 2, :, : tall // 2, :]
        if not (ring.whole and ring.count == 4):
            low_part, high_part = (low_part, jnp.zeros_like(low_part)) if e > 0 else (jnp.zeros_like(low_part), high_part)
        return jnp.concatenate([low_part, high_part], axis=1)

    reached = {}
    for e in range(-2, 3):
        reached[ring.place(e)] = e
    for place in range(len(ring.offsets)):
        if place not in reached:
            for ref in (center_ref, keep_a, keep_b, give_a, give_b):
                ref[place] = jnp.zeros((channels, tall, cols), F32)
            continue
        e = reached[place]
        center_ref[place] = block_of(0, e)
        for one, two, keep, give in ((-1, -2, keep_a, give_a), (1, 2, keep_b, give_b)):
            near_block, far_block = block_of(one, e), block_of(two, e)
            keep[place] = jnp.where(odd, near_block, far_block)
            give[place] = jnp.where(odd, far_block, near_block)


def join_kernel(ring, core_ref, keep_a, keep_b, got_a, got_b, out_a, out_b):
    odd = core_ref[0] == 1
    for offset in ring.offsets:
        here = ring.place(offset)
        there = jnp.where(odd, ring.place(offset + 1), ring.place(offset - 1))
        out_a[here] = keep_a[here] + got_a[there]
        out_b[here] = keep_b[here] + got_b[there]


def gather_kernel(center_ref, a_ref, b_ref, *outs):
    for place, out in enumerate(outs):
        out[...] = center_ref[place] + a_ref[place] + b_ref[place]


def final_kernel(own_ref, *refs):
    out_ref = refs[-1]
    total = refs[0][...]
    for ref in refs[1:-1]:
        total = total + ref[...]
    cols = total.shape[2]
    spread = dot_t(total.reshape(-1, cols), pool_matrix(cols))
    count = spread.shape[0]
    for k in range(4):
        part = spread[:, :cols] if k < 2 else spread[:, cols:]
        at = pl.ds(k, count, stride=4)
        out_ref[at, :] = own_ref[at, :] + part


def in_memory(count, space=pltpu.VMEM):
    return [pl.BlockSpec(memory_space=space)] * count


SCALAR = pl.BlockSpec(memory_space=pltpu.SMEM)


def call(kernel, shapes, *operands, scalars=0, scratch=(), name=None, limit=8 << 20, in_place=False, far=(), out_far=()):
    single = not isinstance(shapes, (list, tuple))
    if in_place:
        operands = [pltpu.with_memory_space_constraint(operand, pltpu.HBM) for operand in operands]
    outs = [shapes] if single else list(shapes)
    if in_place:
        far = range(scalars, len(operands))
    places = [SCALAR] * scalars + in_memory(len(operands) - scalars)
    for k in far:
        places[k] = pl.BlockSpec(memory_space=pltpu.HBM)
    out_places = in_memory(len(outs))
    for k in out_far:
        out_places[k] = pl.BlockSpec(memory_space=pltpu.HBM)
        outs[k] = pltpu.HBM(outs[k].shape, outs[k].dtype)
    result = pl.pallas_call(
        kernel,
        out_shape=outs,
        in_specs=places,
        out_specs=out_places,
        scratch_shapes=list(scratch),
        compiler_params=pltpu.CompilerParams(vmem_limit_bytes=limit),
        name=name,
    )(*operands)
    return result[0] if single else result


def body(field, cotangent, lift, spectral, pointwise, project):
    channels, levels, rows, cols = field.shape
    width = lift.shape[1]
    layers = spectral.shape[0]
    modes = spectral.shape[2]
    features = lift.shape[0]
    cells = rows * cols
    tall = rows // 4
    gx, gy = lax.axis_size("gx"), lax.axis_size("gy")
    ring = Ring(gx)
    blocks = len(ring.offsets)
    core = (lax.axis_index("gx") % 2).astype(jnp.int32).reshape(1)

    def shape(*dims, dtype=F32):
        return jax.ShapeDtypeStruct(dims, dtype)

    def along_x(value, steps):
        return lax.ppermute(value, "gx", [(s, (s + steps) % gx) for s in range(gx)])

    def along_y(value, even_steps, odd_steps):
        pairs = []
        for a in range(gx):
            for b in range(gy):
                steps = odd_steps if a % 2 else even_steps
                pairs.append((a * gy + b, a * gy + (b + steps) % gy))
        return lax.ppermute(value, ("gx", "gy"), pairs)

    def swap(value):
        return lax.ppermute(value, "gx", [(s, s ^ 1) for s in range(gx)])

    flat_field = field.reshape(channels * rows, cols)
    packed = call(pool_kernel, shape(channels * tall, cols), flat_field, name="pool")
    packed = packed.reshape(channels, tall, cols)

    held = [packed] + [along_x(packed, -offset) for offset in ring.offsets[1:]]
    wave = wave_matrix(rows, cols)
    padded = -(-features // 16) * 16
    small = -(-channels // 8) * 8
    quarter = quarter_matrix(cols)
    constants = [jnp.asarray(quarter, BF16), wave_pair(wave, 1), wave_pair(wave.T, 0)]
    packed_weights = shape(layers, width, width, 2 * modes)
    prepared = list(call(
        prepare_kernel,
        [shape(*c.shape, dtype=BF16) for c in constants]
        + [
            packed_weights, packed_weights, shape(padded, width), shape(width, padded), shape(width, 3 * padded, dtype=BF16),
            shape(width, 3 * width, dtype=BF16), shape(width, 3 * width, dtype=BF16), shape(padded, 3 * width, dtype=BF16),
            shape(width, cells),
        ],
        cotangent.reshape(channels * rows, cols), lift, jnp.transpose(spectral, (0, 1, 3, 4, 2)), pointwise, project.T,
        *constants,
        in_place=True, out_far=(4,),
        scratch=(
            pltpu.VMEM((layers, 2, width, width, modes), F32),
            pltpu.VMEM(packed_weights.shape, F32),
            pltpu.VMEM((small * rows, cols), F32),
            pltpu.VMEM((padded, width), F32),
            pltpu.VMEM((layers, width, width), F32),
            pltpu.VMEM((small, width), F32),
            pltpu.SemaphoreType.DMA((7 + 2 * layers,)),
        ),
        limit=16 << 20,
        name="prepare",
    ))
    by_output = prepared.pop(4)
    quarter_t = jnp.asarray(quarter.T.copy(), BF16)
    held = jnp.stack(held)
    from_a = along_y(held, -2, -1)
    from_b = along_y(held, 2, 1)
    from_a, from_b, prepared[4] = lax.optimization_barrier((from_a, from_b, prepared[4]))
    swap_a, swap_b = swap(from_a), swap(from_b)

    group = shape(blocks, channels, tall, cols)
    chunk = 4 * cols
    own, center, keep_a, keep_b, give_a, give_b = call(
        functools.partial(network_kernel, ring, chunk),
        (shape(channels, rows, cols), group, group, group, group, group),
        core, field.reshape(channels, rows, cols), held, from_a, from_b, swap_a, swap_b,
        *(pltpu.with_memory_space_constraint(value, pltpu.HBM) for value in (quarter_t, by_output)), *prepared,
        scalars=1, far=(7, 8),
        scratch=(
            pltpu.VMEM((padded * rows, cols), F32),
            pltpu.VMEM((5, channels, rows, cols), F32),
            pltpu.VMEM((2 * padded, cells), BF16),
            pltpu.VMEM((2 * width, cells), BF16),
            pltpu.VMEM((width, cells), F32),
            pltpu.VMEM((width, cells), F32),
            pltpu.VMEM((padded * rows, cols), F32),
            pltpu.VMEM((width, wave.shape[0]), F32),
            pltpu.VMEM(quarter_t.shape, BF16),
            pltpu.VMEM(packed_weights.shape, F32),
            pltpu.SemaphoreType.DMA((2,)),
        ),
        limit=16 << 20,
        name="network",
    )

    got_a, got_b = swap(give_a), swap(give_b)
    sum_a, sum_b = call(
        functools.partial(join_kernel, ring), (group, group), core, keep_a, keep_b, got_a, got_b, scalars=1, name="join"
    )
    sum_a, sum_b = along_y(sum_a, -2, -1), along_y(sum_b, 2, 1)
    piece = shape(channels, tall, cols)
    parts = call(gather_kernel, [piece] * blocks, center, sum_a, sum_b, name="gather")
    parts = [parts[0]] + [along_x(part, offset) for part, offset in zip(parts[1:], ring.offsets[1:])]
    out = call(
        final_kernel,
        shape(channels * rows, cols),
        own.reshape(channels * rows, cols), *parts,
        name="final",
    )
    return out.reshape(field.shape)


def solution(mesh):
    return jax.shard_map(
        body,
        mesh=mesh,
        in_specs=(P(None, None, "gx", "gy"), P(None, None, "gx", "gy"), P(), P(), P(), P()),
        out_specs=P(None, None, "gx", "gy"),
        check_vma=False,
    )
```

```python
import functools

import jax
import jax.numpy as jnp
import numpy as np
from jax import lax
from jax.experimental import pallas as pl
from jax.experimental.pallas import tpu as pltpu
from jax.sharding import PartitionSpec as P

MODES = 8
F32 = jnp.float32
BF16 = jnp.bfloat16
HIGHEST = lax.Precision.HIGHEST
SQRT_HALF = float(np.sqrt(0.5))
INV_SQRT_2PI = float(1.0 / np.sqrt(2.0 * np.pi))


class Chip:
    def __init__(self, count, channels):
        self.ring = count == 4
        self.offsets = [0, -1, 1, 2] if self.ring else [0, -1, 1, 2, -2, 3, -3]
        self.returned = [0, 1, 2, -1] if self.ring else [0, 1, 2, 3, -3, -2, -1]
        self.shared = [0, 1, 2, -1] if self.ring else [-2, -1, 0, 1, 2, 3]
        self.edge_tiles = channels + (channels + 1) // 2
        self.tiles = self.edge_tiles + channels * -(-len(self.shared) // 4)

    def place(self, offset):
        return self.offsets.index((offset + 1) % 4 - 1 if self.ring else offset)

    def group(self, offset):
        return offset % 4 if self.ring else self.shared.index(offset)

    def within(self, offset):
        return self.ring or offset in self.shared

    def quarter_tile(self, channel, group):
        channels = (self.tiles - self.edge_tiles) // -(-len(self.shared) // 4)
        return self.edge_tiles + (group // 4) * channels + channel


def split(value):
    high = value.astype(BF16)
    return high, (value - high.astype(F32)).astype(BF16)


def dot(left, right):
    return jnp.dot(left, right, preferred_element_type=F32)


def dot_t(left, right):
    return lax.dot_general(left, right, (((1,), (1,)), ((), ())), precision=HIGHEST, preferred_element_type=F32)


def exact_dot(left, right):
    return jnp.dot(left, right, precision=HIGHEST, preferred_element_type=F32)


def stacked(value):
    high, low = split(value)
    top = jnp.concatenate([high, high], axis=1)
    bottom = jnp.concatenate([low, jnp.zeros_like(low)], axis=1)
    return jnp.concatenate([top, bottom], axis=0)


def halves(value):
    rows = value.shape[0] // 2
    return value[:rows] + value[rows:]


def wave_matrix(rows, cols):
    m = np.arange(MODES * MODES)
    wave_x, wave_y = m // MODES - MODES // 2, m % MODES
    b = 2.0 * np.pi * ((np.arange(cols)[:, None] * wave_y[None]) % cols) / cols
    scale = 1.0 / np.sqrt(rows * cols)
    cos, sin = np.cos(b) * scale, np.sin(b) * scale
    parts = []
    for k in range(MODES // 2 + 1):
        held = (np.abs(wave_x) == k)[None]
        parts.append(np.concatenate([cos * held, -sin * held], 1))
    for k in range(1, MODES // 2 + 1):
        held = (np.sign(wave_x) * (np.abs(wave_x) == k))[None]
        parts.append(np.concatenate([-sin * held, -cos * held], 1))
    return np.concatenate(parts, 0).astype(np.float32)


def wave_pair(matrix, axis):
    high = matrix.astype(BF16)
    low = (matrix - high.astype(np.float32)).astype(BF16)
    return jnp.asarray(np.concatenate([high, low], axis))


def weighted(terms):
    groups = {}
    for factor, value in terms:
        size = round(abs(factor), 12)
        if size == 0:
            continue
        groups.setdefault(size, []).append((factor > 0, value, abs(factor)))
    total = None
    for size, members in groups.items():
        members.sort(key=lambda member: not member[0])
        part = members[0][1] if members[0][0] else -members[0][1]
        for positive, value, _ in members[1:]:
            part = part + value if positive else part - value
        if size != 1:
            part = part * members[0][2]
        total = part if total is None else total + part
    return total


def wave_forward(values):
    n = len(values)
    top = MODES // 2
    angle = lambda k, i: 2.0 * np.pi * ((k * i) % n) / n
    plus = [values[0]] + [values[i] + values[n - i] for i in range(1, n // 2)] + [values[n // 2]]
    minus = [None] + [values[i] - values[n - i] for i in range(1, n // 2)]
    even = [plus[i] + plus[n // 2 - i] for i in range(n // 4)] + [plus[n // 4]]
    odd = [plus[i] - plus[n // 2 - i] for i in range(n // 4)]
    minus_odd = [None] + [minus[i] + minus[n // 2 - i] for i in range(1, n // 4)] + [minus[n // 4]]
    minus_even = [None] + [minus[i] - minus[n // 2 - i] for i in range(1, n // 4)]
    deep = {
        1: [even[i] + even[n // 4 - i] for i in range(n // 8)],
        -1: [even[i] - even[n // 4 - i] for i in range(n // 8)],
    }
    deep_minus = {
        1: [None] + [minus_even[i] - minus_even[n // 4 - i] for i in range(1, n // 8)],
        -1: [None] + [minus_even[i] + minus_even[n // 4 - i] for i in range(1, n // 8)],
    }
    out = []
    for k in range(top + 1):
        if k % 2:
            out.append(weighted([(np.cos(angle(k, i)), odd[i]) for i in range(n // 4)]))
        else:
            sign = 1 if k % 4 == 0 else -1
            terms = [(np.cos(angle(k, i)), deep[sign][i]) for i in range(n // 8)]
            out.append(weighted(terms + [(np.cos(angle(k, n // 8)), even[n // 8])]))
    for k in range(1, top + 1):
        if k % 2:
            out.append(weighted([(np.sin(angle(k, i)), minus_odd[i]) for i in range(1, n // 4 + 1)]))
        else:
            sign = 1 if k % 4 == 0 else -1
            terms = [(np.sin(angle(k, i)), deep_minus[sign][i]) for i in range(1, n // 8)]
            out.append(weighted(terms + [(np.sin(angle(k, n // 8)), minus_even[n // 8])]))
    return out


def added(a, b):
    return b if a is None else a if b is None else a + b


def taken(a, b):
    return a if b is None else -b if a is None else a - b


def wave_backward(parts, n):
    top = MODES // 2
    angle = lambda k, i: 2.0 * np.pi * ((k * i) % n) / n
    cosine = lambda i, ks: weighted([(np.cos(angle(k, i)), parts[k]) for k in ks])
    sine = lambda i, ks: weighted([(np.sin(angle(k, i)), parts[top + k]) for k in ks])
    fours = [k for k in range(top + 1) if k % 4 == 0]
    twos = [k for k in range(top + 1) if k % 4 == 2]
    odds = [k for k in range(top + 1) if k % 2]
    even = [None] * (n // 4 + 1)
    for i in range(n // 8):
        a, b = cosine(i, fours), cosine(i, twos)
        even[i], even[n // 4 - i] = added(a, b), taken(a, b)
    even[n // 8] = cosine(n // 8, sorted(fours + twos))
    plus = [None] * (n // 2 + 1)
    for i in range(n // 4):
        b = cosine(i, odds)
        plus[i], plus[n // 2 - i] = added(even[i], b), taken(even[i], b)
    plus[n // 4] = even[n // 4]
    minus_even = [None] * (n // 4)
    for i in range(1, n // 8):
        a, b = sine(i, [k for k in fours if k]), sine(i, twos)
        minus_even[i], minus_even[n // 4 - i] = added(b, a), taken(b, a)
    minus_even[n // 8] = sine(n // 8, sorted(k for k in fours + twos if k))
    minus = [None] * (n // 2)
    for i in range(1, n // 4):
        a = sine(i, odds)
        minus[i], minus[n // 2 - i] = added(a, minus_even[i]), taken(a, minus_even[i])
    minus[n // 4] = sine(n // 4, odds)
    out = [None] * n
    out[0], out[n // 2] = plus[0], plus[n // 2]
    for i in range(1, n // 2):
        out[i], out[n - i] = added(plus[i], minus[i]), taken(plus[i], minus[i])
    return out


def prepare_kernel(
    cotangent_hbm, lift_hbm, spectral_hbm, pointwise_hbm, project_hbm, *refs
):
    constants_hbm, refs = refs[:2], refs[2:]
    constants, refs = refs[:2], refs[2:]
    by_input, lift_ref, lift_t_ref, local_one, local_two, back_two, back_one, target_grad = refs[:8]
    spectral_ref, target_ref, lift_in, pointwise_ref, project_ref, sems = refs[8:]
    layers, _, width, _, modes = spectral_ref.shape
    small, cols = project_ref.shape[0], target_ref.shape[1]
    rows = target_ref.shape[0] // small
    channels, features = project_hbm.shape[0], lift_hbm.shape[0]
    pairs = [(spectral_hbm.at[layer], spectral_ref.at[layer]) for layer in range(layers)]
    pairs += [
        (cotangent_hbm, target_ref.at[: channels * rows]),
        (project_hbm, project_ref.at[:channels]),
        (lift_hbm, lift_in.at[:features]),
        (pointwise_hbm, pointwise_ref),
    ]
    pairs += list(zip(constants_hbm, constants))
    copies = [pltpu.make_async_copy(source, target, sems.at[k]) for k, (source, target) in enumerate(pairs)]
    for copy in copies:
        copy.start()
    target_ref[channels * rows :, :] = jnp.zeros(((small - channels) * rows, cols), F32)
    project_ref[channels:, :] = jnp.zeros((small - channels, width), F32)
    lift_in[features:, :] = jnp.zeros((lift_in.shape[0] - features, width), F32)
    for layer in range(layers):
        copies[layer].wait()
        for w in range(width):
            both = [spectral_ref[layer, part, w] for part in range(2)]
            by_input[layer, w] = jnp.concatenate(both, axis=1)
    for copy in copies[layers : layers + 4]:
        copy.wait()

    lift = lift_in[...]
    lift_t = jnp.transpose(lift)
    lift_ref[...] = lift
    lift_t_ref[...] = lift_t
    back_one[...] = tripled(exact_dot(lift, pointwise_ref[0]))
    local_one[...] = tripled(exact_dot(jnp.transpose(pointwise_ref[0]), lift_t))
    local_two[...] = tripled(jnp.transpose(pointwise_ref[1]))
    back_two[...] = tripled(pointwise_ref[1])
    out = tripled(jnp.transpose(project_ref[...]))
    group = 4
    for first in range(0, rows, group):
        pieces = []
        for i in range(first, first + group):
            value = target_ref[pl.ds(i, small, stride=rows), :]
            high = value.astype(BF16).astype(F32)
            pieces.append(jnp.concatenate([high, value - high, high], axis=0).astype(BF16))
        target_grad[:, first * cols : (first + group) * cols] = dot(out, jnp.concatenate(pieces, axis=1))

    for copy in copies[4 + layers :]:
        copy.wait()


def index_of(shape, axis):
    return lax.broadcasted_iota(jnp.int32, shape, axis)


def quarter_matrix(cols, flipped=False):
    shape = (2 * cols, cols)
    fine, coarse = (index_of(shape, 1), index_of(shape, 0)) if flipped else (index_of(shape, 0), index_of(shape, 1))
    fine, coarse = fine % (cols // 2) // 2, coarse % (cols // 4)
    return jnp.where(fine == coarse, 0.25, 0.0).astype(BF16)


def spread_matrix(cols):
    shape = (2 * cols, 2 * cols)
    row, col = index_of(shape, 0) % cols, index_of(shape, 1)
    return jnp.where(row == col // 2, 0.25, 0.0).astype(BF16)


def pooling_matrix(cols):
    shape = (2 * cols, cols)
    return jnp.where(index_of(shape, 0) // 2 == index_of(shape, 1), 0.25, 0.0).astype(BF16)


def beside(value):
    return jnp.concatenate(split(value), axis=1)


def above(value):
    return jnp.concatenate(split(value), axis=0)


def turned(value, steps):
    lanes = value.shape[-1]
    if steps % lanes == 0:
        return value
    flat = value.reshape(-1, lanes)
    return pltpu.roll(flat, steps % lanes, 1).reshape(value.shape)


def by_group(values, lanes):
    lane = index_of((1,) * (values[0].ndim - 1) + (lanes,), values[0].ndim - 1)
    q = lanes // 4
    low = jnp.where(lane < q, values[0], values[1])
    high = jnp.where(lane < 3 * q, values[2], values[3])
    return jnp.where(lane < 2 * q, low, high)


def pool_kernel(field_ref, out_ref):
    count = field_ref.shape[0] // 4
    rows = [field_ref[pl.ds(k, count, stride=4), :] for k in range(4)]
    pairs = jnp.concatenate([rows[0] + rows[1], rows[2] + rows[3]], axis=1)
    out_ref[...] = halves(dot(above(pairs), pooling_matrix(field_ref.shape[1])))


def pack_kernel(chip, core_ref, *refs):
    blocks, (to_previous, to_following) = refs[: len(chip.offsets)], refs[len(chip.offsets) :]
    channels, tall, cols = blocks[0].shape
    q = cols // 4
    odd = core_ref[0] == 1
    sub = index_of((1, tall, cols), 1)
    shared = {}
    for e in chip.shared:
        even_at, odd_at = chip.place(e), (chip.place(e - 1))
        shared[e] = jnp.where(odd, blocks[odd_at][...], blocks[even_at][...])
    stacked_rows = jnp.concatenate([shared[e].reshape(channels * tall, cols) for e in chip.shared], axis=0)
    coarse = dot(beside(stacked_rows), quarter_matrix(cols)).reshape(len(chip.shared), channels, tall, cols)
    for first in range(0, len(chip.shared), 4):
        groups = [min(first + k, len(chip.shared) - 1) for k in range(4)]
        tile = by_group([coarse[k] for k in groups], cols)
        at = chip.quarter_tile(0, first)
        to_previous[at : at + channels] = tile
        to_following[at : at + channels] = tile
    outer = jnp.where(sub < tall // 2, shared[2], shared[-1])

    def pair(one, two, shifts):
        return by_group([turned(v, k * q) for v, k in zip((one, one, two, two), shifts)], cols)

    for ref, shifts in ((to_previous, (0, -1, 2, 1)), (to_following, (-1, -2, 1, 0))):
        ref[:channels] = pair(shared[0], shared[1], shifts)
        for c in range(0, channels, 2):
            ref[channels + c // 2] = pair(outer[c], outer[min(c + 1, channels - 1)], shifts)


def mix(weights, layer, coefficients):
    width, lanes = coefficients.shape
    half = lanes // 2
    lane = lax.broadcasted_iota(jnp.int32, (width, lanes), 1)
    swapped = pltpu.roll(coefficients, half, 1)
    signed = jnp.where(lane < half, coefficients, -coefficients)
    total_real = jnp.zeros((width, lanes), F32)
    total_imag = jnp.zeros((width, lanes), F32)
    for w in range(width):
        block = weights[layer, w]
        total_real += block * signed[w : w + 1]
        total_imag += block * swapped[w : w + 1]
    total_real += pltpu.roll(total_real, half, 1)
    total_imag += pltpu.roll(total_imag, half, 1)
    return jnp.where(lane < half, total_real, total_imag)


def rows_summed(values):
    row = index_of(values[0].shape, 0)
    step = 1
    while len(values) > 1:
        held = (row & step) != 0
        values = [
            jnp.where(held, x, y) + pltpu.roll(jnp.where(held, y, x), step, 0) for y, x in zip(values[::2], values[1::2])
        ]
        step *= 2
    return values[0]


def unmix(weights, layer, grads):
    width, lanes = grads.shape
    half = lanes // 2
    lane = index_of((width, lanes), 1)
    turned_grads = pltpu.roll(grads, half, 1)
    turned_grads = jnp.where(lane < half, turned_grads, -turned_grads)

    def folded(block, value):
        product = block * value
        return sum(product[k : k + 8] for k in range(8, width, 8)) + product[:8]

    real, imag = [], []
    for first in range(0, width, 8):
        blocks = [weights[layer, w] for w in range(first, first + 8)]
        real.append(rows_summed([folded(block, grads) for block in blocks]))
        imag.append(rows_summed([folded(block, turned_grads) for block in blocks]))
    real, imag = jnp.concatenate(real, axis=0), jnp.concatenate(imag, axis=0)
    real += pltpu.roll(real, half, 1)
    imag += pltpu.roll(imag, half, 1)
    return jnp.where(lane < half, real, imag)


def contract(parts, wave):
    high, low = split(parts)
    both = dot(jnp.concatenate([high, low], axis=0), wave)
    rows, modes = both.shape[0] // 2, both.shape[1] // 2
    return both[:rows, :modes] + both[:rows, modes:] + both[rows:, :modes]


def tripled(value):
    high, low = split(value)
    return jnp.concatenate([high, high, low], axis=1)


def local_product(out_ref, left, pair_ref, steps):
    rows = pair_ref.shape[0] // 2
    for at in steps:
        right = jnp.concatenate([pair_ref[:, at], pair_ref[:rows, at]], axis=0)
        out_ref[:, at] = dot(left, right)


def store_pair(pair_ref, first, rows_total, at, value):
    high, low = split(value)
    count = value.shape[0]
    pair_ref[first : first + count, at] = high
    pair_ref[rows_total + first : rows_total + first + count, at] = low


def network_kernel(
    chip, chunk,
    core_ref, field_ref, here_ref, after_ref, before_ref, mine_ref, got_after, got_before, other_after, other_before,
    wave_ref, wave_t_ref, by_input, lift_ref, lift_t_ref, local_one, local_two, back_two, back_one, target_grad,
    own_ref, center_edge, center_quarter, keep_a, keep_b, give_a, give_b,
    x_ref, even_ref, odd_ref, mid_ref, far_ref, far_blocks, feature_pair, hidden_pair, slope_one, local_ref, grad_x_ref, parts_ref,
):
    channels, rows, cols = field_ref.shape
    tall = rows // 4
    q = cols // 4
    cells = rows * cols
    width = slope_one.shape[0]
    padded = x_ref.shape[0] // rows
    odd = core_ref[0] == 1
    shift = core_ref[0] * tall
    lane = index_of((1, 1, cols), 2)
    for c in range(channels):
        x_ref[c * rows : (c + 1) * rows, :] = field_ref[c]
    mid_ref[:, : tall // 2, :] = before_ref[:, tall // 2 :, :]
    mid_ref[:, tall // 2 : tall // 2 + tall, :] = here_ref[...]
    mid_ref[:, tall // 2 + tall :, :] = after_ref[:, : tall // 2, :]
    edges = slice(0, chip.edge_tiles)
    previous = jnp.where(odd, got_before[edges], other_before[edges])
    following = jnp.where(odd, got_after[edges], other_after[edges])
    first = tall // 2
    for ref, shifts in ((even_ref, ((0, 3), (2, 1))), (odd_ref, ((-1, 2), (1, 0)))):
        one, two = (
            jnp.where(lane < 2 * q, turned(previous, a * q), turned(following, b * q)) for a, b in shifts
        )
        ref[:, first : first + tall, :] = one[:channels]
        ref[:, first + tall : first + 2 * tall, :] = two[:channels]
        for c in range(channels):
            outer = (two if c % 2 else one)[channels + c // 2]
            ref[c, :first, :] = outer[first:]
            ref[c, first + 2 * tall :, :] = outer[:first]
    middle = (lane >= q) & (lane < 3 * q)
    own = mid_ref[...]
    even_rows = jnp.where(middle, turned(own, q), even_ref[:, pl.ds(shift, 2 * tall), :])
    odd_rows = jnp.where(middle, turned(own, -q), odd_ref[:, pl.ds(shift, 2 * tall), :])
    for c in range(channels):
        at = (channels + c) * rows
        x_ref[pl.ds(at, 2 * tall, stride=2), :] = even_rows[c]
        x_ref[pl.ds(at + 1, 2 * tall, stride=2), :] = odd_rows[c]
    eighth = q // 2
    starts = {-2: -eighth, -1: eighth, 0: 3 * eighth, 1: 5 * eighth, 2: 7 * eighth}
    spans = {e: (e, first + (e + 1) * tall, slice(0, tall)) for e in (-1, 0, 1, 2)}
    spans[-2] = (-2, 0, slice(first, tall))
    spans[3] = (3, first + 4 * tall, slice(0, first))
    for group in range(len(chip.shared)):
        at = chip.quarter_tile(0, group)
        at = slice(at, at + channels)
        columns = {
            -2: jnp.where(odd, other_before[at], got_before[at]),
            -1: jnp.where(odd, got_before[at], other_before[at]),
            0: mine_ref[at],
            1: jnp.where(odd, got_after[at], other_after[at]),
            2: jnp.where(odd, other_after[at], got_after[at]),
        }
        value = turned(columns[2], starts[2] - group % 4 * q)
        for d in (1, 0, -1, -2):
            value = jnp.where(lane < starts[d + 1], turned(columns[d], starts[d] - group % 4 * q), value)
        for e, row, part in spans.values():
            if chip.within(e) and chip.group(e) == group:
                far_ref[:, row : row + part.stop - part.start, :] = value[:, part, :]
    far = far_ref[:, pl.ds(shift, rows), :]
    for c in range(channels):
        x_ref[(2 * channels + c) * rows : (2 * channels + c + 1) * rows, :] = far[c]
    for c in range(3 * channels, padded):
        x_ref[c * rows : (c + 1) * rows, :] = jnp.zeros((rows, cols), F32)

    for i in range(rows):
        at = slice(i * cols, (i + 1) * cols)
        high, low = split(x_ref[pl.ds(i, padded, stride=rows), :])
        feature_pair[:padded, at] = high
        feature_pair[padded:, at] = low

    lift = lift_ref[...]
    lift_t = lift_t_ref[...]
    steps = [slice(k, k + chunk) for k in range(0, cells, chunk)]
    columns = [slice(i * cols, (i + 1) * cols) for i in range(rows)]
    part_count = parts_ref.shape[1] // cols
    part_columns = [slice(i * cols, (i + 1) * cols) for i in range(part_count)]

    def store_parts(band, values):
        for at, value in zip(part_columns, wave_forward(values)):
            parts_ref[band, at] = value

    def expanded(modes, band_rows):
        parts_ref[:band_rows, :] = halves(dot(stacked(modes), wave_t_ref[...]))

    def unfolded(band):
        return wave_backward([parts_ref[band, at] for at in part_columns], rows)

    bands = [slice(k, k + 8) for k in range(0, width, 8)]

    for k in range(0, padded, 8):
        store_parts(slice(k, k + 8), [x_ref[pl.ds(k * rows + i, 8, stride=rows), :] for i in range(rows)])
    local_product(local_ref, local_one[...], feature_pair, steps)
    modes = contract(parts_ref[:padded, :], wave_ref[...])
    expanded(mix(by_input, 0, exact_dot(lift_t, modes)), width)
    for band in bands:
        hidden = []
        for at, value in zip(columns, unfolded(band)):
            u = value + local_ref[band, at]
            cdf = 0.5 + 0.5 * lax.erf(u * SQRT_HALF)
            slope_one[band, at] = cdf + u * (INV_SQRT_2PI * jnp.exp(-0.5 * u * u))
            hidden.append(u * cdf)
            store_pair(hidden_pair, band.start, width, at, hidden[-1])
        store_parts(band, hidden)

    local_product(local_ref, local_two[...], hidden_pair, steps)
    modes = contract(parts_ref[...], wave_ref[...])
    expanded(mix(by_input, 1, modes), width)
    for band in bands:
        grads = []
        for at, value in zip(columns, unfolded(band)):
            u = value + local_ref[band, at]
            cdf = 0.5 + 0.5 * lax.erf(u * SQRT_HALF)
            slope = cdf + u * (INV_SQRT_2PI * jnp.exp(-0.5 * u * u))
            grads.append(slope * target_grad[band, at])
            store_pair(hidden_pair, band.start, width, at, grads[-1])
        store_parts(band, grads)
    local_product(local_ref, back_two[...], hidden_pair, steps)
    modes = contract(parts_ref[...], wave_ref[...])
    expanded(unmix(by_input, 1, modes), width)
    for band in bands:
        grads = []
        for at, value in zip(columns, unfolded(band)):
            grads.append((value + local_ref[band, at]) * slope_one[band, at])
            store_pair(hidden_pair, band.start, width, at, grads[-1])
        store_parts(band, grads)

    local_product(local_ref.at[:padded], back_one[...], hidden_pair, steps)
    modes = contract(parts_ref[...], wave_ref[...])
    expanded(exact_dot(lift, unmix(by_input, 0, modes)), padded)
    for k in range(0, padded, 8):
        band = slice(k, k + 8)
        for i, (at, value) in enumerate(zip(columns, unfolded(band))):
            grad_x_ref[pl.ds(k * rows + i, 8, stride=rows), :] = value + local_ref[band, at]

    for c in range(channels):
        own_ref[c] = grad_x_ref[c * rows : (c + 1) * rows, :]

    even_grads, odd_grads = [], []
    for c in range(channels):
        at = (channels + c) * rows
        even_grads.append(grad_x_ref[pl.ds(at, 2 * tall, stride=2), :][None])
        odd_grads.append(grad_x_ref[pl.ds(at + 1, 2 * tall, stride=2), :][None])
    even_grads = jnp.concatenate(even_grads, axis=0)
    odd_grads = jnp.concatenate(odd_grads, axis=0)
    center_edge[...] = jnp.where(lane < 2 * q, turned(even_grads, -q), turned(odd_grads, q))
    for ref, value in ((even_ref, even_grads), (odd_ref, odd_grads)):
        ref[...] = jnp.zeros_like(ref)
        ref[:, pl.ds(shift, 2 * tall), :] = value

    def edge_tiles(shifts):
        def pair(one, two):
            return by_group([turned(v, k * q) for v, k in zip((*one, *two), shifts)], cols)

        refs = (even_ref, odd_ref)
        inner = pair(*([ref[:, first + k * tall : first + (k + 1) * tall, :] for ref in refs] for k in (0, 1)))
        outer = [jnp.concatenate([ref[:, first + 2 * tall :, :], ref[:, :first, :]], axis=1) for ref in refs]
        tiles = [inner]
        for c in range(0, channels, 2):
            other = min(c + 1, channels - 1)
            tiles.append(pair([v[c] for v in outer], [v[other] for v in outer])[None])
        return jnp.concatenate(tiles, axis=0)

    near = {-1: edge_tiles((0, 1, 2, 3)), 1: edge_tiles((1, 2, 3, 0))}
    for one, keep, give in ((-1, keep_a, give_a), (1, keep_b, give_b)):
        zero = jnp.zeros_like(near[one])
        keep[: chip.edge_tiles] = jnp.where(odd, near[one], zero)
        give[: chip.edge_tiles] = jnp.where(odd, zero, near[one])
    far_ref[...] = jnp.zeros_like(far_ref)
    for c in range(channels):
        at = (2 * channels + c) * rows
        far_ref[c, pl.ds(shift, rows), :] = grad_x_ref[at : at + rows, :]
    far_blocks[...] = jnp.zeros_like(far_blocks)
    for e in (-1, 0, 1, 2, -2, 3):
        if chip.within(e):
            _, row, part = spans[e]
            far_blocks[chip.group(e), :, part, :] += far_ref[:, row : row + part.stop - part.start, :]
    for start in range(0, len(chip.shared), 4):
        groups = [min(start + k, len(chip.shared) - 1) for k in range(4)]
        at = chip.quarter_tile(0, start)
        at = slice(at, at + channels)
        tiles = {}
        for d in range(-2, 3):
            value = by_group([turned(far_blocks[g], k * q - starts[d]) for k, g in enumerate(groups)], cols)
            if abs(d) == 2:
                value = jnp.where((lane % q >= eighth) == (d < 0), value, 0.0)
            tiles[d] = value
        center_quarter[at.start - chip.edge_tiles : at.stop - chip.edge_tiles] = tiles[0]
        for one, two, keep, give in ((-1, -2, keep_a, give_a), (1, 2, keep_b, give_b)):
            keep[at] = jnp.where(odd, tiles[one], tiles[two])
            give[at] = jnp.where(odd, tiles[two], tiles[one])


def join_kernel(keep_b, keep_a, got_b, got_a, out_b, out_a):
    out_b[...] = keep_b[...] + got_b[...]
    out_a[...] = keep_a[...] + got_a[...]


def gather_kernel(chip, core_ref, center_edge, center_quarter, from_before, from_after, *outs):
    channels, _, cols = center_edge.shape
    tall = from_after.shape[1]
    q, first = cols // 4, tall // 2
    odd = core_ref[0] == 1
    sub = index_of((1, tall, cols), 1)
    lane = index_of((1, 1, cols), 2)
    edges = chip.edge_tiles
    coarse = center_quarter[...] + from_after[edges:] + from_before[edges:]
    rows = []
    for group in range(len(chip.shared)):
        at = chip.quarter_tile(0, group) - edges
        value = jnp.where(lane // q == group % 4, coarse[at : at + channels], 0.0)
        rows.append(value.reshape(channels * tall, cols))
    shared = dot(beside(jnp.concatenate(rows, axis=0)), quarter_matrix(cols, flipped=True))
    shared = shared.reshape(len(chip.shared), channels, tall, cols)
    tail, head = from_after[:edges], from_before[:edges]

    def unpaired(moves):
        return by_group([turned(v, k * q) for v, k in zip((head, tail, head, tail), moves)], cols)

    one, two = unpaired((0, 1, 1, 2)), unpaired((-2, -1, -1, 0))
    outer = [(two if c % 2 else one)[channels + c // 2][None] for c in range(channels)]
    outer = jnp.concatenate(outer, axis=0)
    edge = {
        0: one[:channels],
        1: two[:channels],
        2: jnp.where(sub < first, outer, 0.0),
        -1: jnp.where(sub < first, 0.0, outer),
    }
    shared = {e: shared[chip.group(e)] + edge[e] if e in edge else shared[chip.group(e)] for e in chip.shared}
    if chip.ring:
        shared[3] = shared[-1]
    zero = jnp.zeros((channels, tall, cols), F32)
    blank = zero[:, :first]
    own = {
        -1: jnp.concatenate([blank, center_edge[:, :first, :]], axis=1),
        0: center_edge[:, first : first + tall, :],
        1: jnp.concatenate([center_edge[:, first + tall :, :], blank], axis=1),
    }
    for out, e in zip(outs, chip.returned):
        value = jnp.where(odd, shared.get(e + 1, zero), shared.get(e, zero))
        out[...] = value + own[e] if e in own else value


def final_kernel(own_ref, *refs):
    out_ref = refs[-1]
    total = refs[0][...]
    for ref in refs[1:-1]:
        total = total + ref[...]
    cols = total.shape[2]
    spread = dot(beside(total.reshape(-1, cols)), spread_matrix(cols))
    count = spread.shape[0]
    for k in range(4):
        part = spread[:, :cols] if k < 2 else spread[:, cols:]
        at = pl.ds(k, count, stride=4)
        out_ref[at, :] = own_ref[at, :] + part


def in_memory(count, space=pltpu.VMEM):
    return [pl.BlockSpec(memory_space=space)] * count


SCALAR = pl.BlockSpec(memory_space=pltpu.SMEM)


def call(kernel, shapes, *operands, scalars=0, scratch=(), name=None, limit=8 << 20, in_place=False, far=(), out_far=()):
    single = not isinstance(shapes, (list, tuple))
    if in_place:
        operands = [pltpu.with_memory_space_constraint(operand, pltpu.HBM) for operand in operands]
    outs = [shapes] if single else list(shapes)
    if in_place:
        far = range(scalars, len(operands))
    places = [SCALAR] * scalars + in_memory(len(operands) - scalars)
    for k in far:
        places[k] = pl.BlockSpec(memory_space=pltpu.HBM)
    out_places = in_memory(len(outs))
    for k in out_far:
        out_places[k] = pl.BlockSpec(memory_space=pltpu.HBM)
        outs[k] = pltpu.HBM(outs[k].shape, outs[k].dtype)
    result = pl.pallas_call(
        kernel,
        out_shape=outs,
        in_specs=places,
        out_specs=out_places,
        scratch_shapes=list(scratch),
        compiler_params=pltpu.CompilerParams(vmem_limit_bytes=limit),
        name=name,
    )(*operands)
    return result[0] if single else result


def body(field, cotangent, lift, spectral, pointwise, project):
    channels, levels, rows, cols = field.shape
    width = lift.shape[1]
    layers = spectral.shape[0]
    modes = spectral.shape[2]
    features = lift.shape[0]
    cells = rows * cols
    tall = rows // 4
    gx, gy = lax.axis_size("gx"), lax.axis_size("gy")
    chip = Chip(gx, channels)
    core = (lax.axis_index("gx") % 2).astype(jnp.int32).reshape(1)

    def shape(*dims, dtype=F32):
        return jax.ShapeDtypeStruct(dims, dtype)

    def along_x(value, steps):
        return lax.ppermute(value, "gx", [(s, (s + steps) % gx) for s in range(gx)])

    def along_y(value, even_steps, odd_steps):
        pairs = []
        for a in range(gx):
            for b in range(gy):
                steps = odd_steps if a % 2 else even_steps
                pairs.append((a * gy + b, a * gy + (b + steps) % gy))
        return lax.ppermute(value, ("gx", "gy"), pairs)

    def swap(value):
        return lax.ppermute(value, "gx", [(s, s ^ 1) for s in range(gx)])

    flat_field = field.reshape(channels * rows, cols)
    packed = call(pool_kernel, shape(channels * tall, cols), flat_field, name="pool")
    packed = packed.reshape(channels, tall, cols)

    held = [packed] + [along_x(packed, -offset) for offset in chip.offsets[1:]]
    wave = wave_matrix(rows, cols)
    padded = -(-features // 16) * 16
    small = -(-channels // 8) * 8
    constants = [wave_pair(wave, 1), wave_pair(wave.T, 0)]
    packed_weights = shape(layers, width, width, 2 * modes)
    prepared = list(call(
        prepare_kernel,
        [shape(*c.shape, dtype=BF16) for c in constants]
        + [
            packed_weights, shape(padded, width), shape(width, padded), shape(width, 3 * padded, dtype=BF16),
            shape(width, 3 * width, dtype=BF16), shape(width, 3 * width, dtype=BF16), shape(padded, 3 * width, dtype=BF16),
            shape(width, cells),
        ],
        cotangent.reshape(channels * rows, cols), lift, jnp.transpose(spectral, (0, 1, 3, 4, 2)), pointwise, project.T,
        *constants,
        in_place=True,
        scratch=(
            pltpu.VMEM((layers, 2, width, width, modes), F32),
            pltpu.VMEM((small * rows, cols), F32),
            pltpu.VMEM((padded, width), F32),
            pltpu.VMEM((layers, width, width), F32),
            pltpu.VMEM((small, width), F32),
            pltpu.SemaphoreType.DMA((6 + layers,)),
        ),
        limit=16 << 20,
        name="prepare",
    ))
    message = shape(chip.tiles, tall, cols)
    to_previous, to_following = call(
        functools.partial(pack_kernel, chip), (message, message), core, *held, scalars=1, name="pack"
    )
    from_a = along_y(to_previous, -2, -1)
    from_b = along_y(to_following, 2, 1)
    from_a, from_b, prepared[3] = lax.optimization_barrier((from_a, from_b, prepared[3]))
    swap_a, swap_b = swap(from_a), swap(from_b)

    chunk = 4 * cols
    quarter_part = shape(chip.tiles - chip.edge_tiles, tall, cols)
    own, center_edge, center_quarter, keep_a, keep_b, give_a, give_b = call(
        functools.partial(network_kernel, chip, chunk),
        (shape(channels, rows, cols), shape(channels, 2 * tall, cols), quarter_part, message, message, message, message),
        core, field.reshape(channels, rows, cols), held[0], held[chip.place(1)], held[chip.place(-1)],
        to_previous, from_a, from_b, swap_a, swap_b, *prepared,
        scalars=1,
        scratch=(
            pltpu.VMEM((padded * rows, cols), F32),
            pltpu.VMEM((channels, 3 * tall, cols), F32),
            pltpu.VMEM((channels, 3 * tall, cols), F32),
            pltpu.VMEM((channels, 2 * tall, cols), F32),
            pltpu.VMEM((channels, rows + tall, cols), F32),
            pltpu.VMEM((len(chip.shared), channels, tall, cols), F32),
            pltpu.VMEM((2 * padded, cells), BF16),
            pltpu.VMEM((2 * width, cells), BF16),
            pltpu.VMEM((width, cells), F32),
            pltpu.VMEM((width, cells), F32),
            pltpu.VMEM((padded * rows, cols), F32),
            pltpu.VMEM((width, wave.shape[0]), F32),
        ),
        limit=16 << 20,
        name="network",
    )

    got_a, got_b = swap(give_a), swap(give_b)
    sum_b, sum_a = call(join_kernel, (message, message), keep_b, keep_a, got_b, got_a, name="join")
    sum_b = along_y(sum_b, 2, 1)
    sum_a = along_y(sum_a, -2, -1)
    parts = call(
        functools.partial(gather_kernel, chip),
        [shape(channels, tall, cols)] * len(chip.offsets),
        core, center_edge, center_quarter, sum_b, sum_a, scalars=1,
        name="gather",
    )
    parts = [parts[0]] + [along_x(part, offset) for part, offset in zip(parts[1:], chip.returned[1:])]
    out = call(
        final_kernel,
        shape(channels * rows, cols),
        own.reshape(channels * rows, cols), *parts,
        name="final",
    )
    return out.reshape(field.shape)


def solution(mesh):
    return jax.shard_map(
        body,
        mesh=mesh,
        in_specs=(P(None, None, "gx", "gy"), P(None, None, "gx", "gy"), P(), P(), P(), P()),
        out_specs=P(None, None, "gx", "gy"),
        check_vma=False,
    )
```

```python
import functools

import jax
import jax.numpy as jnp
import numpy as np
from jax import lax
from jax.experimental import pallas as pl
from jax.experimental.pallas import tpu as pltpu
from jax.sharding import PartitionSpec as P

MODES = 8
F32 = jnp.float32
BF16 = jnp.bfloat16
HIGHEST = lax.Precision.HIGHEST
SQRT_HALF = float(np.sqrt(0.5))
INV_SQRT_2PI = float(1.0 / np.sqrt(2.0 * np.pi))


class Chip:
    def __init__(self, count, channels):
        self.count = count
        self.ring = count == 4
        if self.ring:
            self.slots = [(0, 0), (1, -1), (2, 2), (-1, 1)]
        else:
            self.slots = [(k, k) for k in (0, 1, 2, -1, -2, 3, -3)]
        self.shared = [0, 1, 2, -1] if self.ring else [-2, -1, 0, 1, 2, 3]
        self.edge_tiles = channels + (channels + 1) // 2
        self.tiles = self.edge_tiles + channels * -(-len(self.shared) // 4)

    def place(self, offset, odd):
        offset = (offset + 1) % 4 - 1 if self.ring else offset
        return [slot[odd] for slot in self.slots].index(offset)

    def pairs(self, slot, back=False):
        count = self.count
        if self.ring:
            return [(s, s ^ slot) for s in range(count)]
        steps = self.slots[slot][0] if back else -self.slots[slot][0]
        return [(s, (s + steps) % count) for s in range(count)]

    def group(self, offset):
        return offset % 4 if self.ring else self.shared.index(offset)

    def within(self, offset):
        return self.ring or offset in self.shared

    def quarter_tile(self, channel, group):
        channels = (self.tiles - self.edge_tiles) // -(-len(self.shared) // 4)
        return self.edge_tiles + (group // 4) * channels + channel


def split(value):
    high = value.astype(BF16)
    return high, (value - high.astype(F32)).astype(BF16)


def dot(left, right):
    return jnp.dot(left, right, preferred_element_type=F32)


def dot_t(left, right):
    return lax.dot_general(left, right, (((1,), (1,)), ((), ())), precision=HIGHEST, preferred_element_type=F32)


def exact_dot(left, right):
    return jnp.dot(left, right, precision=HIGHEST, preferred_element_type=F32)


def stacked(value):
    high, low = split(value)
    top = jnp.concatenate([high, high], axis=1)
    bottom = jnp.concatenate([low, jnp.zeros_like(low)], axis=1)
    return jnp.concatenate([top, bottom], axis=0)


def halves(value):
    rows = value.shape[0] // 2
    return value[:rows] + value[rows:]


def wave_matrix(rows, cols):
    m = np.arange(MODES * MODES)
    wave_x, wave_y = m // MODES - MODES // 2, m % MODES
    b = 2.0 * np.pi * ((np.arange(cols)[:, None] * wave_y[None]) % cols) / cols
    scale = 1.0 / np.sqrt(rows * cols)
    cos, sin = np.cos(b) * scale, np.sin(b) * scale
    parts = []
    for k in range(MODES // 2 + 1):
        held = (np.abs(wave_x) == k)[None]
        parts.append(np.concatenate([cos * held, -sin * held], 1))
    for k in range(1, MODES // 2 + 1):
        held = (np.sign(wave_x) * (np.abs(wave_x) == k))[None]
        parts.append(np.concatenate([-sin * held, -cos * held], 1))
    return np.concatenate(parts, 0).astype(np.float32)


def wave_pair(matrix, axis):
    high = matrix.astype(BF16)
    low = (matrix - high.astype(np.float32)).astype(BF16)
    return jnp.asarray(np.concatenate([high, low], axis))


def weighted(terms):
    groups = {}
    for factor, value in terms:
        size = round(abs(factor), 12)
        if size == 0:
            continue
        groups.setdefault(size, []).append((factor > 0, value, abs(factor)))
    total = None
    for size, members in groups.items():
        members.sort(key=lambda member: not member[0])
        part = members[0][1] if members[0][0] else -members[0][1]
        for positive, value, _ in members[1:]:
            part = part + value if positive else part - value
        if size != 1:
            part = part * members[0][2]
        total = part if total is None else total + part
    return total


def wave_forward(values):
    n = len(values)
    top = MODES // 2
    angle = lambda k, i: 2.0 * np.pi * ((k * i) % n) / n
    plus = [values[0]] + [values[i] + values[n - i] for i in range(1, n // 2)] + [values[n // 2]]
    minus = [None] + [values[i] - values[n - i] for i in range(1, n // 2)]
    even = [plus[i] + plus[n // 2 - i] for i in range(n // 4)] + [plus[n // 4]]
    odd = [plus[i] - plus[n // 2 - i] for i in range(n // 4)]
    minus_odd = [None] + [minus[i] + minus[n // 2 - i] for i in range(1, n // 4)] + [minus[n // 4]]
    minus_even = [None] + [minus[i] - minus[n // 2 - i] for i in range(1, n // 4)]
    deep = {
        1: [even[i] + even[n // 4 - i] for i in range(n // 8)],
        -1: [even[i] - even[n // 4 - i] for i in range(n // 8)],
    }
    deep_minus = {
        1: [None] + [minus_even[i] - minus_even[n // 4 - i] for i in range(1, n // 8)],
        -1: [None] + [minus_even[i] + minus_even[n // 4 - i] for i in range(1, n // 8)],
    }
    out = []
    for k in range(top + 1):
        if k % 2:
            out.append(weighted([(np.cos(angle(k, i)), odd[i]) for i in range(n // 4)]))
        else:
            sign = 1 if k % 4 == 0 else -1
            terms = [(np.cos(angle(k, i)), deep[sign][i]) for i in range(n // 8)]
            out.append(weighted(terms + [(np.cos(angle(k, n // 8)), even[n // 8])]))
    for k in range(1, top + 1):
        if k % 2:
            out.append(weighted([(np.sin(angle(k, i)), minus_odd[i]) for i in range(1, n // 4 + 1)]))
        else:
            sign = 1 if k % 4 == 0 else -1
            terms = [(np.sin(angle(k, i)), deep_minus[sign][i]) for i in range(1, n // 8)]
            out.append(weighted(terms + [(np.sin(angle(k, n // 8)), minus_even[n // 8])]))
    return out


def added(a, b):
    return b if a is None else a if b is None else a + b


def taken(a, b):
    return a if b is None else -b if a is None else a - b


def wave_backward(parts, n):
    top = MODES // 2
    angle = lambda k, i: 2.0 * np.pi * ((k * i) % n) / n
    cosine = lambda i, ks: weighted([(np.cos(angle(k, i)), parts[k]) for k in ks])
    sine = lambda i, ks: weighted([(np.sin(angle(k, i)), parts[top + k]) for k in ks])
    fours = [k for k in range(top + 1) if k % 4 == 0]
    twos = [k for k in range(top + 1) if k % 4 == 2]
    odds = [k for k in range(top + 1) if k % 2]
    even = [None] * (n // 4 + 1)
    for i in range(n // 8):
        a, b = cosine(i, fours), cosine(i, twos)
        even[i], even[n // 4 - i] = added(a, b), taken(a, b)
    even[n // 8] = cosine(n // 8, sorted(fours + twos))
    plus = [None] * (n // 2 + 1)
    for i in range(n // 4):
        b = cosine(i, odds)
        plus[i], plus[n // 2 - i] = added(even[i], b), taken(even[i], b)
    plus[n // 4] = even[n // 4]
    minus_even = [None] * (n // 4)
    for i in range(1, n // 8):
        a, b = sine(i, [k for k in fours if k]), sine(i, twos)
        minus_even[i], minus_even[n // 4 - i] = added(b, a), taken(b, a)
    minus_even[n // 8] = sine(n // 8, sorted(k for k in fours + twos if k))
    minus = [None] * (n // 2)
    for i in range(1, n // 4):
        a = sine(i, odds)
        minus[i], minus[n // 2 - i] = added(a, minus_even[i]), taken(a, minus_even[i])
    minus[n // 4] = sine(n // 4, odds)
    out = [None] * n
    out[0], out[n // 2] = plus[0], plus[n // 2]
    for i in range(1, n // 2):
        out[i], out[n - i] = added(plus[i], minus[i]), taken(plus[i], minus[i])
    return out


def prepare_kernel(
    cotangent_hbm, lift_hbm, spectral_hbm, pointwise_hbm, project_hbm, *refs
):
    constants_hbm, refs = refs[:2], refs[2:]
    constants, refs = refs[:2], refs[2:]
    by_input, lift_ref, lift_t_ref, local_one, local_two, back_two, back_one, target_grad = refs[:8]
    spectral_ref, target_ref, lift_in, pointwise_ref, project_ref, sems = refs[8:]
    layers, _, width, _, modes = spectral_ref.shape
    small, cols = project_ref.shape[0], target_ref.shape[1]
    rows = target_ref.shape[0] // small
    channels, features = project_hbm.shape[0], lift_hbm.shape[0]
    pairs = [
        (cotangent_hbm, target_ref.at[: channels * rows]),
        (project_hbm, project_ref.at[:channels]),
        (lift_hbm, lift_in.at[:features]),
        (pointwise_hbm, pointwise_ref),
    ]
    pairs += [(spectral_hbm.at[layer], spectral_ref.at[layer]) for layer in range(layers)]
    pairs += list(zip(constants_hbm, constants))
    copies = [pltpu.make_async_copy(source, target, sems.at[k]) for k, (source, target) in enumerate(pairs)]
    for copy in copies:
        copy.start()
    target_ref[channels * rows :, :] = jnp.zeros(((small - channels) * rows, cols), F32)
    project_ref[channels:, :] = jnp.zeros((small - channels, width), F32)
    lift_in[features:, :] = jnp.zeros((lift_in.shape[0] - features, width), F32)
    for copy in copies[:4]:
        copy.wait()

    lift = lift_in[...]
    lift_t = jnp.transpose(lift)
    lift_ref[...] = lift
    lift_t_ref[...] = lift_t
    back_one[...] = tripled(exact_dot(lift, pointwise_ref[0]))
    local_one[...] = tripled(exact_dot(jnp.transpose(pointwise_ref[0]), lift_t))
    local_two[...] = tripled(jnp.transpose(pointwise_ref[1]))
    back_two[...] = tripled(pointwise_ref[1])
    out = tripled(jnp.transpose(project_ref[...]))
    group = 4
    for first in range(0, rows, group):
        pieces = []
        for i in range(first, first + group):
            value = target_ref[pl.ds(i, small, stride=rows), :]
            high = value.astype(BF16).astype(F32)
            pieces.append(jnp.concatenate([high, value - high, high], axis=0).astype(BF16))
        target_grad[:, first * cols : (first + group) * cols] = dot(out, jnp.concatenate(pieces, axis=1))

    for layer in range(layers):
        copies[4 + layer].wait()
        for w in range(width):
            both = [spectral_ref[layer, part, w] for part in range(2)]
            by_input[layer, w] = jnp.concatenate(both, axis=1)
    for copy in copies[4 + layers :]:
        copy.wait()


def index_of(shape, axis):
    return lax.broadcasted_iota(jnp.int32, shape, axis)


def quarter_matrix(cols, flipped=False):
    shape = (2 * cols, cols)
    fine, coarse = (index_of(shape, 1), index_of(shape, 0)) if flipped else (index_of(shape, 0), index_of(shape, 1))
    fine, coarse = fine % (cols // 2) // 2, coarse % (cols // 4)
    return jnp.where(fine == coarse, 0.25, 0.0).astype(BF16)


def spread_matrix(cols):
    shape = (2 * cols, 2 * cols)
    row, col = index_of(shape, 0) % cols, index_of(shape, 1)
    return jnp.where(row == col // 2, 0.25, 0.0).astype(BF16)


def pooling_matrix(cols):
    shape = (2 * cols, cols)
    return jnp.where(index_of(shape, 0) // 2 == index_of(shape, 1), 0.25, 0.0).astype(BF16)


def beside(value):
    return jnp.concatenate(split(value), axis=1)


def above(value):
    return jnp.concatenate(split(value), axis=0)


def turned(value, steps):
    lanes = value.shape[-1]
    if steps % lanes == 0:
        return value
    flat = value.reshape(-1, lanes)
    return pltpu.roll(flat, steps % lanes, 1).reshape(value.shape)


def by_group(values, lanes):
    lane = index_of((1,) * (values[0].ndim - 1) + (lanes,), values[0].ndim - 1)
    q = lanes // 4
    low = jnp.where(lane < q, values[0], values[1])
    high = jnp.where(lane < 3 * q, values[2], values[3])
    return jnp.where(lane < 2 * q, low, high)


def pool_kernel(field_ref, out_ref):
    count = field_ref.shape[0] // 4
    rows = [field_ref[pl.ds(k, count, stride=4), :] for k in range(4)]
    pairs = jnp.concatenate([rows[0] + rows[1], rows[2] + rows[3]], axis=1)
    out_ref[...] = halves(dot(above(pairs), pooling_matrix(field_ref.shape[1])))


def pack_kernel(chip, core_ref, *refs):
    blocks, (to_previous, to_following) = refs[: len(chip.slots)], refs[len(chip.slots) :]
    channels, tall, cols = blocks[0].shape
    q = cols // 4
    odd = core_ref[0] == 1
    sub = index_of((1, tall, cols), 1)
    shared = {}
    for e in chip.shared:
        even_at, odd_at = chip.place(e, 0), chip.place(e - 1, 1)
        shared[e] = jnp.where(odd, blocks[odd_at][...], blocks[even_at][...])
    stacked_rows = jnp.concatenate([shared[e].reshape(channels * tall, cols) for e in chip.shared], axis=0)
    coarse = dot(beside(stacked_rows), quarter_matrix(cols)).reshape(len(chip.shared), channels, tall, cols)
    for first in range(0, len(chip.shared), 4):
        groups = [min(first + k, len(chip.shared) - 1) for k in range(4)]
        tile = by_group([coarse[k] for k in groups], cols)
        at = chip.quarter_tile(0, first)
        to_previous[at : at + channels] = tile
        to_following[at : at + channels] = tile
    outer = jnp.where(sub < tall // 2, shared[2], shared[-1])

    def pair(one, two, shifts):
        return by_group([turned(v, k * q) for v, k in zip((one, one, two, two), shifts)], cols)

    for ref, shifts in ((to_previous, (0, -1, 2, 1)), (to_following, (-1, -2, 1, 0))):
        ref[:channels] = pair(shared[0], shared[1], shifts)
        for c in range(0, channels, 2):
            ref[channels + c // 2] = pair(outer[c], outer[min(c + 1, channels - 1)], shifts)


def mix(weights, layer, coefficients):
    width, lanes = coefficients.shape
    half = lanes // 2
    lane = lax.broadcasted_iota(jnp.int32, (width, lanes), 1)
    swapped = pltpu.roll(coefficients, half, 1)
    signed = jnp.where(lane < half, coefficients, -coefficients)
    total_real, total_imag = [None] * 2, [None] * 2
    for w in range(width):
        block = weights[layer, w]
        total_real[w % 2] = added(total_real[w % 2], block * signed[w : w + 1])
        total_imag[w % 2] = added(total_imag[w % 2], block * swapped[w : w + 1])
    total_real, total_imag = sum(total_real), sum(total_imag)
    total_real += pltpu.roll(total_real, half, 1)
    total_imag += pltpu.roll(total_imag, half, 1)
    return jnp.where(lane < half, total_real, total_imag)


def rows_summed(values):
    row = index_of(values[0].shape, 0)
    step = 1
    while len(values) > 1:
        held = (row & step) != 0
        values = [
            jnp.where(held, x, y) + pltpu.roll(jnp.where(held, y, x), step, 0) for y, x in zip(values[::2], values[1::2])
        ]
        step *= 2
    return values[0]


def unmix(weights, layer, grads):
    width, lanes = grads.shape
    half = lanes // 2
    lane = index_of((width, lanes), 1)
    turned_grads = pltpu.roll(grads, half, 1)
    turned_grads = jnp.where(lane < half, turned_grads, -turned_grads)

    def folded(block, value):
        product = block * value
        return sum(product[k : k + 8] for k in range(8, width, 8)) + product[:8]

    real, imag = [], []
    for first in range(0, width, 8):
        blocks = [weights[layer, w] for w in range(first, first + 8)]
        real.append(rows_summed([folded(block, grads) for block in blocks]))
        imag.append(rows_summed([folded(block, turned_grads) for block in blocks]))
    real, imag = jnp.concatenate(real, axis=0), jnp.concatenate(imag, axis=0)
    real += pltpu.roll(real, half, 1)
    imag += pltpu.roll(imag, half, 1)
    return jnp.where(lane < half, real, imag)


def contract(parts, wave):
    high, low = split(parts)
    both = dot(jnp.concatenate([high, low], axis=0), wave)
    rows, modes = both.shape[0] // 2, both.shape[1] // 2
    return both[:rows, :modes] + both[:rows, modes:] + both[rows:, :modes]


def tripled(value):
    high, low = split(value)
    return jnp.concatenate([high, high, low], axis=1)


def local_product(out_ref, left, pair_ref, steps):
    rows = pair_ref.shape[0] // 2
    for at in steps:
        right = jnp.concatenate([pair_ref[:, at], pair_ref[:rows, at]], axis=0)
        out_ref[:, at] = dot(left, right)


def store_pair(pair_ref, first, rows_total, at, value):
    high, low = split(value)
    count = value.shape[0]
    pair_ref[first : first + count, at] = high
    pair_ref[rows_total + first : rows_total + first + count, at] = low


def network_kernel(
    chip, chunk,
    core_ref, field_ref, here_ref, next_ref, last_ref, mine_ref, got_after, got_before, other_after, other_before,
    wave_ref, wave_t_ref, by_input, lift_ref, lift_t_ref, local_one, local_two, back_two, back_one, target_grad,
    own_ref, center_edge, center_quarter, keep_a, keep_b, give_a, give_b,
    x_ref, even_ref, odd_ref, mid_ref, far_ref, far_blocks, feature_pair, hidden_pair, slope_one, local_ref, grad_x_ref, parts_ref,
):
    channels, rows, cols = field_ref.shape
    tall = rows // 4
    q = cols // 4
    cells = rows * cols
    width = slope_one.shape[0]
    padded = x_ref.shape[0] // rows
    odd = core_ref[0] == 1
    shift = core_ref[0] * tall
    lane = index_of((1, 1, cols), 2)
    for c in range(channels):
        x_ref[c * rows : (c + 1) * rows, :] = field_ref[c]
    before, after = last_ref[...], next_ref[...]
    if chip.ring:
        before, after = jnp.where(odd, after, before), jnp.where(odd, before, after)
    mid_ref[:, : tall // 2, :] = before[:, tall // 2 :, :]
    mid_ref[:, tall // 2 : tall // 2 + tall, :] = here_ref[...]
    mid_ref[:, tall // 2 + tall :, :] = after[:, : tall // 2, :]
    edges = slice(0, chip.edge_tiles)
    previous = jnp.where(odd, got_before[edges], other_before[edges])
    following = jnp.where(odd, got_after[edges], other_after[edges])
    first = tall // 2
    for ref, shifts in ((even_ref, ((0, 3), (2, 1))), (odd_ref, ((-1, 2), (1, 0)))):
        one, two = (
            jnp.where(lane < 2 * q, turned(previous, a * q), turned(following, b * q)) for a, b in shifts
        )
        ref[:, first : first + tall, :] = one[:channels]
        ref[:, first + tall : first + 2 * tall, :] = two[:channels]
        for c in range(channels):
            outer = (two if c % 2 else one)[channels + c // 2]
            ref[c, :first, :] = outer[first:]
            ref[c, first + 2 * tall :, :] = outer[:first]
    middle = (lane >= q) & (lane < 3 * q)
    own = mid_ref[...]
    even_rows = jnp.where(middle, turned(own, q), even_ref[:, pl.ds(shift, 2 * tall), :])
    odd_rows = jnp.where(middle, turned(own, -q), odd_ref[:, pl.ds(shift, 2 * tall), :])
    for c in range(channels):
        at = (channels + c) * rows
        x_ref[pl.ds(at, 2 * tall, stride=2), :] = even_rows[c]
        x_ref[pl.ds(at + 1, 2 * tall, stride=2), :] = odd_rows[c]
    eighth = q // 2
    starts = {-2: -eighth, -1: eighth, 0: 3 * eighth, 1: 5 * eighth, 2: 7 * eighth}
    spans = {e: (e, first + (e + 1) * tall, slice(0, tall)) for e in (-1, 0, 1, 2)}
    spans[-2] = (-2, 0, slice(first, tall))
    spans[3] = (3, first + 4 * tall, slice(0, first))
    for group in range(len(chip.shared)):
        at = chip.quarter_tile(0, group)
        at = slice(at, at + channels)
        columns = {
            -2: jnp.where(odd, other_before[at], got_before[at]),
            -1: jnp.where(odd, got_before[at], other_before[at]),
            0: mine_ref[at],
            1: jnp.where(odd, got_after[at], other_after[at]),
            2: jnp.where(odd, other_after[at], got_after[at]),
        }
        value = turned(columns[2], starts[2] - group % 4 * q)
        for d in (1, 0, -1, -2):
            value = jnp.where(lane < starts[d + 1], turned(columns[d], starts[d] - group % 4 * q), value)
        for e, row, part in spans.values():
            if chip.within(e) and chip.group(e) == group:
                far_ref[:, row : row + part.stop - part.start, :] = value[:, part, :]
    far = far_ref[:, pl.ds(shift, rows), :]
    for c in range(channels):
        x_ref[(2 * channels + c) * rows : (2 * channels + c + 1) * rows, :] = far[c]
    for c in range(3 * channels, padded):
        x_ref[c * rows : (c + 1) * rows, :] = jnp.zeros((rows, cols), F32)

    for i in range(rows):
        at = slice(i * cols, (i + 1) * cols)
        value = x_ref[pl.ds(i, padded, stride=rows), :]
        local_ref[:padded, at] = value
        high, low = split(value)
        feature_pair[:padded, at] = high
        feature_pair[padded:, at] = low

    lift = lift_ref[...]
    lift_t = lift_t_ref[...]
    steps = [slice(k, k + chunk) for k in range(0, cells, chunk)]
    columns = [slice(i * cols, (i + 1) * cols) for i in range(rows)]
    part_count = parts_ref.shape[1] // cols
    part_columns = [slice(i * cols, (i + 1) * cols) for i in range(part_count)]

    def store_parts(band, values):
        for at, value in zip(part_columns, wave_forward(values)):
            parts_ref[band, at] = value

    def expanded(modes, band_rows):
        parts_ref[:band_rows, :] = halves(dot(stacked(modes), wave_t_ref[...]))

    def unfolded(band):
        return wave_backward([parts_ref[band, at] for at in part_columns], rows)

    bands = [slice(k, k + 8) for k in range(0, width, 8)]

    for k in range(0, padded, 8):
        store_parts(slice(k, k + 8), [local_ref[k : k + 8, at] for at in columns])
    local_product(local_ref, local_one[...], feature_pair, steps)
    modes = contract(parts_ref[:padded, :], wave_ref[...])
    expanded(mix(by_input, 0, exact_dot(lift_t, modes)), width)
    for band in bands:
        hidden = []
        for at, value in zip(columns, unfolded(band)):
            u = value + local_ref[band, at]
            cdf = 0.5 + 0.5 * lax.erf(u * SQRT_HALF)
            slope_one[band, at] = cdf + u * (INV_SQRT_2PI * jnp.exp(-0.5 * u * u))
            hidden.append(u * cdf)
            store_pair(hidden_pair, band.start, width, at, hidden[-1])
        store_parts(band, hidden)

    local_product(local_ref, local_two[...], hidden_pair, steps)
    modes = contract(parts_ref[...], wave_ref[...])
    expanded(mix(by_input, 1, modes), width)
    for band in bands:
        grads = []
        for at, value in zip(columns, unfolded(band)):
            u = value + local_ref[band, at]
            cdf = 0.5 + 0.5 * lax.erf(u * SQRT_HALF)
            slope = cdf + u * (INV_SQRT_2PI * jnp.exp(-0.5 * u * u))
            grads.append(slope * target_grad[band, at])
            store_pair(hidden_pair, band.start, width, at, grads[-1])
        store_parts(band, grads)
    local_product(local_ref, back_two[...], hidden_pair, steps)
    modes = contract(parts_ref[...], wave_ref[...])
    expanded(unmix(by_input, 1, modes), width)
    for band in bands:
        grads = []
        for at, value in zip(columns, unfolded(band)):
            grads.append((value + local_ref[band, at]) * slope_one[band, at])
            store_pair(hidden_pair, band.start, width, at, grads[-1])
        store_parts(band, grads)

    local_product(local_ref.at[:padded], back_one[...], hidden_pair, steps)
    modes = contract(parts_ref[...], wave_ref[...])
    expanded(exact_dot(lift, unmix(by_input, 0, modes)), padded)
    for k in range(0, padded, 8):
        band = slice(k, k + 8)
        for i, (at, value) in enumerate(zip(columns, unfolded(band))):
            grad_x_ref[pl.ds(k * rows + i, 8, stride=rows), :] = value + local_ref[band, at]

    for c in range(channels):
        own_ref[c] = grad_x_ref[c * rows : (c + 1) * rows, :]

    even_grads, odd_grads = [], []
    for c in range(channels):
        at = (channels + c) * rows
        even_grads.append(grad_x_ref[pl.ds(at, 2 * tall, stride=2), :][None])
        odd_grads.append(grad_x_ref[pl.ds(at + 1, 2 * tall, stride=2), :][None])
    even_grads = jnp.concatenate(even_grads, axis=0)
    odd_grads = jnp.concatenate(odd_grads, axis=0)
    center_edge[...] = jnp.where(lane < 2 * q, turned(even_grads, -q), turned(odd_grads, q))
    for ref, value in ((even_ref, even_grads), (odd_ref, odd_grads)):
        ref[...] = jnp.zeros_like(ref)
        ref[:, pl.ds(shift, 2 * tall), :] = value

    def edge_tiles(shifts):
        def pair(one, two):
            return by_group([turned(v, k * q) for v, k in zip((*one, *two), shifts)], cols)

        refs = (even_ref, odd_ref)
        inner = pair(*([ref[:, first + k * tall : first + (k + 1) * tall, :] for ref in refs] for k in (0, 1)))
        outer = [jnp.concatenate([ref[:, first + 2 * tall :, :], ref[:, :first, :]], axis=1) for ref in refs]
        tiles = [inner]
        for c in range(0, channels, 2):
            other = min(c + 1, channels - 1)
            tiles.append(pair([v[c] for v in outer], [v[other] for v in outer])[None])
        return jnp.concatenate(tiles, axis=0)

    near = {-1: edge_tiles((0, 1, 2, 3)), 1: edge_tiles((1, 2, 3, 0))}
    for one, keep, give in ((-1, keep_a, give_a), (1, keep_b, give_b)):
        zero = jnp.zeros_like(near[one])
        keep[: chip.edge_tiles] = jnp.where(odd, near[one], zero)
        give[: chip.edge_tiles] = jnp.where(odd, zero, near[one])
    far_ref[...] = jnp.zeros_like(far_ref)
    for c in range(channels):
        at = (2 * channels + c) * rows
        far_ref[c, pl.ds(shift, rows), :] = grad_x_ref[at : at + rows, :]
    far_blocks[...] = jnp.zeros_like(far_blocks)
    for e in (-1, 0, 1, 2, -2, 3):
        if chip.within(e):
            _, row, part = spans[e]
            far_blocks[chip.group(e), :, part, :] += far_ref[:, row : row + part.stop - part.start, :]
    for start in range(0, len(chip.shared), 4):
        groups = [min(start + k, len(chip.shared) - 1) for k in range(4)]
        at = chip.quarter_tile(0, start)
        at = slice(at, at + channels)
        tiles = {}
        for d in range(-2, 3):
            value = by_group([turned(far_blocks[g], k * q - starts[d]) for k, g in enumerate(groups)], cols)
            if abs(d) == 2:
                value = jnp.where((lane % q >= eighth) == (d < 0), value, 0.0)
            tiles[d] = value
        center_quarter[at.start - chip.edge_tiles : at.stop - chip.edge_tiles] = tiles[0]
        for one, two, keep, give in ((-1, -2, keep_a, give_a), (1, 2, keep_b, give_b)):
            keep[at] = jnp.where(odd, tiles[one], tiles[two])
            give[at] = jnp.where(odd, tiles[two], tiles[one])


def join_kernel(keep_b, keep_a, got_b, got_a, out_b, out_a):
    out_b[...] = keep_b[...] + got_b[...]
    out_a[...] = keep_a[...] + got_a[...]


def gather_kernel(chip, core_ref, center_edge, center_quarter, from_before, from_after, *outs):
    channels, _, cols = center_edge.shape
    tall = from_after.shape[1]
    q, first = cols // 4, tall // 2
    odd = core_ref[0] == 1
    sub = index_of((1, tall, cols), 1)
    lane = index_of((1, 1, cols), 2)
    edges = chip.edge_tiles
    coarse = center_quarter[...] + from_after[edges:] + from_before[edges:]
    rows = []
    for group in range(len(chip.shared)):
        at = chip.quarter_tile(0, group) - edges
        value = jnp.where(lane // q == group % 4, coarse[at : at + channels], 0.0)
        rows.append(value.reshape(channels * tall, cols))
    shared = dot(beside(jnp.concatenate(rows, axis=0)), quarter_matrix(cols, flipped=True))
    shared = shared.reshape(len(chip.shared), channels, tall, cols)
    tail, head = from_after[:edges], from_before[:edges]

    def unpaired(moves):
        return by_group([turned(v, k * q) for v, k in zip((head, tail, head, tail), moves)], cols)

    one, two = unpaired((0, 1, 1, 2)), unpaired((-2, -1, -1, 0))
    outer = [(two if c % 2 else one)[channels + c // 2][None] for c in range(channels)]
    outer = jnp.concatenate(outer, axis=0)
    edge = {
        0: one[:channels],
        1: two[:channels],
        2: jnp.where(sub < first, outer, 0.0),
        -1: jnp.where(sub < first, 0.0, outer),
    }
    shared = {e: shared[chip.group(e)] + edge[e] if e in edge else shared[chip.group(e)] for e in chip.shared}
    if chip.ring:
        shared[3] = shared[-1]
    zero = jnp.zeros((channels, tall, cols), F32)
    blank = zero[:, :first]
    own = {
        -1: jnp.concatenate([blank, center_edge[:, :first, :]], axis=1),
        0: center_edge[:, first : first + tall, :],
        1: jnp.concatenate([center_edge[:, first + tall :, :], blank], axis=1),
    }
    def block_of(offset, is_odd):
        value = shared.get(offset + is_odd, zero)
        return value + own[offset] if offset in own else value

    for out, (even_offset, odd_offset) in zip(outs, chip.slots):
        out[...] = jnp.where(odd, block_of(odd_offset, 1), block_of(even_offset, 0))


def final_kernel(own_ref, *refs):
    out_ref = refs[-1]
    total = refs[0][...]
    for ref in refs[1:-1]:
        total = total + ref[...]
    cols = total.shape[2]
    spread = dot(beside(total.reshape(-1, cols)), spread_matrix(cols))
    count = spread.shape[0]
    for k in range(4):
        part = spread[:, :cols] if k < 2 else spread[:, cols:]
        at = pl.ds(k, count, stride=4)
        out_ref[at, :] = own_ref[at, :] + part


def in_memory(count, space=pltpu.VMEM):
    return [pl.BlockSpec(memory_space=space)] * count


SCALAR = pl.BlockSpec(memory_space=pltpu.SMEM)


def call(kernel, shapes, *operands, scalars=0, scratch=(), name=None, limit=8 << 20, in_place=False, far=(), out_far=()):
    single = not isinstance(shapes, (list, tuple))
    if in_place:
        operands = [pltpu.with_memory_space_constraint(operand, pltpu.HBM) for operand in operands]
    outs = [shapes] if single else list(shapes)
    if in_place:
        far = range(scalars, len(operands))
    places = [SCALAR] * scalars + in_memory(len(operands) - scalars)
    for k in far:
        places[k] = pl.BlockSpec(memory_space=pltpu.HBM)
    out_places = in_memory(len(outs))
    for k in out_far:
        out_places[k] = pl.BlockSpec(memory_space=pltpu.HBM)
        outs[k] = pltpu.HBM(outs[k].shape, outs[k].dtype)
    result = pl.pallas_call(
        kernel,
        out_shape=outs,
        in_specs=places,
        out_specs=out_places,
        scratch_shapes=list(scratch),
        compiler_params=pltpu.CompilerParams(vmem_limit_bytes=limit),
        name=name,
    )(*operands)
    return result[0] if single else result


def body(field, cotangent, lift, spectral, pointwise, project):
    channels, levels, rows, cols = field.shape
    width = lift.shape[1]
    layers = spectral.shape[0]
    modes = spectral.shape[2]
    features = lift.shape[0]
    cells = rows * cols
    tall = rows // 4
    gx, gy = lax.axis_size("gx"), lax.axis_size("gy")
    chip = Chip(gx, channels)
    core = (lax.axis_index("gx") % 2).astype(jnp.int32).reshape(1)

    def shape(*dims, dtype=F32):
        return jax.ShapeDtypeStruct(dims, dtype)

    def along_y(value, even_steps, odd_steps):
        pairs = []
        for a in range(gx):
            for b in range(gy):
                steps = odd_steps if a % 2 else even_steps
                pairs.append((a * gy + b, a * gy + (b + steps) % gy))
        return lax.ppermute(value, ("gx", "gy"), pairs)

    def swap(value):
        return lax.ppermute(value, "gx", [(s, s ^ 1) for s in range(gx)])

    flat_field = field.reshape(channels * rows, cols)
    packed = call(pool_kernel, shape(channels * tall, cols), flat_field, name="pool")
    packed = packed.reshape(channels, tall, cols)

    others = range(1, len(chip.slots))
    held = [packed] + [lax.ppermute(packed, "gx", chip.pairs(slot)) for slot in others]
    wave = wave_matrix(rows, cols)
    padded = -(-features // 16) * 16
    small = -(-channels // 8) * 8
    constants = [wave_pair(wave, 1), wave_pair(wave.T, 0)]
    packed_weights = shape(layers, width, width, 2 * modes)
    prepared = list(call(
        prepare_kernel,
        [shape(*c.shape, dtype=BF16) for c in constants]
        + [
            packed_weights, shape(padded, width), shape(width, padded), shape(width, 3 * padded, dtype=BF16),
            shape(width, 3 * width, dtype=BF16), shape(width, 3 * width, dtype=BF16), shape(padded, 3 * width, dtype=BF16),
            shape(width, cells),
        ],
        cotangent.reshape(channels * rows, cols), lift, jnp.transpose(spectral, (0, 1, 3, 4, 2)), pointwise, project.T,
        *constants,
        in_place=True,
        scratch=(
            pltpu.VMEM((layers, 2, width, width, modes), F32),
            pltpu.VMEM((small * rows, cols), F32),
            pltpu.VMEM((padded, width), F32),
            pltpu.VMEM((layers, width, width), F32),
            pltpu.VMEM((small, width), F32),
            pltpu.SemaphoreType.DMA((6 + layers,)),
        ),
        limit=16 << 20,
        name="prepare",
    ))
    message = shape(chip.tiles, tall, cols)
    to_previous, to_following = call(
        functools.partial(pack_kernel, chip), (message, message), core, *held, scalars=1, name="pack"
    )
    from_a = along_y(to_previous, -2, -1)
    from_b = along_y(to_following, 2, 1)
    from_a, from_b, prepared[3] = lax.optimization_barrier((from_a, from_b, prepared[3]))
    swap_a, swap_b = swap(from_a), swap(from_b)

    chunk = 4 * cols
    quarter_part = shape(chip.tiles - chip.edge_tiles, tall, cols)
    own, center_edge, center_quarter, keep_a, keep_b, give_a, give_b = call(
        functools.partial(network_kernel, chip, chunk),
        (shape(channels, rows, cols), shape(channels, 2 * tall, cols), quarter_part, message, message, message, message),
        core, field.reshape(channels, rows, cols), held[0], held[chip.place(1, 0)], held[chip.place(-1, 0)],
        to_previous, from_a, from_b, swap_a, swap_b, *prepared,
        scalars=1,
        scratch=(
            pltpu.VMEM((padded * rows, cols), F32),
            pltpu.VMEM((channels, 3 * tall, cols), F32),
            pltpu.VMEM((channels, 3 * tall, cols), F32),
            pltpu.VMEM((channels, 2 * tall, cols), F32),
            pltpu.VMEM((channels, rows + tall, cols), F32),
            pltpu.VMEM((len(chip.shared), channels, tall, cols), F32),
            pltpu.VMEM((2 * padded, cells), BF16),
            pltpu.VMEM((2 * width, cells), BF16),
            pltpu.VMEM((width, cells), F32),
            pltpu.VMEM((width, cells), F32),
            pltpu.VMEM((padded * rows, cols), F32),
            pltpu.VMEM((width, wave.shape[0]), F32),
        ),
        limit=16 << 20,
        name="network",
    )

    got_a, got_b = swap(give_a), swap(give_b)
    sum_b, sum_a = call(join_kernel, (message, message), keep_b, keep_a, got_b, got_a, name="join")
    sum_b = along_y(sum_b, 2, 1)
    sum_a = along_y(sum_a, -2, -1)
    parts = call(
        functools.partial(gather_kernel, chip),
        [shape(channels, tall, cols)] * len(chip.slots),
        core, center_edge, center_quarter, sum_b, sum_a, scalars=1,
        name="gather",
    )
    parts = [parts[0]] + [lax.ppermute(parts[slot], "gx", chip.pairs(slot, back=True)) for slot in others]
    out = call(
        final_kernel,
        shape(channels * rows, cols),
        own.reshape(channels * rows, cols), *parts,
        name="final",
    )
    return out.reshape(field.shape)


def solution(mesh):
    return jax.shard_map(
        body,
        mesh=mesh,
        in_specs=(P(None, None, "gx", "gy"), P(None, None, "gx", "gy"), P(), P(), P(), P()),
        out_specs=P(None, None, "gx", "gy"),
        check_vma=False,
    )
```

```python
import functools

import jax
import jax.numpy as jnp
import numpy as np
from jax import lax
from jax.experimental import pallas as pl
from jax.experimental.pallas import tpu as pltpu
from jax.sharding import PartitionSpec as P

MODES = 8
F32 = jnp.float32
BF16 = jnp.bfloat16
HIGHEST = lax.Precision.HIGHEST
SQRT_HALF = float(np.sqrt(0.5))
INV_SQRT_2PI = float(1.0 / np.sqrt(2.0 * np.pi))


class Chip:
    def __init__(self, count, channels):
        self.count = count
        self.ring = count == 4
        if self.ring:
            self.slots = [(0, 0), (1, -1), (2, 2), (-1, 1)]
        else:
            self.slots = [(k, k) for k in (0, 1, 2, -1, -2, 3, -3)]
        self.shared = [0, 1, 2, -1] if self.ring else [-2, -1, 0, 1, 2, 3]
        self.edge_tiles = channels + (channels + 1) // 2
        self.tiles = self.edge_tiles + channels * -(-len(self.shared) // 4)

    def place(self, offset, odd):
        offset = (offset + 1) % 4 - 1 if self.ring else offset
        return [slot[odd] for slot in self.slots].index(offset)

    def pairs(self, slot, back=False):
        count = self.count
        if self.ring:
            return [(s, s ^ slot) for s in range(count)]
        steps = self.slots[slot][0] if back else -self.slots[slot][0]
        return [(s, (s + steps) % count) for s in range(count)]

    def group(self, offset):
        return offset % 4 if self.ring else self.shared.index(offset)

    def within(self, offset):
        return self.ring or offset in self.shared

    def quarter_tile(self, channel, group):
        channels = (self.tiles - self.edge_tiles) // -(-len(self.shared) // 4)
        return self.edge_tiles + (group // 4) * channels + channel


def split(value):
    high = value.astype(BF16)
    return high, (value - high.astype(F32)).astype(BF16)


def dot(left, right):
    return jnp.dot(left, right, preferred_element_type=F32)


def dot_t(left, right):
    return lax.dot_general(left, right, (((1,), (1,)), ((), ())), precision=HIGHEST, preferred_element_type=F32)


def exact_dot(left, right):
    return jnp.dot(left, right, precision=HIGHEST, preferred_element_type=F32)


def stacked(value):
    high, low = split(value)
    top = jnp.concatenate([high, high], axis=1)
    bottom = jnp.concatenate([low, jnp.zeros_like(low)], axis=1)
    return jnp.concatenate([top, bottom], axis=0)


def halves(value):
    rows = value.shape[0] // 2
    return value[:rows] + value[rows:]


def wave_matrix(rows, cols):
    m = np.arange(MODES * MODES)
    wave_x, wave_y = m // MODES - MODES // 2, m % MODES
    b = 2.0 * np.pi * ((np.arange(cols)[:, None] * wave_y[None]) % cols) / cols
    scale = 1.0 / np.sqrt(rows * cols)
    cos, sin = np.cos(b) * scale, np.sin(b) * scale
    parts = []
    for k in range(MODES // 2 + 1):
        held = (np.abs(wave_x) == k)[None]
        parts.append(np.concatenate([cos * held, -sin * held], 1))
    for k in range(1, MODES // 2 + 1):
        held = (np.sign(wave_x) * (np.abs(wave_x) == k))[None]
        parts.append(np.concatenate([-sin * held, -cos * held], 1))
    return np.concatenate(parts, 0).astype(np.float32)


def wave_pair(matrix, axis):
    high = matrix.astype(BF16)
    low = (matrix - high.astype(np.float32)).astype(BF16)
    return jnp.asarray(np.concatenate([high, low], axis))


def weighted(terms):
    groups = {}
    for factor, value in terms:
        size = round(abs(factor), 12)
        if size == 0:
            continue
        groups.setdefault(size, []).append((factor > 0, value, abs(factor)))
    total = None
    for size, members in groups.items():
        members.sort(key=lambda member: not member[0])
        part = members[0][1] if members[0][0] else -members[0][1]
        for positive, value, _ in members[1:]:
            part = part + value if positive else part - value
        if size != 1:
            part = part * members[0][2]
        total = part if total is None else total + part
    return total


def wave_forward(values):
    n = len(values)
    top = MODES // 2
    angle = lambda k, i: 2.0 * np.pi * ((k * i) % n) / n
    plus = [values[0]] + [values[i] + values[n - i] for i in range(1, n // 2)] + [values[n // 2]]
    minus = [None] + [values[i] - values[n - i] for i in range(1, n // 2)]
    even = [plus[i] + plus[n // 2 - i] for i in range(n // 4)] + [plus[n // 4]]
    odd = [plus[i] - plus[n // 2 - i] for i in range(n // 4)]
    minus_odd = [None] + [minus[i] + minus[n // 2 - i] for i in range(1, n // 4)] + [minus[n // 4]]
    minus_even = [None] + [minus[i] - minus[n // 2 - i] for i in range(1, n // 4)]
    deep = {
        1: [even[i] + even[n // 4 - i] for i in range(n // 8)],
        -1: [even[i] - even[n // 4 - i] for i in range(n // 8)],
    }
    deep_minus = {
        1: [None] + [minus_even[i] - minus_even[n // 4 - i] for i in range(1, n // 8)],
        -1: [None] + [minus_even[i] + minus_even[n // 4 - i] for i in range(1, n // 8)],
    }
    out = []
    for k in range(top + 1):
        if k % 2:
            out.append(weighted([(np.cos(angle(k, i)), odd[i]) for i in range(n // 4)]))
        else:
            sign = 1 if k % 4 == 0 else -1
            terms = [(np.cos(angle(k, i)), deep[sign][i]) for i in range(n // 8)]
            out.append(weighted(terms + [(np.cos(angle(k, n // 8)), even[n // 8])]))
    for k in range(1, top + 1):
        if k % 2:
            out.append(weighted([(np.sin(angle(k, i)), minus_odd[i]) for i in range(1, n // 4 + 1)]))
        else:
            sign = 1 if k % 4 == 0 else -1
            terms = [(np.sin(angle(k, i)), deep_minus[sign][i]) for i in range(1, n // 8)]
            out.append(weighted(terms + [(np.sin(angle(k, n // 8)), minus_even[n // 8])]))
    return out


def added(a, b):
    return b if a is None else a if b is None else a + b


def taken(a, b):
    return a if b is None else -b if a is None else a - b


def wave_backward(parts, n):
    top = MODES // 2
    angle = lambda k, i: 2.0 * np.pi * ((k * i) % n) / n
    cosine = lambda i, ks: weighted([(np.cos(angle(k, i)), parts[k]) for k in ks])
    sine = lambda i, ks: weighted([(np.sin(angle(k, i)), parts[top + k]) for k in ks])
    fours = [k for k in range(top + 1) if k % 4 == 0]
    twos = [k for k in range(top + 1) if k % 4 == 2]
    odds = [k for k in range(top + 1) if k % 2]
    even = [None] * (n // 4 + 1)
    for i in range(n // 8):
        a, b = cosine(i, fours), cosine(i, twos)
        even[i], even[n // 4 - i] = added(a, b), taken(a, b)
    even[n // 8] = cosine(n // 8, sorted(fours + twos))
    plus = [None] * (n // 2 + 1)
    for i in range(n // 4):
        b = cosine(i, odds)
        plus[i], plus[n // 2 - i] = added(even[i], b), taken(even[i], b)
    plus[n // 4] = even[n // 4]
    minus_even = [None] * (n // 4)
    for i in range(1, n // 8):
        a, b = sine(i, [k for k in fours if k]), sine(i, twos)
        minus_even[i], minus_even[n // 4 - i] = added(b, a), taken(b, a)
    minus_even[n // 8] = sine(n // 8, sorted(k for k in fours + twos if k))
    minus = [None] * (n // 2)
    for i in range(1, n // 4):
        a = sine(i, odds)
        minus[i], minus[n // 2 - i] = added(a, minus_even[i]), taken(a, minus_even[i])
    minus[n // 4] = sine(n // 4, odds)
    out = [None] * n
    out[0], out[n // 2] = plus[0], plus[n // 2]
    for i in range(1, n // 2):
        out[i], out[n - i] = added(plus[i], minus[i]), taken(plus[i], minus[i])
    return out


def prepare_kernel(
    cotangent_hbm, lift_hbm, spectral_hbm, pointwise_hbm, project_hbm, *refs
):
    constants_hbm, refs = refs[:2], refs[2:]
    constants, refs = refs[:2], refs[2:]
    by_input, lift_ref, lift_t_ref, local_one, local_two, back_two, back_one, target_grad = refs[:8]
    spectral_ref, target_ref, lift_in, pointwise_ref, project_ref, sems = refs[8:]
    layers, _, width, _, modes = spectral_ref.shape
    small, cols = project_ref.shape[0], target_ref.shape[1]
    rows = target_ref.shape[0] // small
    channels, features = project_hbm.shape[0], lift_hbm.shape[0]
    pairs = [
        (cotangent_hbm, target_ref.at[: channels * rows]),
        (project_hbm, project_ref.at[:channels]),
        (lift_hbm, lift_in.at[:features]),
        (pointwise_hbm, pointwise_ref),
    ]
    pairs += [(spectral_hbm.at[layer], spectral_ref.at[layer]) for layer in range(layers)]
    pairs += list(zip(constants_hbm, constants))
    copies = [pltpu.make_async_copy(source, target, sems.at[k]) for k, (source, target) in enumerate(pairs)]
    for copy in copies:
        copy.start()
    target_ref[channels * rows :, :] = jnp.zeros(((small - channels) * rows, cols), F32)
    project_ref[channels:, :] = jnp.zeros((small - channels, width), F32)
    lift_in[features:, :] = jnp.zeros((lift_in.shape[0] - features, width), F32)
    for copy in copies[:4]:
        copy.wait()

    lift = lift_in[...]
    lift_t = jnp.transpose(lift)
    lift_ref[...] = lift
    lift_t_ref[...] = lift_t
    back_one[...] = tripled(exact_dot(lift, pointwise_ref[0]))
    local_one[...] = tripled(exact_dot(jnp.transpose(pointwise_ref[0]), lift_t))
    local_two[...] = tripled(jnp.transpose(pointwise_ref[1]))
    back_two[...] = tripled(pointwise_ref[1])
    out = tripled(jnp.transpose(project_ref[...]))
    group = 4
    for first in range(0, rows, group):
        pieces = []
        for i in range(first, first + group):
            value = target_ref[pl.ds(i, small, stride=rows), :]
            high = value.astype(BF16).astype(F32)
            pieces.append(jnp.concatenate([high, value - high, high], axis=0).astype(BF16))
        target_grad[:, first * cols : (first + group) * cols] = dot(out, jnp.concatenate(pieces, axis=1))

    for layer in range(layers):
        copies[4 + layer].wait()
        for w in range(width):
            both = [spectral_ref[layer, part, w] for part in range(2)]
            by_input[layer, w] = jnp.concatenate(both, axis=1)
    for copy in copies[4 + layers :]:
        copy.wait()


def index_of(shape, axis):
    return lax.broadcasted_iota(jnp.int32, shape, axis)


def quarter_matrix(cols, flipped=False):
    shape = (2 * cols, cols)
    fine, coarse = (index_of(shape, 1), index_of(shape, 0)) if flipped else (index_of(shape, 0), index_of(shape, 1))
    fine, coarse = fine % (cols // 2) // 2, coarse % (cols // 4)
    return jnp.where(fine == coarse, 0.25, 0.0).astype(BF16)


def spread_matrix(cols):
    shape = (2 * cols, 2 * cols)
    row, col = index_of(shape, 0) % cols, index_of(shape, 1)
    return jnp.where(row == col // 2, 0.25, 0.0).astype(BF16)


def pooling_matrix(cols):
    shape = (2 * cols, cols)
    return jnp.where(index_of(shape, 0) // 2 == index_of(shape, 1), 0.25, 0.0).astype(BF16)


def beside(value):
    return jnp.concatenate(split(value), axis=1)


def above(value):
    return jnp.concatenate(split(value), axis=0)


def turned(value, steps):
    lanes = value.shape[-1]
    if steps % lanes == 0:
        return value
    flat = value.reshape(-1, lanes)
    return pltpu.roll(flat, steps % lanes, 1).reshape(value.shape)


def by_group(values, lanes):
    lane = index_of((1,) * (values[0].ndim - 1) + (lanes,), values[0].ndim - 1)
    q = lanes // 4
    low = jnp.where(lane < q, values[0], values[1])
    high = jnp.where(lane < 3 * q, values[2], values[3])
    return jnp.where(lane < 2 * q, low, high)


def pool_kernel(field_ref, out_ref):
    count = field_ref.shape[0] // 4
    rows = [field_ref[pl.ds(k, count, stride=4), :] for k in range(4)]
    pairs = jnp.concatenate([rows[0] + rows[1], rows[2] + rows[3]], axis=1)
    out_ref[...] = halves(dot(above(pairs), pooling_matrix(field_ref.shape[1])))


def pack_kernel(chip, core_ref, *refs):
    blocks, (to_previous, to_following) = refs[: len(chip.slots)], refs[len(chip.slots) :]
    channels, tall, cols = blocks[0].shape
    q = cols // 4
    odd = core_ref[0] == 1
    sub = index_of((1, tall, cols), 1)
    shared = {}
    for e in chip.shared:
        even_at, odd_at = chip.place(e, 0), chip.place(e - 1, 1)
        shared[e] = jnp.where(odd, blocks[odd_at][...], blocks[even_at][...])
    stacked_rows = jnp.concatenate([shared[e].reshape(channels * tall, cols) for e in chip.shared], axis=0)
    coarse = dot(beside(stacked_rows), quarter_matrix(cols)).reshape(len(chip.shared), channels, tall, cols)
    for first in range(0, len(chip.shared), 4):
        groups = [min(first + k, len(chip.shared) - 1) for k in range(4)]
        tile = by_group([coarse[k] for k in groups], cols)
        at = chip.quarter_tile(0, first)
        to_previous[at : at + channels] = tile
        to_following[at : at + channels] = tile
    outer = jnp.where(sub < tall // 2, shared[2], shared[-1])

    def pair(one, two, shifts):
        return by_group([turned(v, k * q) for v, k in zip((one, one, two, two), shifts)], cols)

    for ref, shifts in ((to_previous, (0, -1, 2, 1)), (to_following, (-1, -2, 1, 0))):
        ref[:channels] = pair(shared[0], shared[1], shifts)
        for c in range(0, channels, 2):
            ref[channels + c // 2] = pair(outer[c], outer[min(c + 1, channels - 1)], shifts)


def mix(weights, layer, coefficients):
    width, lanes = coefficients.shape
    half = lanes // 2
    lane = lax.broadcasted_iota(jnp.int32, (width, lanes), 1)
    swapped = pltpu.roll(coefficients, half, 1)
    signed = jnp.where(lane < half, coefficients, -coefficients)
    total_real, total_imag = [None] * 2, [None] * 2
    for w in range(width):
        block = weights[layer, w]
        total_real[w % 2] = added(total_real[w % 2], block * signed[w : w + 1])
        total_imag[w % 2] = added(total_imag[w % 2], block * swapped[w : w + 1])
    total_real, total_imag = sum(total_real), sum(total_imag)
    total_real += pltpu.roll(total_real, half, 1)
    total_imag += pltpu.roll(total_imag, half, 1)
    return jnp.where(lane < half, total_real, total_imag)


def rows_summed(values):
    row = index_of(values[0].shape, 0)
    step = 1
    while len(values) > 1:
        held = (row & step) != 0
        values = [
            jnp.where(held, x, y) + pltpu.roll(jnp.where(held, y, x), step, 0) for y, x in zip(values[::2], values[1::2])
        ]
        step *= 2
    return values[0]


def exchanged(values):
    row = index_of(values[0].shape, 0)
    for step in (1, 2, 4):
        held = (row & step) != 0
        values = list(values)
        for k in range(8):
            if not k & step:
                a, b = values[k], values[k + step]
                values[k] = jnp.where(held, pltpu.roll(b, step, 0), a)
                values[k + step] = jnp.where(held, b, pltpu.roll(a, 8 - step, 0))
    return values


def unmix(weights, layer, grads):
    width, lanes = grads.shape
    half = lanes // 2
    lane = index_of((width, lanes), 1)
    turned_grads = pltpu.roll(grads, half, 1)
    turned_grads = jnp.where(lane < half, turned_grads, -turned_grads)

    def folded(block, value):
        product = block * value
        return sum(product[k : k + 8] for k in range(8, width, 8)) + product[:8]

    real, imag = [], []
    for first in range(0, width, 8):
        blocks = [weights[layer, w] for w in range(first, first + 8)]
        real.append(rows_summed([folded(block, grads) for block in blocks]))
        imag.append(rows_summed([folded(block, turned_grads) for block in blocks]))
    real, imag = jnp.concatenate(real, axis=0), jnp.concatenate(imag, axis=0)
    real += pltpu.roll(real, half, 1)
    imag += pltpu.roll(imag, half, 1)
    return jnp.where(lane < half, real, imag)


def contract(parts, wave):
    high, low = split(parts)
    both = dot(jnp.concatenate([high, low], axis=0), wave)
    rows, modes = both.shape[0] // 2, both.shape[1] // 2
    return both[:rows, :modes] + both[:rows, modes:] + both[rows:, :modes]


def tripled(value):
    high, low = split(value)
    return jnp.concatenate([high, high, low], axis=1)


def local_product(out_ref, left, pair_ref, steps):
    rows = pair_ref.shape[0] // 2
    for at in steps:
        right = jnp.concatenate([pair_ref[:, at], pair_ref[:rows, at]], axis=0)
        out_ref[:, at] = dot(left, right)


def store_pair(pair_ref, first, rows_total, at, value):
    high, low = split(value)
    count = value.shape[0]
    pair_ref[first : first + count, at] = high
    pair_ref[rows_total + first : rows_total + first + count, at] = low


def network_kernel(
    chip, chunk,
    core_ref, field_ref, here_ref, next_ref, last_ref, mine_ref, got_after, got_before, other_after, other_before,
    wave_ref, wave_t_ref, by_input, lift_ref, lift_t_ref, local_one, local_two, back_two, back_one, target_grad,
    own_ref, center_edge, center_quarter, keep_a, keep_b, give_a, give_b,
    x_ref, even_ref, odd_ref, mid_ref, far_ref, far_blocks, feature_pair, hidden_pair, slope_one, local_ref, grad_x_ref, parts_ref,
):
    channels, rows, cols = field_ref.shape
    tall = rows // 4
    q = cols // 4
    cells = rows * cols
    width = slope_one.shape[0]
    padded = x_ref.shape[0] // rows
    odd = core_ref[0] == 1
    shift = core_ref[0] * tall
    lane = index_of((1, 1, cols), 2)
    for c in range(channels):
        x_ref[c * rows : (c + 1) * rows, :] = field_ref[c]
    before, after = last_ref[...], next_ref[...]
    if chip.ring:
        before, after = jnp.where(odd, after, before), jnp.where(odd, before, after)
    mid_ref[:, : tall // 2, :] = before[:, tall // 2 :, :]
    mid_ref[:, tall // 2 : tall // 2 + tall, :] = here_ref[...]
    mid_ref[:, tall // 2 + tall :, :] = after[:, : tall // 2, :]
    edges = slice(0, chip.edge_tiles)
    previous = jnp.where(odd, got_before[edges], other_before[edges])
    following = jnp.where(odd, got_after[edges], other_after[edges])
    first = tall // 2
    for ref, shifts in ((even_ref, ((0, 3), (2, 1))), (odd_ref, ((-1, 2), (1, 0)))):
        one, two = (
            jnp.where(lane < 2 * q, turned(previous, a * q), turned(following, b * q)) for a, b in shifts
        )
        ref[:, first : first + tall, :] = one[:channels]
        ref[:, first + tall : first + 2 * tall, :] = two[:channels]
        for c in range(channels):
            outer = (two if c % 2 else one)[channels + c // 2]
            ref[c, :first, :] = outer[first:]
            ref[c, first + 2 * tall :, :] = outer[:first]
    middle = (lane >= q) & (lane < 3 * q)
    own = mid_ref[...]
    even_rows = jnp.where(middle, turned(own, q), even_ref[:, pl.ds(shift, 2 * tall), :])
    odd_rows = jnp.where(middle, turned(own, -q), odd_ref[:, pl.ds(shift, 2 * tall), :])
    for c in range(channels):
        at = (channels + c) * rows
        x_ref[pl.ds(at, 2 * tall, stride=2), :] = even_rows[c]
        x_ref[pl.ds(at + 1, 2 * tall, stride=2), :] = odd_rows[c]
    eighth = q // 2
    starts = {-2: -eighth, -1: eighth, 0: 3 * eighth, 1: 5 * eighth, 2: 7 * eighth}
    spans = {e: (e, first + (e + 1) * tall, slice(0, tall)) for e in (-1, 0, 1, 2)}
    spans[-2] = (-2, 0, slice(first, tall))
    spans[3] = (3, first + 4 * tall, slice(0, first))
    for group in range(len(chip.shared)):
        at = chip.quarter_tile(0, group)
        at = slice(at, at + channels)
        columns = {
            -2: jnp.where(odd, other_before[at], got_before[at]),
            -1: jnp.where(odd, got_before[at], other_before[at]),
            0: mine_ref[at],
            1: jnp.where(odd, got_after[at], other_after[at]),
            2: jnp.where(odd, other_after[at], got_after[at]),
        }
        value = turned(columns[2], starts[2] - group % 4 * q)
        for d in (1, 0, -1, -2):
            value = jnp.where(lane < starts[d + 1], turned(columns[d], starts[d] - group % 4 * q), value)
        for e, row, part in spans.values():
            if chip.within(e) and chip.group(e) == group:
                far_ref[:, row : row + part.stop - part.start, :] = value[:, part, :]
    far = far_ref[:, pl.ds(shift, rows), :]
    for c in range(channels):
        x_ref[(2 * channels + c) * rows : (2 * channels + c + 1) * rows, :] = far[c]
    for c in range(3 * channels, padded):
        x_ref[c * rows : (c + 1) * rows, :] = jnp.zeros((rows, cols), F32)

    for block in range(0, rows, 8):
        bands = [
            exchanged([x_ref[c * rows + block : c * rows + block + 8, :] for c in range(k, k + 8)])
            for k in range(0, padded, 8)
        ]
        for i in range(8):
            at = slice((block + i) * cols, (block + i + 1) * cols)
            value = jnp.concatenate([band[i] for band in bands], axis=0)
            local_ref[:padded, at] = value
            high, low = split(value)
            feature_pair[:padded, at] = high
            feature_pair[padded:, at] = low

    lift = lift_ref[...]
    lift_t = lift_t_ref[...]
    steps = [slice(k, k + chunk) for k in range(0, cells, chunk)]
    columns = [slice(i * cols, (i + 1) * cols) for i in range(rows)]
    part_count = parts_ref.shape[1] // cols
    part_columns = [slice(i * cols, (i + 1) * cols) for i in range(part_count)]

    def store_parts(band, values):
        for at, value in zip(part_columns, wave_forward(values)):
            parts_ref[band, at] = value

    def expanded(modes, band_rows):
        parts_ref[:band_rows, :] = halves(dot(stacked(modes), wave_t_ref[...]))

    def unfolded(band):
        return wave_backward([parts_ref[band, at] for at in part_columns], rows)

    bands = [slice(k, k + 8) for k in range(0, width, 8)]

    for k in range(0, padded, 8):
        store_parts(slice(k, k + 8), [local_ref[k : k + 8, at] for at in columns])
    local_product(local_ref, local_one[...], feature_pair, steps)
    modes = contract(parts_ref[:padded, :], wave_ref[...])
    expanded(mix(by_input, 0, exact_dot(lift_t, modes)), width)
    for band in bands:
        hidden = []
        for at, value in zip(columns, unfolded(band)):
            u = value + local_ref[band, at]
            cdf = 0.5 + 0.5 * lax.erf(u * SQRT_HALF)
            slope_one[band, at] = cdf + u * (INV_SQRT_2PI * jnp.exp(-0.5 * u * u))
            hidden.append(u * cdf)
            store_pair(hidden_pair, band.start, width, at, hidden[-1])
        store_parts(band, hidden)

    local_product(local_ref, local_two[...], hidden_pair, steps)
    modes = contract(parts_ref[...], wave_ref[...])
    expanded(mix(by_input, 1, modes), width)
    for band in bands:
        grads = []
        for at, value in zip(columns, unfolded(band)):
            u = value + local_ref[band, at]
            cdf = 0.5 + 0.5 * lax.erf(u * SQRT_HALF)
            slope = cdf + u * (INV_SQRT_2PI * jnp.exp(-0.5 * u * u))
            grads.append(slope * target_grad[band, at])
            store_pair(hidden_pair, band.start, width, at, grads[-1])
        store_parts(band, grads)
    local_product(local_ref, back_two[...], hidden_pair, steps)
    modes = contract(parts_ref[...], wave_ref[...])
    expanded(unmix(by_input, 1, modes), width)
    for band in bands:
        grads = []
        for at, value in zip(columns, unfolded(band)):
            grads.append((value + local_ref[band, at]) * slope_one[band, at])
            store_pair(hidden_pair, band.start, width, at, grads[-1])
        store_parts(band, grads)

    local_product(local_ref.at[:padded], back_one[...], hidden_pair, steps)
    modes = contract(parts_ref[...], wave_ref[...])
    expanded(exact_dot(lift, unmix(by_input, 0, modes)), padded)
    for k in range(0, padded, 8):
        band = slice(k, k + 8)
        values = [value + local_ref[band, at] for at, value in zip(columns, unfolded(band))]
        for block in range(0, rows, 8):
            for c, value in enumerate(exchanged(values[block : block + 8])):
                at = (k + c) * rows + block
                grad_x_ref[at : at + 8, :] = value

    for c in range(channels):
        own_ref[c] = grad_x_ref[c * rows : (c + 1) * rows, :]

    even_grads, odd_grads = [], []
    for c in range(channels):
        at = (channels + c) * rows
        even_grads.append(grad_x_ref[pl.ds(at, 2 * tall, stride=2), :][None])
        odd_grads.append(grad_x_ref[pl.ds(at + 1, 2 * tall, stride=2), :][None])
    even_grads = jnp.concatenate(even_grads, axis=0)
    odd_grads = jnp.concatenate(odd_grads, axis=0)
    center_edge[...] = jnp.where(lane < 2 * q, turned(even_grads, -q), turned(odd_grads, q))
    for ref, value in ((even_ref, even_grads), (odd_ref, odd_grads)):
        ref[...] = jnp.zeros_like(ref)
        ref[:, pl.ds(shift, 2 * tall), :] = value

    def edge_tiles(shifts):
        def pair(one, two):
            return by_group([turned(v, k * q) for v, k in zip((*one, *two), shifts)], cols)

        refs = (even_ref, odd_ref)
        inner = pair(*([ref[:, first + k * tall : first + (k + 1) * tall, :] for ref in refs] for k in (0, 1)))
        outer = [jnp.concatenate([ref[:, first + 2 * tall :, :], ref[:, :first, :]], axis=1) for ref in refs]
        tiles = [inner]
        for c in range(0, channels, 2):
            other = min(c + 1, channels - 1)
            tiles.append(pair([v[c] for v in outer], [v[other] for v in outer])[None])
        return jnp.concatenate(tiles, axis=0)

    near = {-1: edge_tiles((0, 1, 2, 3)), 1: edge_tiles((1, 2, 3, 0))}
    for one, keep, give in ((-1, keep_a, give_a), (1, keep_b, give_b)):
        zero = jnp.zeros_like(near[one])
        keep[: chip.edge_tiles] = jnp.where(odd, near[one], zero)
        give[: chip.edge_tiles] = jnp.where(odd, zero, near[one])
    far_ref[...] = jnp.zeros_like(far_ref)
    for c in range(channels):
        at = (2 * channels + c) * rows
        far_ref[c, pl.ds(shift, rows), :] = grad_x_ref[at : at + rows, :]
    far_blocks[...] = jnp.zeros_like(far_blocks)
    for e in (-1, 0, 1, 2, -2, 3):
        if chip.within(e):
            _, row, part = spans[e]
            far_blocks[chip.group(e), :, part, :] += far_ref[:, row : row + part.stop - part.start, :]
    for start in range(0, len(chip.shared), 4):
        groups = [min(start + k, len(chip.shared) - 1) for k in range(4)]
        at = chip.quarter_tile(0, start)
        at = slice(at, at + channels)
        tiles = {}
        for d in range(-2, 3):
            value = by_group([turned(far_blocks[g], k * q - starts[d]) for k, g in enumerate(groups)], cols)
            if abs(d) == 2:
                value = jnp.where((lane % q >= eighth) == (d < 0), value, 0.0)
            tiles[d] = value
        center_quarter[at.start - chip.edge_tiles : at.stop - chip.edge_tiles] = tiles[0]
        for one, two, keep, give in ((-1, -2, keep_a, give_a), (1, 2, keep_b, give_b)):
            keep[at] = jnp.where(odd, tiles[one], tiles[two])
            give[at] = jnp.where(odd, tiles[two], tiles[one])


def join_kernel(keep_b, keep_a, got_b, got_a, out_b, out_a):
    out_b[...] = keep_b[...] + got_b[...]
    out_a[...] = keep_a[...] + got_a[...]


def gather_kernel(chip, core_ref, center_edge, center_quarter, from_before, from_after, *outs):
    channels, _, cols = center_edge.shape
    tall = from_after.shape[1]
    q, first = cols // 4, tall // 2
    odd = core_ref[0] == 1
    sub = index_of((1, tall, cols), 1)
    lane = index_of((1, 1, cols), 2)
    edges = chip.edge_tiles
    coarse = center_quarter[...] + from_after[edges:] + from_before[edges:]
    rows = []
    for group in range(len(chip.shared)):
        at = chip.quarter_tile(0, group) - edges
        value = jnp.where(lane // q == group % 4, coarse[at : at + channels], 0.0)
        rows.append(value.reshape(channels * tall, cols))
    shared = dot(beside(jnp.concatenate(rows, axis=0)), quarter_matrix(cols, flipped=True))
    shared = shared.reshape(len(chip.shared), channels, tall, cols)
    tail, head = from_after[:edges], from_before[:edges]

    def unpaired(moves):
        return by_group([turned(v, k * q) for v, k in zip((head, tail, head, tail), moves)], cols)

    one, two = unpaired((0, 1, 1, 2)), unpaired((-2, -1, -1, 0))
    outer = [(two if c % 2 else one)[channels + c // 2][None] for c in range(channels)]
    outer = jnp.concatenate(outer, axis=0)
    edge = {
        0: one[:channels],
        1: two[:channels],
        2: jnp.where(sub < first, outer, 0.0),
        -1: jnp.where(sub < first, 0.0, outer),
    }
    shared = {e: shared[chip.group(e)] + edge[e] if e in edge else shared[chip.group(e)] for e in chip.shared}
    if chip.ring:
        shared[3] = shared[-1]
    zero = jnp.zeros((channels, tall, cols), F32)
    blank = zero[:, :first]
    own = {
        -1: jnp.concatenate([blank, center_edge[:, :first, :]], axis=1),
        0: center_edge[:, first : first + tall, :],
        1: jnp.concatenate([center_edge[:, first + tall :, :], blank], axis=1),
    }
    def block_of(offset, is_odd):
        value = shared.get(offset + is_odd, zero)
        return value + own[offset] if offset in own else value

    for out, (even_offset, odd_offset) in zip(outs, chip.slots):
        out[...] = jnp.where(odd, block_of(odd_offset, 1), block_of(even_offset, 0))


def final_kernel(own_ref, *refs):
    out_ref = refs[-1]
    total = refs[0][...]
    for ref in refs[1:-1]:
        total = total + ref[...]
    cols = total.shape[2]
    spread = dot(beside(total.reshape(-1, cols)), spread_matrix(cols))
    count = spread.shape[0]
    for k in range(4):
        part = spread[:, :cols] if k < 2 else spread[:, cols:]
        at = pl.ds(k, count, stride=4)
        out_ref[at, :] = own_ref[at, :] + part


def in_memory(count, space=pltpu.VMEM):
    return [pl.BlockSpec(memory_space=space)] * count


SCALAR = pl.BlockSpec(memory_space=pltpu.SMEM)


def call(kernel, shapes, *operands, scalars=0, scratch=(), name=None, limit=8 << 20, in_place=False, far=(), out_far=()):
    single = not isinstance(shapes, (list, tuple))
    if in_place:
        operands = [pltpu.with_memory_space_constraint(operand, pltpu.HBM) for operand in operands]
    outs = [shapes] if single else list(shapes)
    if in_place:
        far = range(scalars, len(operands))
    places = [SCALAR] * scalars + in_memory(len(operands) - scalars)
    for k in far:
        places[k] = pl.BlockSpec(memory_space=pltpu.HBM)
    out_places = in_memory(len(outs))
    for k in out_far:
        out_places[k] = pl.BlockSpec(memory_space=pltpu.HBM)
        outs[k] = pltpu.HBM(outs[k].shape, outs[k].dtype)
    result = pl.pallas_call(
        kernel,
        out_shape=outs,
        in_specs=places,
        out_specs=out_places,
        scratch_shapes=list(scratch),
        compiler_params=pltpu.CompilerParams(vmem_limit_bytes=limit),
        name=name,
    )(*operands)
    return result[0] if single else result


def body(field, cotangent, lift, spectral, pointwise, project):
    channels, levels, rows, cols = field.shape
    width = lift.shape[1]
    layers = spectral.shape[0]
    modes = spectral.shape[2]
    features = lift.shape[0]
    cells = rows * cols
    tall = rows // 4
    gx, gy = lax.axis_size("gx"), lax.axis_size("gy")
    chip = Chip(gx, channels)
    core = (lax.axis_index("gx") % 2).astype(jnp.int32).reshape(1)

    def shape(*dims, dtype=F32):
        return jax.ShapeDtypeStruct(dims, dtype)

    def along_y(value, even_steps, odd_steps):
        pairs = []
        for a in range(gx):
            for b in range(gy):
                steps = odd_steps if a % 2 else even_steps
                pairs.append((a * gy + b, a * gy + (b + steps) % gy))
        return lax.ppermute(value, ("gx", "gy"), pairs)

    def swap(value):
        return lax.ppermute(value, "gx", [(s, s ^ 1) for s in range(gx)])

    flat_field = field.reshape(channels * rows, cols)
    packed = call(pool_kernel, shape(channels * tall, cols), flat_field, name="pool")
    packed = packed.reshape(channels, tall, cols)

    others = range(1, len(chip.slots))
    held = [packed] + [lax.ppermute(packed, "gx", chip.pairs(slot)) for slot in others]
    wave = wave_matrix(rows, cols)
    padded = -(-features // 16) * 16
    small = -(-channels // 8) * 8
    constants = [wave_pair(wave, 1), wave_pair(wave.T, 0)]
    packed_weights = shape(layers, width, width, 2 * modes)
    prepared = list(call(
        prepare_kernel,
        [shape(*c.shape, dtype=BF16) for c in constants]
        + [
            packed_weights, shape(padded, width), shape(width, padded), shape(width, 3 * padded, dtype=BF16),
            shape(width, 3 * width, dtype=BF16), shape(width, 3 * width, dtype=BF16), shape(padded, 3 * width, dtype=BF16),
            shape(width, cells),
        ],
        cotangent.reshape(channels * rows, cols), lift, jnp.transpose(spectral, (0, 1, 3, 4, 2)), pointwise, project.T,
        *constants,
        in_place=True,
        scratch=(
            pltpu.VMEM((layers, 2, width, width, modes), F32),
            pltpu.VMEM((small * rows, cols), F32),
            pltpu.VMEM((padded, width), F32),
            pltpu.VMEM((layers, width, width), F32),
            pltpu.VMEM((small, width), F32),
            pltpu.SemaphoreType.DMA((6 + layers,)),
        ),
        limit=16 << 20,
        name="prepare",
    ))
    message = shape(chip.tiles, tall, cols)
    to_previous, to_following = call(
        functools.partial(pack_kernel, chip), (message, message), core, *held, scalars=1, name="pack"
    )
    from_a = along_y(to_previous, -2, -1)
    from_b = along_y(to_following, 2, 1)
    from_a, from_b, prepared[3] = lax.optimization_barrier((from_a, from_b, prepared[3]))
    swap_a, swap_b = swap(from_a), swap(from_b)

    chunk = 4 * cols
    quarter_part = shape(chip.tiles - chip.edge_tiles, tall, cols)
    own, center_edge, center_quarter, keep_a, keep_b, give_a, give_b = call(
        functools.partial(network_kernel, chip, chunk),
        (shape(channels, rows, cols), shape(channels, 2 * tall, cols), quarter_part, message, message, message, message),
        core, field.reshape(channels, rows, cols), held[0], held[chip.place(1, 0)], held[chip.place(-1, 0)],
        to_previous, from_a, from_b, swap_a, swap_b, *prepared,
        scalars=1,
        scratch=(
            pltpu.VMEM((padded * rows, cols), F32),
            pltpu.VMEM((channels, 3 * tall, cols), F32),
            pltpu.VMEM((channels, 3 * tall, cols), F32),
            pltpu.VMEM((channels, 2 * tall, cols), F32),
            pltpu.VMEM((channels, rows + tall, cols), F32),
            pltpu.VMEM((len(chip.shared), channels, tall, cols), F32),
            pltpu.VMEM((2 * padded, cells), BF16),
            pltpu.VMEM((2 * width, cells), BF16),
            pltpu.VMEM((width, cells), F32),
            pltpu.VMEM((width, cells), F32),
            pltpu.VMEM((padded * rows, cols), F32),
            pltpu.VMEM((width, wave.shape[0]), F32),
        ),
        limit=16 << 20,
        name="network",
    )

    got_a, got_b = swap(give_a), swap(give_b)
    sum_b, sum_a = call(join_kernel, (message, message), keep_b, keep_a, got_b, got_a, name="join")
    sum_b = along_y(sum_b, 2, 1)
    sum_a = along_y(sum_a, -2, -1)
    parts = call(
        functools.partial(gather_kernel, chip),
        [shape(channels, tall, cols)] * len(chip.slots),
        core, center_edge, center_quarter, sum_b, sum_a, scalars=1,
        name="gather",
    )
    parts = [parts[0]] + [lax.ppermute(parts[slot], "gx", chip.pairs(slot, back=True)) for slot in others]
    out = call(
        final_kernel,
        shape(channels * rows, cols),
        own.reshape(channels * rows, cols), *parts,
        name="final",
    )
    return out.reshape(field.shape)


def solution(mesh):
    return jax.shard_map(
        body,
        mesh=mesh,
        in_specs=(P(None, None, "gx", "gy"), P(None, None, "gx", "gy"), P(), P(), P(), P()),
        out_specs=P(None, None, "gx", "gy"),
        check_vma=False,
    )
```

```python
import functools

import jax
import jax.numpy as jnp
import numpy as np
from jax import lax
from jax.experimental import pallas as pl
from jax.experimental.pallas import tpu as pltpu
from jax.sharding import PartitionSpec as P

MODES = 8
F32 = jnp.float32
BF16 = jnp.bfloat16
HIGHEST = lax.Precision.HIGHEST
SQRT_HALF = float(np.sqrt(0.5))
INV_SQRT_2PI = float(1.0 / np.sqrt(2.0 * np.pi))


class Chip:
    def __init__(self, count, channels):
        self.count = count
        self.ring = count == 4
        if self.ring:
            self.slots = [(0, 0), (1, -1), (2, 2), (-1, 1)]
        else:
            self.slots = [(k, k) for k in (0, 1, 2, -1, -2, 3, -3)]
        self.shared = [0, 1, 2, -1] if self.ring else [-2, -1, 0, 1, 2, 3]
        self.edge_tiles = channels + (channels + 1) // 2
        self.tiles = self.edge_tiles + channels * -(-len(self.shared) // 4)

    def place(self, offset, odd):
        offset = (offset + 1) % 4 - 1 if self.ring else offset
        return [slot[odd] for slot in self.slots].index(offset)

    def pairs(self, slot, back=False):
        count = self.count
        if self.ring:
            return [(s, s ^ slot) for s in range(count)]
        steps = self.slots[slot][0] if back else -self.slots[slot][0]
        return [(s, (s + steps) % count) for s in range(count)]

    def group(self, offset):
        return offset % 4 if self.ring else self.shared.index(offset)

    def within(self, offset):
        return self.ring or offset in self.shared

    def quarter_tile(self, channel, group):
        channels = (self.tiles - self.edge_tiles) // -(-len(self.shared) // 4)
        return self.edge_tiles + (group // 4) * channels + channel


def split(value):
    high = value.astype(BF16)
    return high, (value - high.astype(F32)).astype(BF16)


def dot(left, right):
    return jnp.dot(left, right, preferred_element_type=F32)


def dot_t(left, right):
    return lax.dot_general(left, right, (((1,), (1,)), ((), ())), precision=HIGHEST, preferred_element_type=F32)


def exact_dot(left, right):
    return jnp.dot(left, right, precision=HIGHEST, preferred_element_type=F32)


def stacked(value):
    high, low = split(value)
    top = jnp.concatenate([high, high], axis=1)
    bottom = jnp.concatenate([low, jnp.zeros_like(low)], axis=1)
    return jnp.concatenate([top, bottom], axis=0)


def halves(value):
    rows = value.shape[0] // 2
    return value[:rows] + value[rows:]


def wave_matrix(rows, cols):
    m = np.arange(MODES * MODES)
    wave_x, wave_y = m // MODES - MODES // 2, m % MODES
    b = 2.0 * np.pi * ((np.arange(cols)[:, None] * wave_y[None]) % cols) / cols
    scale = 1.0 / np.sqrt(rows * cols)
    cos, sin = np.cos(b) * scale, np.sin(b) * scale
    parts = []
    for k in range(MODES // 2 + 1):
        held = (np.abs(wave_x) == k)[None]
        parts.append(np.concatenate([cos * held, -sin * held], 1))
    for k in range(1, MODES // 2 + 1):
        held = (np.sign(wave_x) * (np.abs(wave_x) == k))[None]
        parts.append(np.concatenate([-sin * held, -cos * held], 1))
    return np.concatenate(parts, 0).astype(np.float32)


def wave_pair(matrix, axis):
    high = matrix.astype(BF16)
    low = (matrix - high.astype(np.float32)).astype(BF16)
    return jnp.asarray(np.concatenate([high, low], axis))


def weighted(terms):
    groups = {}
    for factor, value in terms:
        size = round(abs(factor), 12)
        if size == 0:
            continue
        groups.setdefault(size, []).append((factor > 0, value, abs(factor)))
    total = None
    for size, members in groups.items():
        members.sort(key=lambda member: not member[0])
        part = members[0][1] if members[0][0] else -members[0][1]
        for positive, value, _ in members[1:]:
            part = part + value if positive else part - value
        if size != 1:
            part = part * members[0][2]
        total = part if total is None else total + part
    return total


def wave_forward(values):
    n = len(values)
    top = MODES // 2
    angle = lambda k, i: 2.0 * np.pi * ((k * i) % n) / n
    plus = [values[0]] + [values[i] + values[n - i] for i in range(1, n // 2)] + [values[n // 2]]
    minus = [None] + [values[i] - values[n - i] for i in range(1, n // 2)]
    even = [plus[i] + plus[n // 2 - i] for i in range(n // 4)] + [plus[n // 4]]
    odd = [plus[i] - plus[n // 2 - i] for i in range(n // 4)]
    minus_odd = [None] + [minus[i] + minus[n // 2 - i] for i in range(1, n // 4)] + [minus[n // 4]]
    minus_even = [None] + [minus[i] - minus[n // 2 - i] for i in range(1, n // 4)]
    deep = {
        1: [even[i] + even[n // 4 - i] for i in range(n // 8)],
        -1: [even[i] - even[n // 4 - i] for i in range(n // 8)],
    }
    deep_minus = {
        1: [None] + [minus_even[i] - minus_even[n // 4 - i] for i in range(1, n // 8)],
        -1: [None] + [minus_even[i] + minus_even[n // 4 - i] for i in range(1, n // 8)],
    }
    out = []
    for k in range(top + 1):
        if k % 2:
            out.append(weighted([(np.cos(angle(k, i)), odd[i]) for i in range(n // 4)]))
        else:
            sign = 1 if k % 4 == 0 else -1
            terms = [(np.cos(angle(k, i)), deep[sign][i]) for i in range(n // 8)]
            out.append(weighted(terms + [(np.cos(angle(k, n // 8)), even[n // 8])]))
    for k in range(1, top + 1):
        if k % 2:
            out.append(weighted([(np.sin(angle(k, i)), minus_odd[i]) for i in range(1, n // 4 + 1)]))
        else:
            sign = 1 if k % 4 == 0 else -1
            terms = [(np.sin(angle(k, i)), deep_minus[sign][i]) for i in range(1, n // 8)]
            out.append(weighted(terms + [(np.sin(angle(k, n // 8)), minus_even[n // 8])]))
    return out


def added(a, b):
    return b if a is None else a if b is None else a + b


def taken(a, b):
    return a if b is None else -b if a is None else a - b


def wave_backward(parts, n):
    top = MODES // 2
    angle = lambda k, i: 2.0 * np.pi * ((k * i) % n) / n
    cosine = lambda i, ks: weighted([(np.cos(angle(k, i)), parts[k]) for k in ks])
    sine = lambda i, ks: weighted([(np.sin(angle(k, i)), parts[top + k]) for k in ks])
    fours = [k for k in range(top + 1) if k % 4 == 0]
    twos = [k for k in range(top + 1) if k % 4 == 2]
    odds = [k for k in range(top + 1) if k % 2]
    even = [None] * (n // 4 + 1)
    for i in range(n // 8):
        a, b = cosine(i, fours), cosine(i, twos)
        even[i], even[n // 4 - i] = added(a, b), taken(a, b)
    even[n // 8] = cosine(n // 8, sorted(fours + twos))
    plus = [None] * (n // 2 + 1)
    for i in range(n // 4):
        b = cosine(i, odds)
        plus[i], plus[n // 2 - i] = added(even[i], b), taken(even[i], b)
    plus[n // 4] = even[n // 4]
    minus_even = [None] * (n // 4)
    for i in range(1, n // 8):
        a, b = sine(i, [k for k in fours if k]), sine(i, twos)
        minus_even[i], minus_even[n // 4 - i] = added(b, a), taken(b, a)
    minus_even[n // 8] = sine(n // 8, sorted(k for k in fours + twos if k))
    minus = [None] * (n // 2)
    for i in range(1, n // 4):
        a = sine(i, odds)
        minus[i], minus[n // 2 - i] = added(a, minus_even[i]), taken(a, minus_even[i])
    minus[n // 4] = sine(n // 4, odds)
    out = [None] * n
    out[0], out[n // 2] = plus[0], plus[n // 2]
    for i in range(1, n // 2):
        out[i], out[n - i] = added(plus[i], minus[i]), taken(plus[i], minus[i])
    return out


def prepare_kernel(
    cotangent_hbm, lift_hbm, spectral_hbm, pointwise_hbm, project_hbm, *refs
):
    constants_hbm, refs = refs[:2], refs[2:]
    constants, refs = refs[:2], refs[2:]
    by_input, lift_ref, lift_t_ref, local_one, local_two, back_two, back_one, target_grad = refs[:8]
    spectral_ref, target_ref, lift_in, pointwise_ref, project_ref, sems = refs[8:]
    layers, _, width, _, modes = spectral_ref.shape
    small, cols = project_ref.shape[0], target_ref.shape[1]
    rows = target_ref.shape[0] // small
    channels, features = project_hbm.shape[0], lift_hbm.shape[0]
    pairs = [
        (cotangent_hbm, target_ref.at[: channels * rows]),
        (project_hbm, project_ref.at[:channels]),
        (lift_hbm, lift_in.at[:features]),
        (pointwise_hbm, pointwise_ref),
    ]
    pairs += [(spectral_hbm.at[layer], spectral_ref.at[layer]) for layer in range(layers)]
    pairs += list(zip(constants_hbm, constants))
    copies = [pltpu.make_async_copy(source, target, sems.at[k]) for k, (source, target) in enumerate(pairs)]
    for copy in copies:
        copy.start()
    target_ref[channels * rows :, :] = jnp.zeros(((small - channels) * rows, cols), F32)
    project_ref[channels:, :] = jnp.zeros((small - channels, width), F32)
    lift_in[features:, :] = jnp.zeros((lift_in.shape[0] - features, width), F32)
    for copy in copies[:4]:
        copy.wait()

    lift = lift_in[...]
    lift_t = jnp.transpose(lift)
    lift_ref[...] = lift
    lift_t_ref[...] = lift_t
    back_one[...] = tripled(exact_dot(lift, pointwise_ref[0]))
    local_one[...] = tripled(exact_dot(jnp.transpose(pointwise_ref[0]), lift_t))
    local_two[...] = tripled(jnp.transpose(pointwise_ref[1]))
    back_two[...] = tripled(pointwise_ref[1])
    out = tripled(jnp.transpose(project_ref[...]))
    group = 4
    for first in range(0, rows, group):
        pieces = []
        for i in range(first, first + group):
            value = target_ref[pl.ds(i, small, stride=rows), :]
            high = value.astype(BF16).astype(F32)
            pieces.append(jnp.concatenate([high, value - high, high], axis=0).astype(BF16))
        target_grad[:, first * cols : (first + group) * cols] = dot(out, jnp.concatenate(pieces, axis=1))

    for layer in range(layers):
        copies[4 + layer].wait()
        for w in range(width):
            both = [spectral_ref[layer, part, w] for part in range(2)]
            by_input[layer, w] = jnp.concatenate(both, axis=1)
    for copy in copies[4 + layers :]:
        copy.wait()


def index_of(shape, axis):
    return lax.broadcasted_iota(jnp.int32, shape, axis)


def quarter_matrix(cols, flipped=False):
    shape = (2 * cols, cols)
    fine, coarse = (index_of(shape, 1), index_of(shape, 0)) if flipped else (index_of(shape, 0), index_of(shape, 1))
    fine, coarse = fine % (cols // 2) // 2, coarse % (cols // 4)
    return jnp.where(fine == coarse, 0.25, 0.0).astype(BF16)


def spread_matrix(cols):
    shape = (2 * cols, 2 * cols)
    row, col = index_of(shape, 0) % cols, index_of(shape, 1)
    return jnp.where(row == col // 2, 0.25, 0.0).astype(BF16)


def pooling_matrix(cols):
    shape = (2 * cols, cols)
    return jnp.where(index_of(shape, 0) // 2 == index_of(shape, 1), 0.25, 0.0).astype(BF16)


def beside(value):
    return jnp.concatenate(split(value), axis=1)


def above(value):
    return jnp.concatenate(split(value), axis=0)


def turned(value, steps):
    lanes = value.shape[-1]
    if steps % lanes == 0:
        return value
    flat = value.reshape(-1, lanes)
    return pltpu.roll(flat, steps % lanes, 1).reshape(value.shape)


def by_group(values, lanes):
    lane = index_of((1,) * (values[0].ndim - 1) + (lanes,), values[0].ndim - 1)
    q = lanes // 4
    low = jnp.where(lane < q, values[0], values[1])
    high = jnp.where(lane < 3 * q, values[2], values[3])
    return jnp.where(lane < 2 * q, low, high)


def pool_kernel(field_ref, out_ref):
    count = field_ref.shape[0] // 4
    rows = [field_ref[pl.ds(k, count, stride=4), :] for k in range(4)]
    pairs = jnp.concatenate([rows[0] + rows[1], rows[2] + rows[3]], axis=1)
    out_ref[...] = halves(dot(above(pairs), pooling_matrix(field_ref.shape[1])))


def pack_kernel(chip, core_ref, *refs):
    blocks, (to_previous, to_following) = refs[: len(chip.slots)], refs[len(chip.slots) :]
    channels, tall, cols = blocks[0].shape
    q = cols // 4
    odd = core_ref[0] == 1
    sub = index_of((1, tall, cols), 1)
    shared = {}
    for e in chip.shared:
        even_at, odd_at = chip.place(e, 0), chip.place(e - 1, 1)
        shared[e] = jnp.where(odd, blocks[odd_at][...], blocks[even_at][...])
    stacked_rows = jnp.concatenate([shared[e].reshape(channels * tall, cols) for e in chip.shared], axis=0)
    coarse = dot(beside(stacked_rows), quarter_matrix(cols)).reshape(len(chip.shared), channels, tall, cols)
    for first in range(0, len(chip.shared), 4):
        groups = [min(first + k, len(chip.shared) - 1) for k in range(4)]
        tile = by_group([coarse[k] for k in groups], cols)
        at = chip.quarter_tile(0, first)
        to_previous[at : at + channels] = tile
        to_following[at : at + channels] = tile
    outer = jnp.where(sub < tall // 2, shared[2], shared[-1])

    def pair(one, two, shifts):
        return by_group([turned(v, k * q) for v, k in zip((one, one, two, two), shifts)], cols)

    for ref, shifts in ((to_previous, (0, -1, 2, 1)), (to_following, (-1, -2, 1, 0))):
        ref[:channels] = pair(shared[0], shared[1], shifts)
        for c in range(0, channels, 2):
            ref[channels + c // 2] = pair(outer[c], outer[min(c + 1, channels - 1)], shifts)


def mix(weights, layer, coefficients):
    width, lanes = coefficients.shape
    half = lanes // 2
    lane = lax.broadcasted_iota(jnp.int32, (width, lanes), 1)
    swapped = pltpu.roll(coefficients, half, 1)
    signed = jnp.where(lane < half, coefficients, -coefficients)
    total_real, total_imag = [None] * 2, [None] * 2
    for w in range(width):
        block = weights[layer, w]
        total_real[w % 2] = added(total_real[w % 2], block * signed[w : w + 1])
        total_imag[w % 2] = added(total_imag[w % 2], block * swapped[w : w + 1])
    total_real, total_imag = sum(total_real), sum(total_imag)
    total_real += pltpu.roll(total_real, half, 1)
    total_imag += pltpu.roll(total_imag, half, 1)
    return jnp.where(lane < half, total_real, total_imag)


def rows_summed(values):
    row = index_of(values[0].shape, 0)
    step = 1
    while len(values) > 1:
        held = (row & step) != 0
        values = [
            jnp.where(held, x, y) + pltpu.roll(jnp.where(held, y, x), step, 0) for y, x in zip(values[::2], values[1::2])
        ]
        step *= 2
    return values[0]


def exchanged(values):
    row = index_of(values[0].shape, 0)
    for step in (1, 2, 4):
        held = (row & step) != 0
        values = list(values)
        for k in range(8):
            if not k & step:
                a, b = values[k], values[k + step]
                values[k] = jnp.where(held, pltpu.roll(b, step, 0), a)
                values[k + step] = jnp.where(held, b, pltpu.roll(a, 8 - step, 0))
    return values


def unmix(weights, layer, grads):
    width, lanes = grads.shape
    half = lanes // 2
    lane = index_of((width, lanes), 1)
    turned_grads = pltpu.roll(grads, half, 1)
    turned_grads = jnp.where(lane < half, turned_grads, -turned_grads)

    def folded(block, value):
        product = block * value
        return sum(product[k : k + 8] for k in range(8, width, 8)) + product[:8]

    real, imag = [], []
    for first in range(0, width, 8):
        blocks = [weights[layer, w] for w in range(first, first + 8)]
        real.append(rows_summed([folded(block, grads) for block in blocks]))
        imag.append(rows_summed([folded(block, turned_grads) for block in blocks]))
    real, imag = jnp.concatenate(real, axis=0), jnp.concatenate(imag, axis=0)
    real += pltpu.roll(real, half, 1)
    imag += pltpu.roll(imag, half, 1)
    return jnp.where(lane < half, real, imag)


def contract(parts, wave):
    high, low = split(parts)
    both = dot(jnp.concatenate([high, low], axis=0), wave)
    rows, modes = both.shape[0] // 2, both.shape[1] // 2
    return both[:rows, :modes] + both[:rows, modes:] + both[rows:, :modes]


def tripled(value):
    high, low = split(value)
    return jnp.concatenate([high, high, low], axis=1)


def local_product(out_ref, left, pair_ref, steps):
    rows = pair_ref.shape[0] // 2
    for at in steps:
        right = jnp.concatenate([pair_ref[:, at], pair_ref[:rows, at]], axis=0)
        out_ref[:, at] = dot(left, right)


def store_pair(pair_ref, first, rows_total, at, value):
    high, low = split(value)
    count = value.shape[0]
    pair_ref[first : first + count, at] = high
    pair_ref[rows_total + first : rows_total + first + count, at] = low


def network_kernel(
    chip, chunk,
    core_ref, field_ref, here_ref, next_ref, last_ref, mine_ref, got_after, got_before, other_after, other_before,
    wave_ref, wave_t_ref, by_input, lift_ref, lift_t_ref, local_one, local_two, back_two, back_one, target_grad,
    own_ref, center_edge, center_quarter, keep_a, keep_b, give_a, give_b,
    x_ref, even_ref, odd_ref, mid_ref, far_ref, far_blocks, feature_pair, hidden_pair, slope_one, local_ref, grad_x_ref, parts_ref,
):
    channels, rows, cols = field_ref.shape
    tall = rows // 4
    q = cols // 4
    cells = rows * cols
    width = slope_one.shape[0]
    padded = x_ref.shape[0] // rows
    odd = core_ref[0] == 1
    shift = core_ref[0] * tall
    lane = index_of((1, 1, cols), 2)
    for c in range(channels):
        x_ref[c * rows : (c + 1) * rows, :] = field_ref[c]
    before, after = last_ref[...], next_ref[...]
    if chip.ring:
        before, after = jnp.where(odd, after, before), jnp.where(odd, before, after)
    mid_ref[:, : tall // 2, :] = before[:, tall // 2 :, :]
    mid_ref[:, tall // 2 : tall // 2 + tall, :] = here_ref[...]
    mid_ref[:, tall // 2 + tall :, :] = after[:, : tall // 2, :]
    edges = slice(0, chip.edge_tiles)
    previous = jnp.where(odd, got_before[edges], other_before[edges])
    following = jnp.where(odd, got_after[edges], other_after[edges])
    first = tall // 2
    for ref, shifts in ((even_ref, ((0, 3), (2, 1))), (odd_ref, ((-1, 2), (1, 0)))):
        one, two = (
            jnp.where(lane < 2 * q, turned(previous, a * q), turned(following, b * q)) for a, b in shifts
        )
        ref[:, first : first + tall, :] = one[:channels]
        ref[:, first + tall : first + 2 * tall, :] = two[:channels]
        for c in range(channels):
            outer = (two if c % 2 else one)[channels + c // 2]
            ref[c, :first, :] = outer[first:]
            ref[c, first + 2 * tall :, :] = outer[:first]
    middle = (lane >= q) & (lane < 3 * q)
    own = mid_ref[...]
    even_rows = jnp.where(middle, turned(own, q), even_ref[:, pl.ds(shift, 2 * tall), :])
    odd_rows = jnp.where(middle, turned(own, -q), odd_ref[:, pl.ds(shift, 2 * tall), :])
    for c in range(channels):
        at = (channels + c) * rows
        x_ref[pl.ds(at, 2 * tall, stride=2), :] = even_rows[c]
        x_ref[pl.ds(at + 1, 2 * tall, stride=2), :] = odd_rows[c]
    eighth = q // 2
    starts = {-2: -eighth, -1: eighth, 0: 3 * eighth, 1: 5 * eighth, 2: 7 * eighth}
    spans = {e: (e, first + (e + 1) * tall, slice(0, tall)) for e in (-1, 0, 1, 2)}
    spans[-2] = (-2, 0, slice(first, tall))
    spans[3] = (3, first + 4 * tall, slice(0, first))
    for group in range(len(chip.shared)):
        at = chip.quarter_tile(0, group)
        at = slice(at, at + channels)
        columns = {
            -2: jnp.where(odd, other_before[at], got_before[at]),
            -1: jnp.where(odd, got_before[at], other_before[at]),
            0: mine_ref[at],
            1: jnp.where(odd, got_after[at], other_after[at]),
            2: jnp.where(odd, other_after[at], got_after[at]),
        }
        value = turned(columns[2], starts[2] - group % 4 * q)
        for d in (1, 0, -1, -2):
            value = jnp.where(lane < starts[d + 1], turned(columns[d], starts[d] - group % 4 * q), value)
        for e, row, part in spans.values():
            if chip.within(e) and chip.group(e) == group:
                far_ref[:, row : row + part.stop - part.start, :] = value[:, part, :]
    far = far_ref[:, pl.ds(shift, rows), :]
    for c in range(channels):
        x_ref[(2 * channels + c) * rows : (2 * channels + c + 1) * rows, :] = far[c]
    for c in range(3 * channels, padded):
        x_ref[c * rows : (c + 1) * rows, :] = jnp.zeros((rows, cols), F32)

    for block in range(0, rows, 8):
        bands = [
            exchanged([x_ref[c * rows + block : c * rows + block + 8, :] for c in range(k, k + 8)])
            for k in range(0, padded, 8)
        ]
        for i in range(8):
            at = slice((block + i) * cols, (block + i + 1) * cols)
            value = jnp.concatenate([band[i] for band in bands], axis=0)
            local_ref[:padded, at] = value
            high, low = split(value)
            feature_pair[:padded, at] = high
            feature_pair[padded:, at] = low

    lift = lift_ref[...]
    lift_t = lift_t_ref[...]
    steps = [slice(k, k + chunk) for k in range(0, cells, chunk)]
    columns = [slice(i * cols, (i + 1) * cols) for i in range(rows)]
    part_count = parts_ref.shape[1] // cols
    part_columns = [slice(i * cols, (i + 1) * cols) for i in range(part_count)]

    def store_parts(band, values):
        for at, value in zip(part_columns, wave_forward(values)):
            parts_ref[band, at] = value

    def expanded(modes, band_rows):
        parts_ref[:band_rows, :] = halves(dot(stacked(modes), wave_t_ref[...]))

    def unfolded(band):
        return wave_backward([parts_ref[band, at] for at in part_columns], rows)

    bands = [slice(k, k + 8) for k in range(0, width, 8)]

    for k in range(0, padded, 8):
        store_parts(slice(k, k + 8), [local_ref[k : k + 8, at] for at in columns])
    local_product(local_ref, local_one[...], feature_pair, steps)
    modes = contract(parts_ref[:padded, :], wave_ref[...])
    expanded(mix(by_input, 0, exact_dot(lift_t, modes)), width)
    for band in bands:
        hidden = []
        for at, value in zip(columns, unfolded(band)):
            u = value + local_ref[band, at]
            cdf = 0.5 + 0.5 * lax.erf(u * SQRT_HALF)
            slope_one[band, at] = cdf + u * (INV_SQRT_2PI * jnp.exp(-0.5 * u * u))
            hidden.append(u * cdf)
            store_pair(hidden_pair, band.start, width, at, hidden[-1])
        store_parts(band, hidden)

    local_product(local_ref, local_two[...], hidden_pair, steps)
    modes = contract(parts_ref[...], wave_ref[...])
    expanded(mix(by_input, 1, modes), width)
    for band in bands:
        grads = []
        for at, value in zip(columns, unfolded(band)):
            u = value + local_ref[band, at]
            cdf = 0.5 + 0.5 * lax.erf(u * SQRT_HALF)
            slope = cdf + u * (INV_SQRT_2PI * jnp.exp(-0.5 * u * u))
            grads.append(slope * target_grad[band, at])
            store_pair(hidden_pair, band.start, width, at, grads[-1])
        store_parts(band, grads)
    local_product(local_ref, back_two[...], hidden_pair, steps)
    modes = contract(parts_ref[...], wave_ref[...])
    expanded(unmix(by_input, 1, modes), width)
    for band in bands:
        grads = []
        for at, value in zip(columns, unfolded(band)):
            grads.append((value + local_ref[band, at]) * slope_one[band, at])
            store_pair(hidden_pair, band.start, width, at, grads[-1])
        store_parts(band, grads)

    local_product(local_ref.at[:padded], back_one[...], hidden_pair, steps)
    modes = contract(parts_ref[...], wave_ref[...])
    expanded(exact_dot(lift, unmix(by_input, 0, modes)), padded)
    for k in range(0, padded, 8):
        band = slice(k, k + 8)
        values = [value + local_ref[band, at] for at, value in zip(columns, unfolded(band))]
        for block in range(0, rows, 8):
            for c, value in enumerate(exchanged(values[block : block + 8])):
                at = (k + c) * rows + block
                grad_x_ref[at : at + 8, :] = value

    for c in range(channels):
        own_ref[c] = grad_x_ref[c * rows : (c + 1) * rows, :]

    even_grads, odd_grads = [], []
    for c in range(channels):
        at = (channels + c) * rows
        even_grads.append(grad_x_ref[pl.ds(at, 2 * tall, stride=2), :][None])
        odd_grads.append(grad_x_ref[pl.ds(at + 1, 2 * tall, stride=2), :][None])
    even_grads = jnp.concatenate(even_grads, axis=0)
    odd_grads = jnp.concatenate(odd_grads, axis=0)
    center_edge[...] = jnp.where(lane < 2 * q, turned(even_grads, -q), turned(odd_grads, q))
    for ref, value in ((even_ref, even_grads), (odd_ref, odd_grads)):
        ref[...] = jnp.zeros_like(ref)
        ref[:, pl.ds(shift, 2 * tall), :] = value

    def edge_tiles(shifts):
        def pair(one, two):
            return by_group([turned(v, k * q) for v, k in zip((*one, *two), shifts)], cols)

        refs = (even_ref, odd_ref)
        inner = pair(*([ref[:, first + k * tall : first + (k + 1) * tall, :] for ref in refs] for k in (0, 1)))
        outer = [jnp.concatenate([ref[:, first + 2 * tall :, :], ref[:, :first, :]], axis=1) for ref in refs]
        tiles = [inner]
        for c in range(0, channels, 2):
            other = min(c + 1, channels - 1)
            tiles.append(pair([v[c] for v in outer], [v[other] for v in outer])[None])
        return jnp.concatenate(tiles, axis=0)

    near = {-1: edge_tiles((0, 1, 2, 3)), 1: edge_tiles((1, 2, 3, 0))}
    for one, keep, give in ((-1, keep_a, give_a), (1, keep_b, give_b)):
        zero = jnp.zeros_like(near[one])
        keep[: chip.edge_tiles] = jnp.where(odd, near[one], zero)
        give[: chip.edge_tiles] = jnp.where(odd, zero, near[one])
    far_ref[...] = jnp.zeros_like(far_ref)
    for c in range(channels):
        at = (2 * channels + c) * rows
        far_ref[c, pl.ds(shift, rows), :] = grad_x_ref[at : at + rows, :]
    far_blocks[...] = jnp.zeros_like(far_blocks)
    for e in (-1, 0, 1, 2, -2, 3):
        if chip.within(e):
            _, row, part = spans[e]
            far_blocks[chip.group(e), :, part, :] += far_ref[:, row : row + part.stop - part.start, :]
    for start in range(0, len(chip.shared), 4):
        groups = [min(start + k, len(chip.shared) - 1) for k in range(4)]
        at = chip.quarter_tile(0, start)
        at = slice(at, at + channels)
        tiles = {}
        for d in range(-2, 3):
            value = by_group([turned(far_blocks[g], k * q - starts[d]) for k, g in enumerate(groups)], cols)
            if abs(d) == 2:
                value = jnp.where((lane % q >= eighth) == (d < 0), value, 0.0)
            tiles[d] = value
        center_quarter[at.start - chip.edge_tiles : at.stop - chip.edge_tiles] = tiles[0]
        for one, two, keep, give in ((-1, -2, keep_a, give_a), (1, 2, keep_b, give_b)):
            keep[at] = jnp.where(odd, tiles[one], tiles[two])
            give[at] = jnp.where(odd, tiles[two], tiles[one])


def join_kernel(keep_b, keep_a, got_b, got_a, out_b, out_a):
    out_b[...] = keep_b[...] + got_b[...]
    out_a[...] = keep_a[...] + got_a[...]


def gather_kernel(chip, core_ref, center_edge, center_quarter, from_before, from_after, *outs):
    channels, _, cols = center_edge.shape
    tall = from_after.shape[1]
    q, first = cols // 4, tall // 2
    odd = core_ref[0] == 1
    sub = index_of((1, tall, cols), 1)
    lane = index_of((1, 1, cols), 2)
    edges = chip.edge_tiles
    coarse = center_quarter[...] + from_after[edges:] + from_before[edges:]
    rows = []
    for group in range(len(chip.shared)):
        at = chip.quarter_tile(0, group) - edges
        value = jnp.where(lane // q == group % 4, coarse[at : at + channels], 0.0)
        rows.append(value.reshape(channels * tall, cols))
    shared = dot(beside(jnp.concatenate(rows, axis=0)), quarter_matrix(cols, flipped=True))
    shared = shared.reshape(len(chip.shared), channels, tall, cols)
    tail, head = from_after[:edges], from_before[:edges]

    def unpaired(moves):
        return by_group([turned(v, k * q) for v, k in zip((head, tail, head, tail), moves)], cols)

    one, two = unpaired((0, 1, 1, 2)), unpaired((-2, -1, -1, 0))
    outer = [(two if c % 2 else one)[channels + c // 2][None] for c in range(channels)]
    outer = jnp.concatenate(outer, axis=0)
    edge = {
        0: one[:channels],
        1: two[:channels],
        2: jnp.where(sub < first, outer, 0.0),
        -1: jnp.where(sub < first, 0.0, outer),
    }
    shared = {e: shared[chip.group(e)] + edge[e] if e in edge else shared[chip.group(e)] for e in chip.shared}
    if chip.ring:
        shared[3] = shared[-1]
    zero = jnp.zeros((channels, tall, cols), F32)
    blank = zero[:, :first]
    own = {
        -1: jnp.concatenate([blank, center_edge[:, :first, :]], axis=1),
        0: center_edge[:, first : first + tall, :],
        1: jnp.concatenate([center_edge[:, first + tall :, :], blank], axis=1),
    }
    def block_of(offset, is_odd):
        value = shared.get(offset + is_odd, zero)
        return value + own[offset] if offset in own else value

    for out, (even_offset, odd_offset) in zip(outs, chip.slots):
        out[...] = jnp.where(odd, block_of(odd_offset, 1), block_of(even_offset, 0))


def final_kernel(own_ref, *refs):
    out_ref = refs[-1]
    total = refs[0][...]
    for ref in refs[1:-1]:
        total = total + ref[...]
    cols = total.shape[2]
    spread = dot(beside(total.reshape(-1, cols)), spread_matrix(cols))
    count = spread.shape[0]
    for k in range(4):
        part = spread[:, :cols] if k < 2 else spread[:, cols:]
        at = pl.ds(k, count, stride=4)
        out_ref[at, :] = own_ref[at, :] + part


def in_memory(count, space=pltpu.VMEM):
    return [pl.BlockSpec(memory_space=space)] * count


SCALAR = pl.BlockSpec(memory_space=pltpu.SMEM)


def call(kernel, shapes, *operands, scalars=0, scratch=(), name=None, limit=8 << 20, in_place=False, far=(), out_far=()):
    single = not isinstance(shapes, (list, tuple))
    if in_place:
        operands = [pltpu.with_memory_space_constraint(operand, pltpu.HBM) for operand in operands]
    outs = [shapes] if single else list(shapes)
    if in_place:
        far = range(scalars, len(operands))
    places = [SCALAR] * scalars + in_memory(len(operands) - scalars)
    for k in far:
        places[k] = pl.BlockSpec(memory_space=pltpu.HBM)
    out_places = in_memory(len(outs))
    for k in out_far:
        out_places[k] = pl.BlockSpec(memory_space=pltpu.HBM)
        outs[k] = pltpu.HBM(outs[k].shape, outs[k].dtype)
    result = pl.pallas_call(
        kernel,
        out_shape=outs,
        in_specs=places,
        out_specs=out_places,
        scratch_shapes=list(scratch),
        compiler_params=pltpu.CompilerParams(vmem_limit_bytes=limit),
        name=name,
    )(*operands)
    return result[0] if single else result


def body(field, cotangent, lift, spectral, pointwise, project):
    channels, levels, rows, cols = field.shape
    width = lift.shape[1]
    layers = spectral.shape[0]
    modes = spectral.shape[2]
    features = lift.shape[0]
    cells = rows * cols
    tall = rows // 4
    gx, gy = lax.axis_size("gx"), lax.axis_size("gy")
    chip = Chip(gx, channels)
    core = (lax.axis_index("gx") % 2).astype(jnp.int32).reshape(1)

    def shape(*dims, dtype=F32):
        return jax.ShapeDtypeStruct(dims, dtype)

    def along_y(value, even_steps, odd_steps):
        pairs = []
        for a in range(gx):
            for b in range(gy):
                steps = odd_steps if a % 2 else even_steps
                pairs.append((a * gy + b, a * gy + (b + steps) % gy))
        return lax.ppermute(value, ("gx", "gy"), pairs)

    def swap(value):
        return lax.ppermute(value, "gx", [(s, s ^ 1) for s in range(gx)])

    flat_field = field.reshape(channels * rows, cols)
    packed = call(pool_kernel, shape(channels * tall, cols), flat_field, name="pool")
    packed = packed.reshape(channels, tall, cols)

    others = range(1, len(chip.slots))
    held = [packed] + [lax.ppermute(packed, "gx", chip.pairs(slot)) for slot in others]
    wave = wave_matrix(rows, cols)
    padded = -(-features // 16) * 16
    small = -(-channels // 8) * 8
    constants = [wave_pair(wave, 1), wave_pair(wave.T, 0)]
    packed_weights = shape(layers, width, width, 2 * modes)
    prepared = list(call(
        prepare_kernel,
        [shape(*c.shape, dtype=BF16) for c in constants]
        + [
            packed_weights, shape(padded, width), shape(width, padded), shape(width, 3 * padded, dtype=BF16),
            shape(width, 3 * width, dtype=BF16), shape(width, 3 * width, dtype=BF16), shape(padded, 3 * width, dtype=BF16),
            shape(width, cells),
        ],
        cotangent.reshape(channels * rows, cols), lift, jnp.transpose(spectral, (0, 1, 3, 4, 2)), pointwise, project.T,
        *constants,
        in_place=True,
        scratch=(
            pltpu.VMEM((layers, 2, width, width, modes), F32),
            pltpu.VMEM((small * rows, cols), F32),
            pltpu.VMEM((padded, width), F32),
            pltpu.VMEM((layers, width, width), F32),
            pltpu.VMEM((small, width), F32),
            pltpu.SemaphoreType.DMA((6 + layers,)),
        ),
        limit=16 << 20,
        name="prepare",
    ))
    *held[1:], prepared[3] = lax.optimization_barrier((*held[1:], prepared[3]))
    message = shape(chip.tiles, tall, cols)
    to_previous, to_following = call(
        functools.partial(pack_kernel, chip), (message, message), core, *held, scalars=1, name="pack"
    )
    from_a = along_y(to_previous, -2, -1)
    from_b = along_y(to_following, 2, 1)
    swap_a, swap_b = swap(from_a), swap(from_b)

    chunk = 4 * cols
    quarter_part = shape(chip.tiles - chip.edge_tiles, tall, cols)
    own, center_edge, center_quarter, keep_a, keep_b, give_a, give_b = call(
        functools.partial(network_kernel, chip, chunk),
        (shape(channels, rows, cols), shape(channels, 2 * tall, cols), quarter_part, message, message, message, message),
        core, field.reshape(channels, rows, cols), held[0], held[chip.place(1, 0)], held[chip.place(-1, 0)],
        to_previous, from_a, from_b, swap_a, swap_b, *prepared,
        scalars=1,
        scratch=(
            pltpu.VMEM((padded * rows, cols), F32),
            pltpu.VMEM((channels, 3 * tall, cols), F32),
            pltpu.VMEM((channels, 3 * tall, cols), F32),
            pltpu.VMEM((channels, 2 * tall, cols), F32),
            pltpu.VMEM((channels, rows + tall, cols), F32),
            pltpu.VMEM((len(chip.shared), channels, tall, cols), F32),
            pltpu.VMEM((2 * padded, cells), BF16),
            pltpu.VMEM((2 * width, cells), BF16),
            pltpu.VMEM((width, cells), F32),
            pltpu.VMEM((width, cells), F32),
            pltpu.VMEM((padded * rows, cols), F32),
            pltpu.VMEM((width, wave.shape[0]), F32),
        ),
        limit=16 << 20,
        name="network",
    )

    got_a, got_b = swap(give_a), swap(give_b)
    sum_b, sum_a = call(join_kernel, (message, message), keep_b, keep_a, got_b, got_a, name="join")
    sum_b = along_y(sum_b, 2, 1)
    sum_a = along_y(sum_a, -2, -1)
    parts = call(
        functools.partial(gather_kernel, chip),
        [shape(channels, tall, cols)] * len(chip.slots),
        core, center_edge, center_quarter, sum_b, sum_a, scalars=1,
        name="gather",
    )
    parts = [parts[0]] + [lax.ppermute(parts[slot], "gx", chip.pairs(slot, back=True)) for slot in others]
    out = call(
        final_kernel,
        shape(channels * rows, cols),
        own.reshape(channels * rows, cols), *parts,
        name="final",
    )
    return out.reshape(field.shape)


def solution(mesh):
    return jax.shard_map(
        body,
        mesh=mesh,
        in_specs=(P(None, None, "gx", "gy"), P(None, None, "gx", "gy"), P(), P(), P(), P()),
        out_specs=P(None, None, "gx", "gy"),
        check_vma=False,
    )
```

```python
import functools

import jax
import jax.numpy as jnp
import numpy as np
from jax import lax
from jax.experimental import pallas as pl
from jax.experimental.pallas import tpu as pltpu
from jax.sharding import PartitionSpec as P

MODES = 8
F32 = jnp.float32
BF16 = jnp.bfloat16
HIGHEST = lax.Precision.HIGHEST
SQRT_HALF = float(np.sqrt(0.5))
INV_SQRT_2PI = float(1.0 / np.sqrt(2.0 * np.pi))


class Chip:
    def __init__(self, count, channels):
        self.count = count
        self.ring = count == 4
        if self.ring:
            self.slots = [(0, 0), (1, -1), (2, 2), (-1, 1)]
        else:
            self.slots = [(k, k) for k in (0, 1, 2, -1, -2, 3, -3)]
        self.shared = [0, 1, 2, -1] if self.ring else [-2, -1, 0, 1, 2, 3]
        self.edge_tiles = channels + (channels + 1) // 2
        self.tiles = self.edge_tiles + channels * -(-len(self.shared) // 4)

    def place(self, offset, odd):
        offset = (offset + 1) % 4 - 1 if self.ring else offset
        return [slot[odd] for slot in self.slots].index(offset)

    def pairs(self, slot, back=False):
        count = self.count
        if self.ring:
            return [(s, s ^ slot) for s in range(count)]
        steps = self.slots[slot][0] if back else -self.slots[slot][0]
        return [(s, (s + steps) % count) for s in range(count)]

    def group(self, offset):
        return offset % 4 if self.ring else self.shared.index(offset)

    def within(self, offset):
        return self.ring or offset in self.shared

    def quarter_tile(self, channel, group):
        channels = (self.tiles - self.edge_tiles) // -(-len(self.shared) // 4)
        return self.edge_tiles + (group // 4) * channels + channel


def split(value):
    high = value.astype(BF16)
    return high, (value - high.astype(F32)).astype(BF16)


def dot(left, right):
    return jnp.dot(left, right, preferred_element_type=F32)


def dot_t(left, right):
    return lax.dot_general(left, right, (((1,), (1,)), ((), ())), precision=HIGHEST, preferred_element_type=F32)


def exact_dot(left, right):
    return jnp.dot(left, right, precision=HIGHEST, preferred_element_type=F32)


def stacked(value):
    high, low = split(value)
    top = jnp.concatenate([high, high], axis=1)
    bottom = jnp.concatenate([low, jnp.zeros_like(low)], axis=1)
    return jnp.concatenate([top, bottom], axis=0)


def halves(value):
    rows = value.shape[0] // 2
    return value[:rows] + value[rows:]


def wave_matrix(rows, cols):
    m = np.arange(MODES * MODES)
    wave_x, wave_y = m // MODES - MODES // 2, m % MODES
    b = 2.0 * np.pi * ((np.arange(cols)[:, None] * wave_y[None]) % cols) / cols
    scale = 1.0 / np.sqrt(rows * cols)
    cos, sin = np.cos(b) * scale, np.sin(b) * scale
    parts = []
    for k in range(MODES // 2 + 1):
        held = (np.abs(wave_x) == k)[None]
        parts.append(np.concatenate([cos * held, -sin * held], 1))
    for k in range(1, MODES // 2 + 1):
        held = (np.sign(wave_x) * (np.abs(wave_x) == k))[None]
        parts.append(np.concatenate([-sin * held, -cos * held], 1))
    return np.concatenate(parts, 0).astype(np.float32)


def wave_pair(matrix, axis):
    high = matrix.astype(BF16)
    low = (matrix - high.astype(np.float32)).astype(BF16)
    return jnp.asarray(np.concatenate([high, low], axis))


def weighted(terms):
    groups = {}
    for factor, value in terms:
        size = round(abs(factor), 12)
        if size == 0:
            continue
        groups.setdefault(size, []).append((factor > 0, value, abs(factor)))
    total = None
    for size, members in groups.items():
        members.sort(key=lambda member: not member[0])
        part = members[0][1] if members[0][0] else -members[0][1]
        for positive, value, _ in members[1:]:
            part = part + value if positive else part - value
        if size != 1:
            part = part * members[0][2]
        total = part if total is None else total + part
    return total


def wave_forward(values):
    n = len(values)
    top = MODES // 2
    angle = lambda k, i: 2.0 * np.pi * ((k * i) % n) / n
    plus = [values[0]] + [values[i] + values[n - i] for i in range(1, n // 2)] + [values[n // 2]]
    minus = [None] + [values[i] - values[n - i] for i in range(1, n // 2)]
    even = [plus[i] + plus[n // 2 - i] for i in range(n // 4)] + [plus[n // 4]]
    odd = [plus[i] - plus[n // 2 - i] for i in range(n // 4)]
    minus_odd = [None] + [minus[i] + minus[n // 2 - i] for i in range(1, n // 4)] + [minus[n // 4]]
    minus_even = [None] + [minus[i] - minus[n // 2 - i] for i in range(1, n // 4)]
    deep = {
        1: [even[i] + even[n // 4 - i] for i in range(n // 8)],
        -1: [even[i] - even[n // 4 - i] for i in range(n // 8)],
    }
    deep_minus = {
        1: [None] + [minus_even[i] - minus_even[n // 4 - i] for i in range(1, n // 8)],
        -1: [None] + [minus_even[i] + minus_even[n // 4 - i] for i in range(1, n // 8)],
    }
    out = []
    for k in range(top + 1):
        if k % 2:
            out.append(weighted([(np.cos(angle(k, i)), odd[i]) for i in range(n // 4)]))
        else:
            sign = 1 if k % 4 == 0 else -1
            terms = [(np.cos(angle(k, i)), deep[sign][i]) for i in range(n // 8)]
            out.append(weighted(terms + [(np.cos(angle(k, n // 8)), even[n // 8])]))
    for k in range(1, top + 1):
        if k % 2:
            out.append(weighted([(np.sin(angle(k, i)), minus_odd[i]) for i in range(1, n // 4 + 1)]))
        else:
            sign = 1 if k % 4 == 0 else -1
            terms = [(np.sin(angle(k, i)), deep_minus[sign][i]) for i in range(1, n // 8)]
            out.append(weighted(terms + [(np.sin(angle(k, n // 8)), minus_even[n // 8])]))
    return out


def added(a, b):
    return b if a is None else a if b is None else a + b


def taken(a, b):
    return a if b is None else -b if a is None else a - b


def wave_backward(parts, n):
    top = MODES // 2
    angle = lambda k, i: 2.0 * np.pi * ((k * i) % n) / n
    cosine = lambda i, ks: weighted([(np.cos(angle(k, i)), parts[k]) for k in ks])
    sine = lambda i, ks: weighted([(np.sin(angle(k, i)), parts[top + k]) for k in ks])
    fours = [k for k in range(top + 1) if k % 4 == 0]
    twos = [k for k in range(top + 1) if k % 4 == 2]
    odds = [k for k in range(top + 1) if k % 2]
    even = [None] * (n // 4 + 1)
    for i in range(n // 8):
        a, b = cosine(i, fours), cosine(i, twos)
        even[i], even[n // 4 - i] = added(a, b), taken(a, b)
    even[n // 8] = cosine(n // 8, sorted(fours + twos))
    plus = [None] * (n // 2 + 1)
    for i in range(n // 4):
        b = cosine(i, odds)
        plus[i], plus[n // 2 - i] = added(even[i], b), taken(even[i], b)
    plus[n // 4] = even[n // 4]
    minus_even = [None] * (n // 4)
    for i in range(1, n // 8):
        a, b = sine(i, [k for k in fours if k]), sine(i, twos)
        minus_even[i], minus_even[n // 4 - i] = added(b, a), taken(b, a)
    minus_even[n // 8] = sine(n // 8, sorted(k for k in fours + twos if k))
    minus = [None] * (n // 2)
    for i in range(1, n // 4):
        a = sine(i, odds)
        minus[i], minus[n // 2 - i] = added(a, minus_even[i]), taken(a, minus_even[i])
    minus[n // 4] = sine(n // 4, odds)
    out = [None] * n
    out[0], out[n // 2] = plus[0], plus[n // 2]
    for i in range(1, n // 2):
        out[i], out[n - i] = added(plus[i], minus[i]), taken(plus[i], minus[i])
    return out


def prepare_kernel(
    cotangent_hbm, lift_hbm, spectral_hbm, pointwise_hbm, project_hbm, *refs
):
    constants_hbm, refs = refs[:2], refs[2:]
    constants, refs = refs[:2], refs[2:]
    by_input, lift_ref, lift_t_ref, local_one, local_two, back_two, back_one, target_grad = refs[:8]
    spectral_ref, target_ref, lift_in, pointwise_ref, project_ref, sems = refs[8:]
    layers, _, width, _, modes = spectral_ref.shape
    small, cols = project_ref.shape[0], target_ref.shape[1]
    rows = target_ref.shape[0] // small
    channels, features = project_hbm.shape[0], lift_hbm.shape[0]
    pairs = [
        (cotangent_hbm, target_ref.at[: channels * rows]),
        (project_hbm, project_ref.at[:channels]),
        (lift_hbm, lift_in.at[:features]),
        (pointwise_hbm, pointwise_ref),
    ]
    pairs += [(spectral_hbm.at[layer], spectral_ref.at[layer]) for layer in range(layers)]
    pairs += list(zip(constants_hbm, constants))
    copies = [pltpu.make_async_copy(source, target, sems.at[k]) for k, (source, target) in enumerate(pairs)]
    for copy in copies:
        copy.start()
    target_ref[channels * rows :, :] = jnp.zeros(((small - channels) * rows, cols), F32)
    project_ref[channels:, :] = jnp.zeros((small - channels, width), F32)
    lift_in[features:, :] = jnp.zeros((lift_in.shape[0] - features, width), F32)
    for copy in copies[:4]:
        copy.wait()

    lift = lift_in[...]
    lift_t = jnp.transpose(lift)
    lift_ref[...] = lift
    lift_t_ref[...] = lift_t
    back_one[...] = tripled(exact_dot(lift, pointwise_ref[0]))
    local_one[...] = tripled(exact_dot(jnp.transpose(pointwise_ref[0]), lift_t))
    local_two[...] = tripled(jnp.transpose(pointwise_ref[1]))
    back_two[...] = tripled(pointwise_ref[1])
    out = tripled(jnp.transpose(project_ref[...]))
    group = 4
    for first in range(0, rows, group):
        pieces = []
        for i in range(first, first + group):
            value = target_ref[pl.ds(i, small, stride=rows), :]
            high = value.astype(BF16).astype(F32)
            pieces.append(jnp.concatenate([high, value - high, high], axis=0).astype(BF16))
        target_grad[:, first * cols : (first + group) * cols] = dot(out, jnp.concatenate(pieces, axis=1))

    for layer in range(layers):
        copies[4 + layer].wait()
        for w in range(width):
            both = [spectral_ref[layer, part, w] for part in range(2)]
            by_input[layer, w] = jnp.concatenate(both, axis=1)
    for copy in copies[4 + layers :]:
        copy.wait()


def index_of(shape, axis):
    return lax.broadcasted_iota(jnp.int32, shape, axis)


def quarter_matrix(cols, flipped=False):
    shape = (2 * cols, cols)
    fine, coarse = (index_of(shape, 1), index_of(shape, 0)) if flipped else (index_of(shape, 0), index_of(shape, 1))
    fine, coarse = fine % (cols // 2) // 2, coarse % (cols // 4)
    return jnp.where(fine == coarse, 0.25, 0.0).astype(BF16)


def spread_matrix(cols):
    shape = (2 * cols, 2 * cols)
    row, col = index_of(shape, 0) % cols, index_of(shape, 1)
    return jnp.where(row == col // 2, 0.25, 0.0).astype(BF16)


def pooling_matrix(cols):
    shape = (2 * cols, cols)
    return jnp.where(index_of(shape, 0) // 2 == index_of(shape, 1), 0.25, 0.0).astype(BF16)


def beside(value):
    return jnp.concatenate(split(value), axis=1)


def above(value):
    return jnp.concatenate(split(value), axis=0)


def turned(value, steps):
    lanes = value.shape[-1]
    if steps % lanes == 0:
        return value
    flat = value.reshape(-1, lanes)
    return pltpu.roll(flat, steps % lanes, 1).reshape(value.shape)


def by_group(values, lanes):
    lane = index_of((1,) * (values[0].ndim - 1) + (lanes,), values[0].ndim - 1)
    q = lanes // 4
    low = jnp.where(lane < q, values[0], values[1])
    high = jnp.where(lane < 3 * q, values[2], values[3])
    return jnp.where(lane < 2 * q, low, high)


def pool_kernel(field_ref, out_ref):
    count = field_ref.shape[0] // 4
    rows = [field_ref[pl.ds(k, count, stride=4), :] for k in range(4)]
    pairs = jnp.concatenate([rows[0] + rows[1], rows[2] + rows[3]], axis=1)
    out_ref[...] = halves(dot(above(pairs), pooling_matrix(field_ref.shape[1])))


def pack_kernel(chip, core_ref, *refs):
    blocks, (to_previous, to_following) = refs[: len(chip.slots)], refs[len(chip.slots) :]
    channels, tall, cols = blocks[0].shape
    q = cols // 4
    odd = core_ref[0] == 1
    sub = index_of((1, tall, cols), 1)
    shared = {}
    for e in chip.shared:
        even_at, odd_at = chip.place(e, 0), chip.place(e - 1, 1)
        shared[e] = jnp.where(odd, blocks[odd_at][...], blocks[even_at][...])
    stacked_rows = jnp.concatenate([shared[e].reshape(channels * tall, cols) for e in chip.shared], axis=0)
    coarse = dot(beside(stacked_rows), quarter_matrix(cols)).reshape(len(chip.shared), channels, tall, cols)
    for first in range(0, len(chip.shared), 4):
        groups = [min(first + k, len(chip.shared) - 1) for k in range(4)]
        tile = by_group([coarse[k] for k in groups], cols)
        at = chip.quarter_tile(0, first)
        to_previous[at : at + channels] = tile
        to_following[at : at + channels] = tile
    outer = jnp.where(sub < tall // 2, shared[2], shared[-1])

    def pair(one, two, shifts):
        return by_group([turned(v, k * q) for v, k in zip((one, one, two, two), shifts)], cols)

    for ref, shifts in ((to_previous, (0, -1, 2, 1)), (to_following, (-1, -2, 1, 0))):
        ref[:channels] = pair(shared[0], shared[1], shifts)
        for c in range(0, channels, 2):
            ref[channels + c // 2] = pair(outer[c], outer[min(c + 1, channels - 1)], shifts)


def mix(weights, layer, coefficients):
    width, lanes = coefficients.shape
    half = lanes // 2
    lane = lax.broadcasted_iota(jnp.int32, (width, lanes), 1)
    swapped = pltpu.roll(coefficients, half, 1)
    signed = jnp.where(lane < half, coefficients, -coefficients)
    total_real, total_imag = [None] * 4, [None] * 4
    for w in range(width):
        block = weights[layer, w]
        total_real[w % 4] = added(total_real[w % 4], block * signed[w : w + 1])
        total_imag[w % 4] = added(total_imag[w % 4], block * swapped[w : w + 1])
    total_real, total_imag = sum(total_real), sum(total_imag)
    total_real += pltpu.roll(total_real, half, 1)
    total_imag += pltpu.roll(total_imag, half, 1)
    return jnp.where(lane < half, total_real, total_imag)


def rows_summed(values):
    row = index_of(values[0].shape, 0)
    step = 1
    while len(values) > 1:
        held = (row & step) != 0
        values = [
            jnp.where(held, x, y) + pltpu.roll(jnp.where(held, y, x), step, 0) for y, x in zip(values[::2], values[1::2])
        ]
        step *= 2
    return values[0]


def exchanged(values):
    row = index_of(values[0].shape, 0)
    for step in (1, 2, 4):
        held = (row & step) != 0
        values = list(values)
        for k in range(8):
            if not k & step:
                a, b = values[k], values[k + step]
                values[k] = jnp.where(held, pltpu.roll(b, step, 0), a)
                values[k + step] = jnp.where(held, b, pltpu.roll(a, 8 - step, 0))
    return values


def unmix(weights, layer, grads):
    width, lanes = grads.shape
    half = lanes // 2
    lane = index_of((width, lanes), 1)
    turned_grads = pltpu.roll(grads, half, 1)
    turned_grads = jnp.where(lane < half, turned_grads, -turned_grads)

    def folded(block, value):
        product = block * value
        return sum(product[k : k + 8] for k in range(8, width, 8)) + product[:8]

    real, imag = [], []
    for first in range(0, width, 8):
        blocks = [weights[layer, w] for w in range(first, first + 8)]
        real.append(rows_summed([folded(block, grads) for block in blocks]))
        imag.append(rows_summed([folded(block, turned_grads) for block in blocks]))
    real, imag = jnp.concatenate(real, axis=0), jnp.concatenate(imag, axis=0)
    real += pltpu.roll(real, half, 1)
    imag += pltpu.roll(imag, half, 1)
    return jnp.where(lane < half, real, imag)


def contract(parts, wave):
    high, low = split(parts)
    both = dot(jnp.concatenate([high, low], axis=0), wave)
    rows, modes = both.shape[0] // 2, both.shape[1] // 2
    return both[:rows, :modes] + both[:rows, modes:] + both[rows:, :modes]


def tripled(value):
    high, low = split(value)
    return jnp.concatenate([high, high, low], axis=1)


def local_product(out_ref, left, pair_ref, steps):
    rows = pair_ref.shape[0] // 2
    for at in steps:
        right = jnp.concatenate([pair_ref[:, at], pair_ref[:rows, at]], axis=0)
        out_ref[:, at] = dot(left, right)


def store_pair(pair_ref, first, rows_total, at, value):
    high, low = split(value)
    count = value.shape[0]
    pair_ref[first : first + count, at] = high
    pair_ref[rows_total + first : rows_total + first + count, at] = low


def network_kernel(
    chip, chunk,
    core_ref, field_ref, here_ref, next_ref, last_ref, mine_ref, got_after, got_before, other_after, other_before,
    wave_ref, wave_t_ref, by_input, lift_ref, lift_t_ref, local_one, local_two, back_two, back_one, target_grad,
    own_ref, center_edge, center_quarter, keep_a, keep_b, give_a, give_b,
    x_ref, even_ref, odd_ref, mid_ref, far_ref, far_blocks, feature_pair, hidden_pair, slope_one, local_ref, grad_x_ref, parts_ref,
):
    channels, rows, cols = field_ref.shape
    tall = rows // 4
    q = cols // 4
    cells = rows * cols
    width = slope_one.shape[0]
    padded = x_ref.shape[0] // rows
    odd = core_ref[0] == 1
    shift = core_ref[0] * tall
    lane = index_of((1, 1, cols), 2)
    for c in range(channels):
        x_ref[c * rows : (c + 1) * rows, :] = field_ref[c]
    before, after = last_ref[...], next_ref[...]
    if chip.ring:
        before, after = jnp.where(odd, after, before), jnp.where(odd, before, after)
    mid_ref[:, : tall // 2, :] = before[:, tall // 2 :, :]
    mid_ref[:, tall // 2 : tall // 2 + tall, :] = here_ref[...]
    mid_ref[:, tall // 2 + tall :, :] = after[:, : tall // 2, :]
    edges = slice(0, chip.edge_tiles)
    previous = jnp.where(odd, got_before[edges], other_before[edges])
    following = jnp.where(odd, got_after[edges], other_after[edges])
    first = tall // 2
    for ref, shifts in ((even_ref, ((0, 3), (2, 1))), (odd_ref, ((-1, 2), (1, 0)))):
        one, two = (
            jnp.where(lane < 2 * q, turned(previous, a * q), turned(following, b * q)) for a, b in shifts
        )
        ref[:, first : first + tall, :] = one[:channels]
        ref[:, first + tall : first + 2 * tall, :] = two[:channels]
        for c in range(channels):
            outer = (two if c % 2 else one)[channels + c // 2]
            ref[c, :first, :] = outer[first:]
            ref[c, first + 2 * tall :, :] = outer[:first]
    middle = (lane >= q) & (lane < 3 * q)
    own = mid_ref[...]
    even_rows = jnp.where(middle, turned(own, q), even_ref[:, pl.ds(shift, 2 * tall), :])
    odd_rows = jnp.where(middle, turned(own, -q), odd_ref[:, pl.ds(shift, 2 * tall), :])
    for c in range(channels):
        at = (channels + c) * rows
        x_ref[pl.ds(at, 2 * tall, stride=2), :] = even_rows[c]
        x_ref[pl.ds(at + 1, 2 * tall, stride=2), :] = odd_rows[c]
    eighth = q // 2
    starts = {-2: -eighth, -1: eighth, 0: 3 * eighth, 1: 5 * eighth, 2: 7 * eighth}
    spans = {e: (e, first + (e + 1) * tall, slice(0, tall)) for e in (-1, 0, 1, 2)}
    spans[-2] = (-2, 0, slice(first, tall))
    spans[3] = (3, first + 4 * tall, slice(0, first))
    for group in range(len(chip.shared)):
        at = chip.quarter_tile(0, group)
        at = slice(at, at + channels)
        columns = {
            -2: jnp.where(odd, other_before[at], got_before[at]),
            -1: jnp.where(odd, got_before[at], other_before[at]),
            0: mine_ref[at],
            1: jnp.where(odd, got_after[at], other_after[at]),
            2: jnp.where(odd, other_after[at], got_after[at]),
        }
        value = turned(columns[2], starts[2] - group % 4 * q)
        for d in (1, 0, -1, -2):
            value = jnp.where(lane < starts[d + 1], turned(columns[d], starts[d] - group % 4 * q), value)
        for e, row, part in spans.values():
            if chip.within(e) and chip.group(e) == group:
                far_ref[:, row : row + part.stop - part.start, :] = value[:, part, :]
    far = far_ref[:, pl.ds(shift, rows), :]
    for c in range(channels):
        x_ref[(2 * channels + c) * rows : (2 * channels + c + 1) * rows, :] = far[c]
    for c in range(3 * channels, padded):
        x_ref[c * rows : (c + 1) * rows, :] = jnp.zeros((rows, cols), F32)

    for block in range(0, rows, 8):
        bands = [
            exchanged([x_ref[c * rows + block : c * rows + block + 8, :] for c in range(k, k + 8)])
            for k in range(0, padded, 8)
        ]
        for i in range(8):
            at = slice((block + i) * cols, (block + i + 1) * cols)
            value = jnp.concatenate([band[i] for band in bands], axis=0)
            local_ref[:padded, at] = value
            high, low = split(value)
            feature_pair[:padded, at] = high
            feature_pair[padded:, at] = low

    lift = lift_ref[...]
    lift_t = lift_t_ref[...]
    steps = [slice(k, k + chunk) for k in range(0, cells, chunk)]
    columns = [slice(i * cols, (i + 1) * cols) for i in range(rows)]
    part_count = parts_ref.shape[1] // cols
    part_columns = [slice(i * cols, (i + 1) * cols) for i in range(part_count)]

    def store_parts(band, values):
        for at, value in zip(part_columns, wave_forward(values)):
            parts_ref[band, at] = value

    def expanded(modes, band_rows):
        parts_ref[:band_rows, :] = halves(dot(stacked(modes), wave_t_ref[...]))

    def unfolded(band):
        return wave_backward([parts_ref[band, at] for at in part_columns], rows)

    bands = [slice(k, k + 8) for k in range(0, width, 8)]

    for k in range(0, padded, 8):
        store_parts(slice(k, k + 8), [local_ref[k : k + 8, at] for at in columns])
    local_product(local_ref, local_one[...], feature_pair, steps)
    modes = contract(parts_ref[:padded, :], wave_ref[...])
    expanded(mix(by_input, 0, exact_dot(lift_t, modes)), width)
    for band in bands:
        hidden = []
        for at, value in zip(columns, unfolded(band)):
            u = value + local_ref[band, at]
            cdf = 0.5 + 0.5 * lax.erf(u * SQRT_HALF)
            slope_one[band, at] = cdf + u * (INV_SQRT_2PI * jnp.exp(-0.5 * u * u))
            hidden.append(u * cdf)
            store_pair(hidden_pair, band.start, width, at, hidden[-1])
        store_parts(band, hidden)

    local_product(local_ref, local_two[...], hidden_pair, steps)
    modes = contract(parts_ref[...], wave_ref[...])
    expanded(mix(by_input, 1, modes), width)
    for band in bands:
        grads = []
        for at, value in zip(columns, unfolded(band)):
            u = value + local_ref[band, at]
            cdf = 0.5 + 0.5 * lax.erf(u * SQRT_HALF)
            slope = cdf + u * (INV_SQRT_2PI * jnp.exp(-0.5 * u * u))
            grads.append(slope * target_grad[band, at])
            store_pair(hidden_pair, band.start, width, at, grads[-1])
        store_parts(band, grads)
    local_product(local_ref, back_two[...], hidden_pair, steps)
    modes = contract(parts_ref[...], wave_ref[...])
    expanded(unmix(by_input, 1, modes), width)
    for band in bands:
        grads = []
        for at, value in zip(columns, unfolded(band)):
            grads.append((value + local_ref[band, at]) * slope_one[band, at])
            store_pair(hidden_pair, band.start, width, at, grads[-1])
        store_parts(band, grads)

    local_product(local_ref.at[:padded], back_one[...], hidden_pair, steps)
    modes = contract(parts_ref[...], wave_ref[...])
    expanded(exact_dot(lift, unmix(by_input, 0, modes)), padded)
    for k in range(0, padded, 8):
        band = slice(k, k + 8)
        values = [value + local_ref[band, at] for at, value in zip(columns, unfolded(band))]
        for block in range(0, rows, 8):
            for c, value in enumerate(exchanged(values[block : block + 8])):
                at = (k + c) * rows + block
                grad_x_ref[at : at + 8, :] = value

    for c in range(channels):
        own_ref[c] = grad_x_ref[c * rows : (c + 1) * rows, :]

    even_grads, odd_grads = [], []
    for c in range(channels):
        at = (channels + c) * rows
        even_grads.append(grad_x_ref[pl.ds(at, 2 * tall, stride=2), :][None])
        odd_grads.append(grad_x_ref[pl.ds(at + 1, 2 * tall, stride=2), :][None])
    even_grads = jnp.concatenate(even_grads, axis=0)
    odd_grads = jnp.concatenate(odd_grads, axis=0)
    center_edge[...] = jnp.where(lane < 2 * q, turned(even_grads, -q), turned(odd_grads, q))
    for ref, value in ((even_ref, even_grads), (odd_ref, odd_grads)):
        ref[...] = jnp.zeros_like(ref)
        ref[:, pl.ds(shift, 2 * tall), :] = value

    def edge_tiles(shifts):
        def pair(one, two):
            return by_group([turned(v, k * q) for v, k in zip((*one, *two), shifts)], cols)

        refs = (even_ref, odd_ref)
        inner = pair(*([ref[:, first + k * tall : first + (k + 1) * tall, :] for ref in refs] for k in (0, 1)))
        outer = [jnp.concatenate([ref[:, first + 2 * tall :, :], ref[:, :first, :]], axis=1) for ref in refs]
        tiles = [inner]
        for c in range(0, channels, 2):
            other = min(c + 1, channels - 1)
            tiles.append(pair([v[c] for v in outer], [v[other] for v in outer])[None])
        return jnp.concatenate(tiles, axis=0)

    near = {-1: edge_tiles((0, 1, 2, 3)), 1: edge_tiles((1, 2, 3, 0))}
    for one, keep, give in ((-1, keep_a, give_a), (1, keep_b, give_b)):
        zero = jnp.zeros_like(near[one])
        keep[: chip.edge_tiles] = jnp.where(odd, near[one], zero)
        give[: chip.edge_tiles] = jnp.where(odd, zero, near[one])
    far_ref[...] = jnp.zeros_like(far_ref)
    for c in range(channels):
        at = (2 * channels + c) * rows
        far_ref[c, pl.ds(shift, rows), :] = grad_x_ref[at : at + rows, :]
    far_blocks[...] = jnp.zeros_like(far_blocks)
    for e in (-1, 0, 1, 2, -2, 3):
        if chip.within(e):
            _, row, part = spans[e]
            far_blocks[chip.group(e), :, part, :] += far_ref[:, row : row + part.stop - part.start, :]
    for start in range(0, len(chip.shared), 4):
        groups = [min(start + k, len(chip.shared) - 1) for k in range(4)]
        at = chip.quarter_tile(0, start)
        at = slice(at, at + channels)
        tiles = {}
        for d in range(-2, 3):
            value = by_group([turned(far_blocks[g], k * q - starts[d]) for k, g in enumerate(groups)], cols)
            if abs(d) == 2:
                value = jnp.where((lane % q >= eighth) == (d < 0), value, 0.0)
            tiles[d] = value
        center_quarter[at.start - chip.edge_tiles : at.stop - chip.edge_tiles] = tiles[0]
        for one, two, keep, give in ((-1, -2, keep_a, give_a), (1, 2, keep_b, give_b)):
            keep[at] = jnp.where(odd, tiles[one], tiles[two])
            give[at] = jnp.where(odd, tiles[two], tiles[one])


def join_kernel(keep_b, keep_a, got_b, got_a, out_b, out_a):
    out_b[...] = keep_b[...] + got_b[...]
    out_a[...] = keep_a[...] + got_a[...]


def gather_kernel(chip, core_ref, center_edge, center_quarter, from_before, from_after, *outs):
    channels, _, cols = center_edge.shape
    tall = from_after.shape[1]
    q, first = cols // 4, tall // 2
    odd = core_ref[0] == 1
    sub = index_of((1, tall, cols), 1)
    lane = index_of((1, 1, cols), 2)
    edges = chip.edge_tiles
    coarse = center_quarter[...] + from_after[edges:] + from_before[edges:]
    rows = []
    for group in range(len(chip.shared)):
        at = chip.quarter_tile(0, group) - edges
        value = jnp.where(lane // q == group % 4, coarse[at : at + channels], 0.0)
        rows.append(value.reshape(channels * tall, cols))
    shared = dot(beside(jnp.concatenate(rows, axis=0)), quarter_matrix(cols, flipped=True))
    shared = shared.reshape(len(chip.shared), channels, tall, cols)
    tail, head = from_after[:edges], from_before[:edges]

    def unpaired(moves):
        return by_group([turned(v, k * q) for v, k in zip((head, tail, head, tail), moves)], cols)

    one, two = unpaired((0, 1, 1, 2)), unpaired((-2, -1, -1, 0))
    outer = [(two if c % 2 else one)[channels + c // 2][None] for c in range(channels)]
    outer = jnp.concatenate(outer, axis=0)
    edge = {
        0: one[:channels],
        1: two[:channels],
        2: jnp.where(sub < first, outer, 0.0),
        -1: jnp.where(sub < first, 0.0, outer),
    }
    shared = {e: shared[chip.group(e)] + edge[e] if e in edge else shared[chip.group(e)] for e in chip.shared}
    if chip.ring:
        shared[3] = shared[-1]
    zero = jnp.zeros((channels, tall, cols), F32)
    blank = zero[:, :first]
    own = {
        -1: jnp.concatenate([blank, center_edge[:, :first, :]], axis=1),
        0: center_edge[:, first : first + tall, :],
        1: jnp.concatenate([center_edge[:, first + tall :, :], blank], axis=1),
    }
    def block_of(offset, is_odd):
        value = shared.get(offset + is_odd, zero)
        return value + own[offset] if offset in own else value

    for out, (even_offset, odd_offset) in zip(outs, chip.slots):
        out[...] = jnp.where(odd, block_of(odd_offset, 1), block_of(even_offset, 0))


def final_kernel(own_ref, *refs):
    out_ref = refs[-1]
    total = refs[0][...]
    for ref in refs[1:-1]:
        total = total + ref[...]
    cols = total.shape[2]
    spread = dot(beside(total.reshape(-1, cols)), spread_matrix(cols))
    count = spread.shape[0]
    for k in range(4):
        part = spread[:, :cols] if k < 2 else spread[:, cols:]
        at = pl.ds(k, count, stride=4)
        out_ref[at, :] = own_ref[at, :] + part


def in_memory(count, space=pltpu.VMEM):
    return [pl.BlockSpec(memory_space=space)] * count


SCALAR = pl.BlockSpec(memory_space=pltpu.SMEM)


def call(kernel, shapes, *operands, scalars=0, scratch=(), name=None, limit=8 << 20, in_place=False, far=(), out_far=()):
    single = not isinstance(shapes, (list, tuple))
    if in_place:
        operands = [pltpu.with_memory_space_constraint(operand, pltpu.HBM) for operand in operands]
    outs = [shapes] if single else list(shapes)
    if in_place:
        far = range(scalars, len(operands))
    places = [SCALAR] * scalars + in_memory(len(operands) - scalars)
    for k in far:
        places[k] = pl.BlockSpec(memory_space=pltpu.HBM)
    out_places = in_memory(len(outs))
    for k in out_far:
        out_places[k] = pl.BlockSpec(memory_space=pltpu.HBM)
        outs[k] = pltpu.HBM(outs[k].shape, outs[k].dtype)
    result = pl.pallas_call(
        kernel,
        out_shape=outs,
        in_specs=places,
        out_specs=out_places,
        scratch_shapes=list(scratch),
        compiler_params=pltpu.CompilerParams(vmem_limit_bytes=limit),
        name=name,
    )(*operands)
    return result[0] if single else result


def body(field, cotangent, lift, spectral, pointwise, project):
    channels, levels, rows, cols = field.shape
    width = lift.shape[1]
    layers = spectral.shape[0]
    modes = spectral.shape[2]
    features = lift.shape[0]
    cells = rows * cols
    tall = rows // 4
    gx, gy = lax.axis_size("gx"), lax.axis_size("gy")
    chip = Chip(gx, channels)
    core = (lax.axis_index("gx") % 2).astype(jnp.int32).reshape(1)

    def shape(*dims, dtype=F32):
        return jax.ShapeDtypeStruct(dims, dtype)

    def along_y(value, even_steps, odd_steps):
        pairs = []
        for a in range(gx):
            for b in range(gy):
                steps = odd_steps if a % 2 else even_steps
                pairs.append((a * gy + b, a * gy + (b + steps) % gy))
        return lax.ppermute(value, ("gx", "gy"), pairs)

    def swap(value):
        return lax.ppermute(value, "gx", [(s, s ^ 1) for s in range(gx)])

    flat_field = field.reshape(channels * rows, cols)
    packed = call(pool_kernel, shape(channels * tall, cols), flat_field, name="pool")
    packed = packed.reshape(channels, tall, cols)

    others = range(1, len(chip.slots))
    held = [packed] + [lax.ppermute(packed, "gx", chip.pairs(slot)) for slot in others]
    wave = wave_matrix(rows, cols)
    padded = -(-features // 16) * 16
    small = -(-channels // 8) * 8
    constants = [wave_pair(wave, 1), wave_pair(wave.T, 0)]
    packed_weights = shape(layers, width, width, 2 * modes)
    prepared = list(call(
        prepare_kernel,
        [shape(*c.shape, dtype=BF16) for c in constants]
        + [
            packed_weights, shape(padded, width), shape(width, padded), shape(width, 3 * padded, dtype=BF16),
            shape(width, 3 * width, dtype=BF16), shape(width, 3 * width, dtype=BF16), shape(padded, 3 * width, dtype=BF16),
            shape(width, cells),
        ],
        cotangent.reshape(channels * rows, cols), lift, jnp.transpose(spectral, (0, 1, 3, 4, 2)), pointwise, project.T,
        *constants,
        in_place=True,
        scratch=(
            pltpu.VMEM((layers, 2, width, width, modes), F32),
            pltpu.VMEM((small * rows, cols), F32),
            pltpu.VMEM((padded, width), F32),
            pltpu.VMEM((layers, width, width), F32),
            pltpu.VMEM((small, width), F32),
            pltpu.SemaphoreType.DMA((6 + layers,)),
        ),
        limit=16 << 20,
        name="prepare",
    ))
    *held[1:], prepared[3] = lax.optimization_barrier((*held[1:], prepared[3]))
    message = shape(chip.tiles, tall, cols)
    to_previous, to_following = call(
        functools.partial(pack_kernel, chip), (message, message), core, *held, scalars=1, name="pack"
    )
    from_a = along_y(to_previous, -2, -1)
    from_b = along_y(to_following, 2, 1)
    swap_a, swap_b = swap(from_a), swap(from_b)

    chunk = 4 * cols
    quarter_part = shape(chip.tiles - chip.edge_tiles, tall, cols)
    own, center_edge, center_quarter, keep_a, keep_b, give_a, give_b = call(
        functools.partial(network_kernel, chip, chunk),
        (shape(channels, rows, cols), shape(channels, 2 * tall, cols), quarter_part, message, message, message, message),
        core, field.reshape(channels, rows, cols), held[0], held[chip.place(1, 0)], held[chip.place(-1, 0)],
        to_previous, from_a, from_b, swap_a, swap_b, *prepared,
        scalars=1,
        scratch=(
            pltpu.VMEM((padded * rows, cols), F32),
            pltpu.VMEM((channels, 3 * tall, cols), F32),
            pltpu.VMEM((channels, 3 * tall, cols), F32),
            pltpu.VMEM((channels, 2 * tall, cols), F32),
            pltpu.VMEM((channels, rows + tall, cols), F32),
            pltpu.VMEM((len(chip.shared), channels, tall, cols), F32),
            pltpu.VMEM((2 * padded, cells), BF16),
            pltpu.VMEM((2 * width, cells), BF16),
            pltpu.VMEM((width, cells), F32),
            pltpu.VMEM((width, cells), F32),
            pltpu.VMEM((padded * rows, cols), F32),
            pltpu.VMEM((width, wave.shape[0]), F32),
        ),
        limit=16 << 20,
        name="network",
    )

    got_a, got_b = swap(give_a), swap(give_b)
    sum_b, sum_a = call(join_kernel, (message, message), keep_b, keep_a, got_b, got_a, name="join")
    sum_b = along_y(sum_b, 2, 1)
    sum_a = along_y(sum_a, -2, -1)
    parts = call(
        functools.partial(gather_kernel, chip),
        [shape(channels, tall, cols)] * len(chip.slots),
        core, center_edge, center_quarter, sum_b, sum_a, scalars=1,
        name="gather",
    )
    parts = [parts[0]] + [lax.ppermute(parts[slot], "gx", chip.pairs(slot, back=True)) for slot in others]
    out = call(
        final_kernel,
        shape(channels * rows, cols),
        own.reshape(channels * rows, cols), *parts,
        name="final",
    )
    return out.reshape(field.shape)


def solution(mesh):
    return jax.shard_map(
        body,
        mesh=mesh,
        in_specs=(P(None, None, "gx", "gy"), P(None, None, "gx", "gy"), P(), P(), P(), P()),
        out_specs=P(None, None, "gx", "gy"),
        check_vma=False,
    )
```
